32 devices in a mesh: shard: 8 (over z, y), replica: 4 (over x, core).
Axes of the slice: x: 2, y: 2, z: 4, core: 2. Of those that a mesh axis runs over, the one named last changes fastest.
Arguments:
- inputs: bfloat16 [2, 4, 2048, 1024], P(None, 'replica', 'shard'), may hold values from -6 to 6
- prefix: int32 [2, 4, 1], P(None, 'replica'), may hold values from 1 to 2048
- qkv_weight: bfloat16 [1024, 3072], P('shard'), may hold values from -0.1875 to 0.1875
- qv_bias: bfloat16 [2, 1024], P(None, 'shard'), may hold values from -3 to 3
- out_weight: bfloat16 [1024, 1024], P('shard'), may hold values from -0.1875 to 0.1875
- branch_bias: bfloat16 [2, 1024], P(None, 'shard'), may hold values from -3 to 3
- up_weight: bfloat16 [1024, 4096], P('shard'), may hold values from -0.1875 to 0.1875
- up_bias: bfloat16 [4096], P('shard'), may hold values from -3 to 3
- down_weight: bfloat16 [4096, 1024], P('shard'), may hold values from -0.09375 to 0.09375
- norm_gain: bfloat16 [4, 1024], P(None, 'shard'), may hold values from 0.5 to 1.5
- norm_bias: bfloat16 [4, 1024], P(None, 'shard'), may hold values from -2 to 2
- cotangent: bfloat16 [2, 4, 2048, 1024], P(None, 'replica', 'shard'), may hold values from -6 to 6
Outputs:
- output: bfloat16 [2, 4, 2048, 1024], P(None, 'replica', 'shard')
- input_grad: bfloat16 [2, 4, 2048, 1024], P(None, 'replica', 'shard')
- grad_qkv_weight: float32 [1024, 3072], P('shard')
- grad_qv_bias: float32 [2, 1024], P(None, 'shard')
- grad_out_weight: float32 [1024, 1024], P('shard')
- grad_branch_bias: float32 [2, 1024], P(None, 'shard')
- grad_up_weight: float32 [1024, 4096], P('shard')
- grad_up_bias: float32 [4096], P('shard')
- grad_down_weight: float32 [4096, 1024], P('shard')
- grad_norm_gain: float32 [4, 1024], P(None, 'shard')
- grad_norm_bias: float32 [4, 1024], P(None, 'shard')
The draws below stay inside these ranges and needn't reach their ends.
Inputs may be any that keep to these rules, and one draw needn't show every extreme that they name: Each sequence's first prefix positions are seen by all of its positions.
All inputs are finite; a program needn't handle non-finite values.
Results may differ from the reference program's by a relative error of at most 0.022.
Values may be sent and summed in bfloat16 or wider, within the bound.
A program may use at most 320 MiB of HBM per device.

```python
import jax
import jax.numpy as jnp
from jax import lax

D = 1024
HEADS = 16
HEAD = 64
FF = 4096
LEN = 2048
MICRO = 2
GROUPS = 4
GROUP_TOK = 2048
SEQ_G = 1


def with_ends(values, own_key, least, top_value):
    longest = values.shape.index(max(values.shape))
    spots = []
    for shift in (0, 1):
        where = [jax.random.randint(jax.random.fold_in(own_key, axis), (), 0, length) for axis, length in enumerate(values.shape)]
        where[longest] = (where[longest] + shift) % values.shape[longest]
        spots.append(tuple(where))
    return values.at[spots[0]].set(least).at[spots[1]].set(top_value)


def block_scale(stream_key, dims, shards, low, top_value):
    gain, own = 1.0, jax.random.fold_in(stream_key, 6)
    for dim, parts in shards:
        draws = jnp.exp(jax.random.uniform(jax.random.fold_in(own, dim), (parts,), jnp.float32, low / len(shards), top_value / len(shards)))
        gain = gain * jnp.repeat(draws, dims[dim] // parts).reshape([-1 if axis == dim else 1 for axis in range(len(dims))])
    return gain


def centred(key, dims, scale, most, pieces=(), kind=jnp.bfloat16):
    loudness = block_scale(key, dims, pieces, -0.22, 0.18) if pieces else 1.0
    entries = jax.random.normal(key, dims, jnp.float32) * scale * loudness
    return jnp.minimum(jnp.maximum(entries, -most), most).astype(kind)


def setup_inputs(seed: int = 0) -> dict:
    streams_of = jax.random.split(jax.random.key(seed), 13)
    return {
        "inputs": centred(streams_of[0], (MICRO, GROUPS, GROUP_TOK, D), 1.0, 6.0, ((1, 4), (2, 8))),
        "prefix": with_ends(jax.random.randint(streams_of[1], (MICRO, GROUPS, SEQ_G), 1, LEN + 1), jax.random.fold_in(streams_of[1], 1), 1, LEN).astype(jnp.int32),
        "qkv_weight": centred(streams_of[2], (D, 3 * D), D ** -0.5, 0.1875, ((0, 8),)),
        "qv_bias": centred(streams_of[3], (2, D), 0.5, 3.0, ((1, 8),)),
        "out_weight": centred(streams_of[4], (D, D), D ** -0.5, 0.1875, ((0, 8),)),
        "branch_bias": centred(streams_of[5], (2, D), 0.5, 3.0, ((1, 8),)),
        "up_weight": centred(streams_of[6], (D, FF), D ** -0.5, 0.1875, ((0, 8),)),
        "up_bias": centred(streams_of[7], (FF,), 0.5, 3.0, ((0, 8),)),
        "down_weight": centred(streams_of[8], (FF, D), FF ** -0.5, 0.09375, ((0, 8),)),
        "norm_gain": jnp.clip(1.0 + 0.1 * jax.random.normal(streams_of[9], (4, D), jnp.float32), 0.5, 1.5).astype(jnp.bfloat16),
        "norm_bias": centred(streams_of[10], (4, D), 0.3, 2.0, ((1, 8),)),
        "cotangent": centred(streams_of[11], (MICRO, GROUPS, GROUP_TOK, D), 1.0, 6.0, ((1, 4), (2, 8))),
    }


@jax.custom_vjp
def low(v):
    return lax.optimization_barrier(v.astype(jnp.bfloat16)).astype(jnp.float32)

@jax.custom_vjp
def low_back(v):
    return v

def low_keep(v):
    return (low(v), None)

def low_pass(kept, grad):
    return (grad,)

def back_keep(v):
    return (v, None)

def back_low(kept, grad):
    return (low(grad),)
low.defvjp(low_keep, low_pass)
low_back.defvjp(back_keep, back_low)
epsilon = 1e-05
masked_value = -1e+30
highest = lax.Precision.HIGHEST

def rounded_both(values):
    return low(low_back(values))

def normed(values, gain_row, shift_row):
    centre = values - lax.optimization_barrier(jnp.mean(values, axis=-1, keepdims=True))
    spread = lax.optimization_barrier(jnp.mean(centre * centre, axis=-1, keepdims=True))
    return centre * lax.rsqrt(spread + epsilon) * gain_row + shift_row

def product(former, latter):
    return jnp.dot(former, latter, precision=highest, preferred_element_type=jnp.float32)

def layer(tokens, prefix_len, qkv_weight, qv_bias, out_weight, branch_bias, up_weight, up_bias, down_weight, norm_gain, norm_bias):
    normal_in = low(normed(tokens, norm_gain[0], norm_bias[0]))
    joined = product(normal_in, qkv_weight)
    queries = rounded_both(joined[:, :D] + qv_bias[0])
    keys = rounded_both(joined[:, D:2 * D])
    values = rounded_both(joined[:, 2 * D:] + qv_bias[1])
    query_heads = queries.reshape(LEN, HEADS, HEAD)
    key_heads = keys.reshape(LEN, HEADS, HEAD)
    value_heads = values.reshape(LEN, HEADS, HEAD)
    block_rows = min(512, LEN)
    key_pos = jnp.arange(LEN, dtype=jnp.int32)
    score_scale = HEAD ** (-0.5)

    def attend_block(row_start):
        query_block = lax.dynamic_slice_in_dim(query_heads, row_start, block_rows, 0)
        row_pos = row_start + jnp.arange(block_rows, dtype=jnp.int32)
        seen = (key_pos[None, :] <= row_pos[:, None]) | (key_pos[None, :] < prefix_len)
        logits = low_back(jnp.einsum('qhd,khd->hqk', query_block, key_heads, precision=highest) * score_scale)
        logits = jnp.where(seen[None], logits, masked_value)
        row_max = lax.optimization_barrier(jnp.max(logits, axis=-1, keepdims=True))
        powers = jnp.exp(logits - row_max)
        probs = low(powers / lax.optimization_barrier(jnp.sum(powers, axis=-1, keepdims=True)))
        mixed = jnp.einsum('hqk,khd->qhd', probs, value_heads, precision=highest)
        return mixed.reshape(block_rows, D)
    starts = jnp.arange(0, LEN, block_rows, dtype=jnp.int32)
    mixed_all = rounded_both(lax.map(jax.checkpoint(attend_block), starts).reshape(LEN, D))
    branch = low_back(product(mixed_all, out_weight) + branch_bias[0])
    stream = tokens + normed(branch, norm_gain[1], norm_bias[1])
    normal_mid = low(normed(stream, norm_gain[2], norm_bias[2]))
    upper = low_back(product(normal_mid, up_weight) + up_bias)
    active = low(jax.nn.gelu(upper, approximate=False))
    lower = low_back(product(active, down_weight) + branch_bias[1])
    return stream + normed(lower, norm_gain[3], norm_bias[3])

def reference(inputs, prefix, qkv_weight, qv_bias, out_weight, branch_bias, up_weight, up_bias, down_weight, norm_gain, norm_bias, cotangent):
    weights = tuple((array.astype(jnp.float32) for array in (qkv_weight, qv_bias, out_weight, branch_bias, up_weight, up_bias, down_weight, norm_gain, norm_bias)))
    token_seqs = inputs.astype(jnp.float32).reshape(-1, LEN, D)
    upstream_seqs = cotangent.astype(jnp.float32).reshape(-1, LEN, D)
    prefix_seqs = prefix.reshape(-1).astype(jnp.int32)

    def one_sequence(totals, sequence_item):
        tokens, prefix_len, upstream = sequence_item

        def forward(token_rows, *params):
            return layer(token_rows, prefix_len, *params)
        result, pullback = jax.vjp(forward, tokens, *weights)
        gradients = pullback(upstream)
        totals = tuple((running + grad_part for running, grad_part in zip(totals, gradients[1:])))
        return (totals, (result, gradients[0]))
    zeros = tuple((jnp.zeros(array.shape, jnp.float32) for array in weights))
    totals, (results, token_grads) = lax.scan(one_sequence, zeros, (token_seqs, prefix_seqs, upstream_seqs))
    return (results.reshape(inputs.shape).astype(jnp.bfloat16), token_grads.reshape(inputs.shape).astype(jnp.bfloat16), totals[0], totals[1], totals[2], totals[3], totals[4], totals[5], totals[6], totals[7], totals[8])
```

```python
import functools
import math

import jax
import jax.numpy as jnp
from jax import lax
from jax.experimental import pallas as pl
from jax.experimental.pallas import tpu as pltpu
from jax.sharding import PartitionSpec as P

HEAD = 64
LEN = 2048
CORES = 2
PAIR = 2 * HEAD
BQ = 256
EPS = 1e-05
MASKED = -1e30
SCALE = HEAD ** (-0.5)
SCALE2 = SCALE * math.log2(math.e)
F32 = jnp.float32
BF16 = jnp.bfloat16
MESH = pl.DeviceIdType.MESH
VMEM_LIMIT = 66_000_000


class Plan:
    def __init__(self, mesh_shape, inputs_shape):
        self.S = mesh_shape["shard"]
        self.R = mesh_shape["replica"]
        self.M, _, self.T, self.D = inputs_shape
        self.Q = self.T * self.S // LEN
        self.P = LEN // self.T
        self.U = self.M * self.Q * CORES
        self.cpu = self.S // self.U
        self.heads = self.D // HEAD
        self.W = self.D // (CORES * self.cpu)
        self.pairs = self.W // PAIR
        self.groups = CORES * self.cpu
        self.pieces = self.T // BQ
        self.nq = LEN // BQ


class Place:
    def __init__(self, plan):
        self.p = plan
        self.s = lax.axis_index("shard")
        self.r = lax.axis_index("replica")
        self.c = lax.rem(self.r, CORES)
        self.chip = self.r - self.c
        self.mate = self.chip + (1 - self.c)
        self.unit = self.s // plan.cpu
        self.lane = lax.rem(self.s, plan.cpu)
        self.group = self.c * plan.cpu + self.lane
        self.uc = lax.rem(self.unit, CORES)
        self.um = lax.rem(self.unit // CORES, plan.M)
        self.uq = self.unit // (CORES * plan.M)
        self.ring = self.to_ring(self.s)

    def unit_of(self, c, m, s):
        return ((s // self.p.P) * self.p.M + m) * CORES + c

    def to_ring(self, s):
        half = self.p.S // 2
        row, col = s // 2, lax.rem(s, 2)
        return row + col * (2 * half - 1 - 2 * row)

    def from_ring(self, i):
        n = self.p.S
        return jnp.where(i < n // 2, 2 * i, 2 * (n - 1 - i) + 1)


def remote(src, dst, send, recv, s, r):
    return pltpu.make_async_remote_copy(
        src_ref=src, dst_ref=dst, send_sem=send, recv_sem=recv, device_id=(s, r), device_id_type=MESH
    )


def launch(away, far, near):
    @pl.when(away)
    def _():
        far().start()

    @pl.when(jnp.logical_not(away))
    def _():
        pltpu.make_async_copy(*near).start()


def sent(away, far, near):
    @pl.when(away)
    def _():
        far().wait_send()


def greet(peers):
    barrier = pltpu.get_barrier_semaphore()
    for s, r in peers:
        pl.semaphore_signal(barrier, inc=1, device_id=(s, r), device_id_type=MESH)
    pl.semaphore_wait(barrier, len(peers))


def plane_peers(here):
    n = here.p.S * CORES
    own = here.s * CORES + here.c
    out = []
    for k in range(1, n):
        i = lax.rem(own + k, n)
        out.append((i // CORES, here.chip + lax.rem(i, CORES)))
    return out


def normed(values, gain, shift):
    centre = values - jnp.mean(values, axis=-1, keepdims=True)
    spread = jnp.mean(centre * centre, axis=-1, keepdims=True)
    return centre * lax.rsqrt(spread + EPS) * gain + shift


def dot(a, b, ca=1, cb=0):
    return lax.dot_general(a, b, (((ca,), (cb,)), ((), ())), preferred_element_type=F32)


def head_lanes(rows, which):
    lane = lax.broadcasted_iota(jnp.int32, (rows, PAIR), 1)
    return (lane < HEAD) if which == 0 else (lane >= HEAD)


def fore_kernel(
    plan, x, par, pre, wq, wo, wu, wd,
    wqf, wof, wuf, wdf, parf, ah, q_out, k_out, v_out, o_out, lse_out, preu, oh,
    parg, a_all, wcol, pre2,
    par_ss, par_rs, pre_sem, loc_sem, a_ss, a_rs, af_ss, w_ss, w_rs, wf_ss, wf_rs, o_ss, o_rs, col_sem,
):
    p = plan
    here = Place(p)
    s, c = here.s, here.c
    mine, full = (wq, wo, wu, wd), (wqf, wof, wuf, wdf)
    nw = len(mine)
    steps = p.S - 1
    greet(plane_peers(here))

    parg[s] = par[...]
    small = []
    for k in range(1, p.S):
        to = lax.rem(s + k, p.S)
        small.append(remote(par, parg.at[s], par_ss.at[k], par_rs.at[k], to, here.r))
        small[-1].start()
    swap = remote(pre, pre2, pre_sem.at[0], pre_sem.at[1], s, here.mate)
    swap.start()

    def block(w, origin, core, d):
        n = mine[w].shape[0]
        return pl.ds(pl.multiple_of(origin * n + core * (n // 2) + d * (n // 4), n // 4), n // 4)

    def own_block(w, d):
        n = mine[w].shape[0]
        return pl.ds(pl.multiple_of(c * (n // 2) + d * (n // 4), n // 4), n // 4)

    def origin_of(d, t):
        i = lax.rem(here.ring + (p.S - 1 - t if d == 0 else 1 + t), p.S)
        return here.from_ring(i)

    ahead = [here.from_ring(lax.rem(here.ring + (1 if d == 0 else p.S - 1), p.S)) for d in (0, 1)]

    def ring_first(w):
        for d in (0, 1):
            remote(
                mine[w].at[own_block(w, d), :], full[w].at[block(w, s, c, d), :],
                w_ss.at[w, d, 0], w_rs.at[w, d, 0], ahead[d], here.r,
            ).start()

    def ring_pass(w, d, t):
        rows = block(w, origin_of(d, t), c, d)
        part = full[w].at[rows, :]
        remote(part, part, w_ss.at[w, d, t], w_rs.at[w, d, t], ahead[d], here.r).wait_recv()

        @pl.when(t < steps - 1)
        def _():
            later = jnp.minimum(t + 1, steps - 1)
            remote(part, part, w_ss.at[w, d, later], w_rs.at[w, d, later], ahead[d], here.r).start()

        remote(part, part, wf_ss.at[w, d, t], wf_rs.at[w, d, t], s, here.mate).start()

    def ring_mate(w, d, t):
        part = full[w].at[block(w, origin_of(d, t), 1 - c, d), :]
        return remote(part, part, wf_ss.at[w, d, t], wf_rs.at[w, d, t], s, here.mate)

    ring_first(0)
    local = []
    for w in range(nw):
        n = mine[w].shape[0]
        local.append(
            pltpu.make_async_copy(mine[w], full[w].at[pl.ds(pl.multiple_of(s * n, n), n), :], loc_sem.at[w])
        )
        local[-1].start()

    for k in range(1, p.S):
        small[k - 1].wait_recv()
    parf[...] = jnp.concatenate([parg[k][:, : p.D // p.S] for k in range(p.S)], axis=1)
    gain = parf[4:5, :].astype(F32)
    shift = parf[8:9, :].astype(F32)
    rows_here = pl.ds(pl.multiple_of(lax.rem(s, p.P) * p.T, p.T), p.T)

    def first_hop(m):
        to = here.unit_of(c, m, s) * p.cpu + here.lane
        far = lambda: remote(ah.at[m], a_all.at[rows_here, :], a_ss.at[m], a_rs.at[lax.rem(s, p.P)], to, here.r)
        return to, far

    for m in range(p.M):
        ah[m] = normed(x[m].astype(F32), gain, shift).astype(BF16)
        to, far = first_hop(m)

        @pl.when(to != s)
        def _():
            far().start()

        @pl.when(to == s)
        def _():
            a_all[rows_here, :] = ah[m]

    primary = c == here.uc

    def a_rows(j):
        return pl.ds(pl.multiple_of(j * p.T, p.T), p.T)

    def a_forward(j, k):
        part = a_all.at[a_rows(j), :]
        if k == 0:
            return remote(part, part, af_ss.at[j, 0], a_rs.at[j], s, here.mate)
        to = here.unit * p.cpu + lax.rem(here.lane + k, p.cpu)
        return remote(part, part, af_ss.at[j, k], a_rs.at[j], to, here.r)

    def a_wait(j):
        part = a_all.at[a_rows(j), :]
        remote(part, part, af_ss.at[j, 0], a_rs.at[j], s, here.mate).wait_recv()

    near = p.P // p.cpu

    def a_near(jj):
        @pl.when(primary)
        def _():
            j = jj * p.cpu + here.lane

            @pl.when(here.uq * p.P + j != s)
            def _():
                a_wait(j)

            for k in list(range(1, p.cpu)) + [0]:
                a_forward(j, k).start()

    def a_far(jj):
        @pl.when(primary)
        def _():
            for k in range(1, p.cpu):
                j = jj * p.cpu + lax.rem(here.lane + k, p.cpu)
                a_wait(j)
                a_forward(j, 0).start()

    for t in range(steps):
        for d in (0, 1):
            ring_pass(0, d, t)
        if t < near:
            a_near(t)
        if 2 <= t < near + 2:
            a_far(t - 2)
    for w in range(1, nw):
        ring_first(w)

    @pl.when(jnp.logical_not(primary))
    def _():
        for j in range(p.P):
            a_wait(j)

    swap.wait_recv()
    pre2[...] = jnp.where(primary, pre[...], pre2[...])
    row = here.um * p.Q + here.uq
    preu[...] = jnp.broadcast_to(pre2[pl.ds(row, 1), :], preu.shape)

    for t in range(steps):
        for d in (0, 1):
            ring_mate(0, d, t).wait_recv()
    local[0].wait()
    cols = []
    for k in range(3):
        start = pl.multiple_of(k * p.D + here.group * p.W, PAIR)
        cols.append(pltpu.make_async_copy(wqf.at[:, pl.ds(start, p.W)], wcol.at[k], col_sem.at[k]))
        cols[-1].start()
    for copy in cols:
        copy.wait()
    own = pl.ds(pl.multiple_of(here.group * p.W, PAIR), p.W)
    q_bias = parf[0:1, own].astype(F32)
    v_bias = parf[1:2, own].astype(F32)

    def project(i, carry):
        rows = pl.ds(pl.multiple_of(i * BQ, BQ), BQ)
        part = a_all[rows, :]
        q_out[rows, :] = (dot(part, wcol[0]) + q_bias).astype(BF16)
        k_out[rows, :] = dot(part, wcol[1]).astype(BF16)
        v_out[rows, :] = (dot(part, wcol[2]) + v_bias).astype(BF16)
        return carry

    lax.fori_loop(0, p.nq, project, 0)

    prefix = preu[0:1, 0:1]
    per = -(-steps // p.nq)

    def o_copy(i):
        rows = pl.ds(pl.multiple_of(i * BQ, BQ), BQ)
        home = here.uq * p.P + i // p.pieces
        piece = lax.rem(i, p.pieces)
        there = pl.ds(pl.multiple_of(piece * BQ, BQ), BQ)
        src = o_out.at[rows, :]
        dst = oh.at[here.um, there, own]
        away = jnp.logical_or(home != s, here.uc != c)
        recv = o_rs.at[here.um, here.group, piece]
        return away, lambda: remote(src, dst, o_ss.at[i], recv, home, here.chip + here.uc), (src, dst, recv)

    def attend(i, carry):
        rows = pl.ds(pl.multiple_of(i * BQ, BQ), BQ)
        row_pos = (lax.broadcasted_iota(jnp.int32, (BQ, 1), 0) + i * BQ + 1).astype(F32)
        bound = jnp.maximum(row_pos, prefix)
        key_pos = lax.broadcasted_iota(jnp.int32, (1, LEN), 1).astype(F32)
        seen = key_pos < bound

        def pair_step(h, inner):
            lanes = pl.ds(pl.multiple_of(h * PAIR, PAIR), PAIR)
            qp, kp, vp = q_out[rows, lanes], k_out[:, lanes], v_out[:, lanes]
            halves = []
            for e in (0, 1):
                logits = dot(jnp.where(head_lanes(BQ, e), qp, jnp.zeros_like(qp)), kp, 1, 1)
                logits = jnp.where(seen, logits, MASKED)
                top = jnp.max(logits, axis=1, keepdims=True)
                powers = jnp.exp2((logits - top) * SCALE2)
                total = jnp.sum(powers, axis=1, keepdims=True)
                halves.append(dot(powers.astype(BF16), vp) * (1.0 / total))
                level = top * SCALE2 + jnp.log2(total)
                turned = jnp.broadcast_to(level, (BQ, 128)).T
                lse_out[2 * h + e, :, pl.ds(pl.multiple_of(i * BQ, BQ), BQ)] = turned[0:8]
            o_out[rows, lanes] = jnp.where(head_lanes(BQ, 0), halves[0], halves[1]).astype(BF16)
            return inner

        lax.fori_loop(0, p.pairs, pair_step, 0)
        launch(*o_copy(i))

        for extra in range(per):
            t = i * per + extra

            @pl.when(t < steps)
            def _():
                for w in range(1, nw):
                    for d in (0, 1):
                        ring_pass(w, d, jnp.minimum(t, steps - 1))

        return carry

    lax.fori_loop(0, p.nq, attend, 0)

    for m in range(p.M):
        for g in range(p.groups):
            for piece in range(p.pieces):
                src = o_out.at[pl.ds(0, BQ), :]
                dst = oh.at[m, pl.ds(piece * BQ, BQ), pl.ds(g * p.W, p.W)]
                pltpu.make_async_copy(src, dst, o_rs.at[m, g, piece]).wait()

    def o_sent(i, carry):
        sent(*o_copy(i))
        return carry

    lax.fori_loop(0, p.nq, o_sent, 0)
    for copy in small:
        copy.wait_send()
    swap.wait_send()
    for copy in local[1:]:
        copy.wait()
    for m in range(p.M):
        to, far = first_hop(m)

        @pl.when(to != s)
        def _():
            far().wait_send()

    @pl.when(primary)
    def _():
        for jj in range(near):
            for k in range(p.cpu):
                a_forward(jj * p.cpu + here.lane, k).wait_send()
            for k in range(1, p.cpu):
                a_forward(jj * p.cpu + lax.rem(here.lane + k, p.cpu), 0).wait_send()

    def drain(t, carry):
        for w in range(nw):
            for d in (0, 1):
                if w:
                    ring_mate(w, d, t).wait_recv()
                ring_mate(w, d, t).wait_send()
                part = full[w].at[block(w, origin_of(d, t), c, d), :]
                remote(part, part, w_ss.at[w, d, t], w_rs.at[w, d, t], ahead[d], here.r).wait_send()
        return carry

    lax.fori_loop(0, steps, drain, 0)


def fore(plan, x, par, pre, weights):
    p = plan
    steps = p.S - 1
    nw = len(weights)
    any_space = pl.BlockSpec(memory_space=pl.ANY)
    vmem = pl.BlockSpec(memory_space=pltpu.VMEM)
    shape = jax.ShapeDtypeStruct
    out_shape = (
        [shape((w.shape[0] * p.S, w.shape[1]), BF16) for w in weights]
        + [shape((par.shape[0], p.D), BF16), shape((p.M, p.T, p.D), BF16)]
        + [shape((LEN, p.W), BF16)] * 4
        + [shape((2 * p.pairs, 8, LEN), F32), shape((8, 128), F32), shape((p.M, p.T, p.D), BF16)]
    )
    dma = pltpu.SemaphoreType.DMA
    return pl.pallas_call(
        functools.partial(fore_kernel, p),
        out_shape=out_shape,
        in_specs=[vmem] * (3 + nw),
        out_specs=[any_space] * nw + [vmem] * 9,
        scratch_shapes=[
            pltpu.VMEM((p.S,) + par.shape, BF16),
            pltpu.VMEM((LEN, p.D), BF16),
            pltpu.VMEM((3, p.D, p.W), BF16),
            pltpu.VMEM((8, 128), F32),
            dma((p.S,)), dma((p.S,)), dma((2,)), dma((nw,)),
            dma((p.M,)), dma((p.P,)), dma((p.P, p.cpu)),
            dma((nw, 2, steps)), dma((nw, 2, steps)), dma((nw, 2, steps)), dma((nw, 2, steps)),
            dma((p.nq,)), dma((p.M, p.groups, p.pieces)), dma((3,)),
        ],
        compiler_params=pltpu.CompilerParams(
            collective_id=0, has_side_effects=True, vmem_limit_bytes=VMEM_LIMIT
        ),
        name="fore",
    )(x, par, pre, *weights)


def back_kernel(
    plan, q, k, v, o, lse, preu, dh_home,
    home_out,
    do_all, dq_buf, dkv_buf, dk_acc, dv_acc, k_turn,
    do_ss, do_rs, g_ss, g_rs,
):
    p = plan
    here = Place(p)
    s, c = here.s, here.c
    greet(plane_peers(here))
    rows_here = pl.ds(pl.multiple_of(lax.rem(s, p.P) * p.T, p.T), p.T)

    def do_copy(m, g):
        core, lane = g // p.cpu, g % p.cpu
        to = here.unit_of(c, m, s) * p.cpu + lane
        src = dh_home.at[m, :, pl.ds(g * p.W, p.W)]
        dst = do_all.at[rows_here, :]
        away = jnp.logical_or(to != s, c != core)
        recv = do_rs.at[lax.rem(s, p.P)]
        return away, lambda: remote(src, dst, do_ss.at[m, g], recv, to, here.chip + core), (src, dst, recv)

    for m in range(p.M):
        for g in range(p.groups):
            launch(*do_copy(m, g))

    prefix = preu[0:1, 0:1]
    unit_dev = here.chip + here.uc

    def g_copy(part, h, i):
        rows = pl.ds(pl.multiple_of(i * BQ, BQ), BQ)
        src = dq_buf.at[h, rows, :] if part == 0 else dkv_buf.at[part - 1, h, rows, :]
        home = here.uq * p.P + i // p.pieces
        piece = lax.rem(i, p.pieces)
        there = pl.ds(pl.multiple_of(piece * BQ, BQ), BQ)
        lanes = pl.ds(pl.multiple_of(part * p.D + here.group * p.W + h * PAIR, PAIR), PAIR)
        dst = home_out.at[here.um, there, lanes]
        recv = g_rs.at[part, here.um, here.group * p.pairs + h, piece]
        away = jnp.logical_or(home != s, here.uc != c)
        return away, lambda: remote(src, dst, g_ss.at[part, h, i], recv, home, unit_dev), (src, dst, recv)

    def pair_step(h, carry):
        lanes = pl.ds(pl.multiple_of(h * PAIR, PAIR), PAIR)
        k_turn[...] = k[:, lanes].astype(F32).T.astype(BF16)
        dk_acc[...] = jnp.zeros_like(dk_acc)
        dv_acc[...] = jnp.zeros_like(dv_acc)

        def query_step(i, inner):
            rows = pl.ds(pl.multiple_of(i * BQ, BQ), BQ)

            @pl.when(jnp.logical_and(h == 0, lax.rem(i, p.pieces) == 0))
            def _():
                j = i // p.pieces
                part = do_all.at[pl.ds(pl.multiple_of(j * p.T, p.T), p.T), :]
                pltpu.make_async_copy(part, part, do_rs.at[j]).wait()

            qp, dop, op = q[rows, lanes], do_all[rows, lanes], o[rows, lanes]
            kp, vp = k[:, lanes], v[:, lanes]
            turned = (dop.astype(F32) * op.astype(F32)).T
            pos = (lax.broadcasted_iota(jnp.int32, (1, BQ), 1) + i * BQ + 1).astype(F32)
            bound = jnp.maximum(pos, prefix)
            key_pos = lax.broadcasted_iota(jnp.int32, (LEN, 1), 0).astype(F32)
            seen = key_pos < bound
            dq_t = []
            for e in (0, 1):
                lit = head_lanes(BQ, e)
                qe = jnp.where(lit, qp, jnp.zeros_like(qp))
                de = jnp.where(lit, dop, jnp.zeros_like(dop))
                level = lse[2 * h + e, 0:1, pl.ds(pl.multiple_of(i * BQ, BQ), BQ)]
                inner_sum = jnp.sum(turned[e * HEAD : (e + 1) * HEAD], axis=0, keepdims=True)
                logits = dot(kp, qe, 1, 1)
                probs = jnp.where(seen, jnp.exp2(logits * SCALE2 - level), 0.0)
                slope = dot(vp, de, 1, 1)
                dlog = (probs * (slope - inner_sum)).astype(BF16)
                dv_acc[...] += dot(probs.astype(BF16), de)
                dk_acc[...] += dot(dlog, qe)
                dq_t.append(dot(k_turn[e * HEAD : (e + 1) * HEAD, :], dlog))
            dq_buf[h, rows, :] = (jnp.concatenate(dq_t, axis=0).T * SCALE).astype(BF16)
            launch(*g_copy(0, h, i))
            return inner

        lax.fori_loop(0, p.nq, query_step, 0)
        dkv_buf[0, h] = (dk_acc[...] * SCALE).astype(BF16)
        dkv_buf[1, h] = dv_acc[...].astype(BF16)

        def send(i, inner):
            launch(*g_copy(1, h, i))
            launch(*g_copy(2, h, i))
            return inner

        lax.fori_loop(0, p.nq, send, 0)
        return carry

    lax.fori_loop(0, p.pairs, pair_step, 0)

    for m in range(p.M):
        for g in range(p.groups):
            sent(*do_copy(m, g))

    def g_sent(i, carry):
        for part in range(3):
            for h in range(p.pairs):
                sent(*g_copy(part, h, i))
        return carry

    lax.fori_loop(0, p.nq, g_sent, 0)
    every = p.groups * p.pairs
    for part in range(3):
        for m in range(p.M):
            for piece in range(p.pieces):

                def got(n, carry):
                    lanes = pl.ds(pl.multiple_of(part * p.D + n * PAIR, PAIR), PAIR)
                    dst = home_out.at[m, pl.ds(piece * BQ, BQ), lanes]
                    pltpu.make_async_copy(dst, dst, g_rs.at[part, m, n, piece]).wait()
                    return carry

                lax.fori_loop(0, every, got, 0)


def back(plan, q, k, v, o, lse, preu, do_home):
    p = plan
    vmem = pl.BlockSpec(memory_space=pltpu.VMEM)
    dma = pltpu.SemaphoreType.DMA
    return pl.pallas_call(
        functools.partial(back_kernel, p),
        out_shape=jax.ShapeDtypeStruct((p.M, p.T, 3 * p.D), BF16),
        in_specs=[vmem] * 7,
        out_specs=vmem,
        scratch_shapes=[
            pltpu.VMEM((LEN, p.W), BF16),
            pltpu.VMEM((p.pairs, LEN, PAIR), BF16),
            pltpu.VMEM((2, p.pairs, LEN, PAIR), BF16),
            pltpu.VMEM((LEN, PAIR), F32),
            pltpu.VMEM((LEN, PAIR), F32),
            pltpu.VMEM((PAIR, LEN), BF16),
            dma((p.M, p.groups)), dma((p.P,)),
            dma((3, p.pairs, p.nq)), dma((3, p.M, p.groups * p.pairs, p.pieces)),
        ],
        compiler_params=pltpu.CompilerParams(
            collective_id=1, has_side_effects=True, vmem_limit_bytes=VMEM_LIMIT
        ),
        name="back",
    )(q, k, v, o, lse, preu, do_home)


def sum_kernel(plan, planes, nw, *refs):
    p = plan
    here = Place(p)
    s, c = here.s, here.c
    g = refs[:nw]
    small = refs[nw]
    outs = refs[nw + 1 : 2 * nw + 1]
    small_out = refs[2 * nw + 1]
    rest = refs[2 * nw + 2 :]
    held, mate, came, cross = rest[:nw], rest[nw : 2 * nw], rest[2 * nw : 3 * nw], rest[3 * nw : 4 * nw]
    small_in, small_all, ld, cx_s, cx_r, r_s, r_r, x_s, x_r, f_s, f_r, ss_s, ss_r, sa_s, sa_r = rest[4 * nw :]
    steps = p.S - 1
    plane = here.r // CORES

    peers = plane_peers(here) + [
        (s, lax.rem(plane + k, planes) * CORES + j) for k in range(1, planes) for j in range(CORES)
    ]
    greet(peers)

    loads, swaps = [], []
    for w in range(nw):
        loads.append(pltpu.make_async_copy(g[w].at[:, c], held[w], ld.at[w]))
        swaps.append(remote(g[w].at[:, 1 - c], mate[w], cx_s.at[w], cx_r.at[w], s, here.mate))
        swaps[-1].start()
        loads[-1].start()

    small_in[0] = small[s]
    tiny = []
    for k in range(1, p.S):
        to = lax.rem(s + k, p.S)
        tiny.append(remote(small.at[to], small_in.at[k], ss_s.at[k], ss_r.at[k], to, here.r))
        tiny[-1].start()

    ahead = [here.from_ring(lax.rem(here.ring + (1 if d == 0 else p.S - 1), p.S)) for d in (0, 1)]

    def target(d, t):
        i = lax.rem(here.ring + (2 * p.S - 1 - t if d == 0 else 1 + t), p.S)
        return here.from_ring(i)

    def part_rows(w, d):
        n = held[w].shape[1] // 2
        return pl.ds(d * n, n)

    def ring(w, d, t, to):
        return remote(
            held[w].at[to, part_rows(w, d), :], came[w].at[d, t], r_s.at[w, d, t], r_r.at[w, d, t], ahead[d], here.r
        )

    for w in range(nw):
        loads[w].wait()
        swaps[w].wait_recv()
        for d in (0, 1):
            to = target(d, 0)
            rows = part_rows(w, d)
            held[w][to, rows, :] = (held[w][to, rows, :].astype(F32) + mate[w][to, rows, :].astype(F32)).astype(BF16)
            ring(w, d, 0, to).start()

    def step(t, carry):
        for w in range(nw):
            for d in (0, 1):
                to = target(d, t)
                rows = part_rows(w, d)
                ring(w, d, t - 1, to).wait_recv()
                held[w][to, rows, :] = (
                    held[w][to, rows, :].astype(F32)
                    + mate[w][to, rows, :].astype(F32)
                    + came[w][d, t - 1].astype(F32)
                ).astype(BF16)

                @pl.when(t < steps)
                def _():
                    ring(w, d, jnp.minimum(t, steps - 1), to).start()

        return carry

    lax.fori_loop(1, steps + 1, step, 0)

    def over(w, k):
        to = lax.rem(plane + k, planes) * CORES + c
        return remote(held[w].at[s], cross[w].at[plane], x_s.at[w, k], x_r.at[w, plane], s, to)

    for w in range(nw):
        for k in range(1, planes):
            over(w, k).start()
        cross[w][plane] = held[w][s]

    for k in range(1, p.S):
        tiny[k - 1].wait_recv()
    total = small_in[0]
    for k in range(1, p.S):
        total = total + small_in[k]
    small_all[here.r] = total
    every = []
    for k in range(1, p.R):
        to = lax.rem(here.r + k, p.R)
        every.append(remote(small_all.at[here.r], small_all.at[here.r], sa_s.at[k], sa_r.at[here.r], s, to))
        every[-1].start()

    hand = []
    for w in range(nw):
        for k in range(1, planes):
            off = lax.rem(plane + k, planes)
            remote(held[w].at[s], cross[w].at[off], x_s.at[w, k], x_r.at[w, off], s, here.r).wait_recv()
        sum_ = cross[w][0].astype(F32)
        for k in range(1, planes):
            sum_ = sum_ + cross[w][k].astype(F32)
        half = outs[w].at[c]
        half[...] = sum_.astype(BF16)
        hand.append(remote(half, half, f_s.at[w], f_r.at[w], s, here.mate))
        hand[-1].start()

    for k in range(1, p.R):
        off = lax.rem(here.r + k, p.R)
        remote(small_all.at[0], small_all.at[off], sa_s.at[k], sa_r.at[off], s, here.r).wait_recv()
    total = small_all[0]
    for k in range(1, p.R):
        total = total + small_all[k]
    small_out[...] = total

    for copy in swaps + tiny + every:
        copy.wait_send()
    for w in range(nw):
        for k in range(1, planes):
            over(w, k).wait_send()
        hand[w].wait_send()
        other = outs[w].at[1 - c]
        remote(other, other, f_s.at[w], f_r.at[w], s, here.mate).wait_recv()

    def drain(t, carry):
        for w in range(nw):
            for d in (0, 1):
                ring(w, d, t, target(d, t)).wait_send()
        return carry

    lax.fori_loop(0, steps, drain, 0)


def summed(plan, grads, small):
    p = plan
    nw = len(grads)
    planes = p.R // CORES
    steps = p.S - 1
    split = []
    for grad in grads:
        rows, cols = grad.shape
        split.append(grad.reshape(p.S, CORES, rows // (p.S * CORES), cols))
    any_space = pl.BlockSpec(memory_space=pl.ANY)
    vmem = pl.BlockSpec(memory_space=pltpu.VMEM)
    dma = pltpu.SemaphoreType.DMA
    shapes = [(h.shape[2], h.shape[3]) for h in split]
    outs = pl.pallas_call(
        functools.partial(sum_kernel, p, planes, nw),
        out_shape=[jax.ShapeDtypeStruct((CORES,) + sh, BF16) for sh in shapes]
        + [jax.ShapeDtypeStruct(small.shape[1:], F32)],
        in_specs=[any_space] * nw + [vmem],
        out_specs=[vmem] * (nw + 1),
        scratch_shapes=[pltpu.VMEM((p.S,) + sh, BF16) for sh in shapes]
        + [pltpu.VMEM((p.S,) + sh, BF16) for sh in shapes]
        + [pltpu.VMEM((2, steps, sh[0] // 2, sh[1]), BF16) for sh in shapes]
        + [pltpu.VMEM((planes,) + sh, BF16) for sh in shapes]
        + [
            pltpu.VMEM(small.shape, F32),
            pltpu.VMEM((p.R,) + small.shape[1:], F32),
            dma((nw,)), dma((nw,)), dma((nw,)),
            dma((nw, 2, steps)), dma((nw, 2, steps)),
            dma((nw, planes)), dma((nw, planes)),
            dma((nw,)), dma((nw,)),
            dma((p.S,)), dma((p.S,)), dma((p.R,)), dma((p.R,)),
        ],
        compiler_params=pltpu.CompilerParams(
            collective_id=2, has_side_effects=True, vmem_limit_bytes=VMEM_LIMIT
        ),
        name="sums",
    )(*split, small)
    full = [o.reshape(CORES * o.shape[1], o.shape[2]).astype(F32) for o in outs[:nw]]
    return full, outs[nw]


def smooth(values):
    return jax.nn.gelu(values, approximate=False)


def per_device(
    sizes,
    inputs,
    prefix,
    qkv_weight,
    qv_bias,
    out_weight,
    branch_bias,
    up_weight,
    up_bias,
    down_weight,
    norm_gain,
    norm_bias,
    cotangent,
):
    p = Plan(sizes, (inputs.shape[0], 1, inputs.shape[2], inputs.shape[3]))
    tokens_all = p.M * p.T
    x = inputs[:, 0]
    width = p.D // p.S
    spare = max(128 - width, 0)
    par = jnp.concatenate([qv_bias, branch_bias, norm_gain, norm_bias, up_bias.reshape(-1, width)], axis=0)
    par = jnp.pad(par, ((0, 0), (0, spare)))
    pre = jnp.broadcast_to(prefix[:, 0].reshape(-1, 1).astype(F32), (p.M * p.Q, 128))
    pre = jnp.pad(pre, ((0, 8 - p.M * p.Q), (0, 0)))
    (wq, wo, wu, wd, parf, a_home, q, k, v, o, lse, preu, o_home) = fore(
        p, x, par, pre, (qkv_weight, out_weight, up_weight, down_weight)
    )
    par32 = parf.astype(F32)
    bias_branch = par32[2:4]
    gains, shifts = par32[4:8], par32[8:12]
    bias_up = par32[12:].reshape(-1, p.S, width).transpose(1, 0, 2).reshape(-1)

    tokens = x.reshape(tokens_all, p.D).astype(F32)
    upstream = cotangent[:, 0].reshape(tokens_all, p.D).astype(F32)
    mixed_low = o_home.reshape(tokens_all, p.D)
    a_low = a_home.reshape(tokens_all, p.D)
    branch = dot(mixed_low, wo) + bias_branch[0]
    side, pull_side = jax.vjp(normed, branch, gains[1:2], shifts[1:2])
    stream = tokens + side
    normal_mid, pull_mid = jax.vjp(normed, stream, gains[2:3], shifts[2:3])
    middle_low = normal_mid.astype(BF16)
    upper = dot(middle_low, wu) + bias_up
    active, pull_active = jax.vjp(smooth, upper)
    active_low = active.astype(BF16)
    lower = dot(active_low, wd) + bias_branch[1]
    closing, pull_close = jax.vjp(normed, lower, gains[3:4], shifts[3:4])
    output = (stream + closing).astype(BF16)
    grad_lower, gain_three, shift_three = pull_close(upstream)
    lower_low = grad_lower.astype(BF16)
    grad_active = dot(lower_low, wd, 1, 1)
    (grad_upper,) = pull_active(grad_active)
    upper_low = grad_upper.astype(BF16)
    grad_middle = dot(upper_low, wu, 1, 1)
    grad_mid_in, gain_two, shift_two = pull_mid(grad_middle)
    grad_stream = grad_mid_in + upstream
    grad_branch, gain_one, shift_one = pull_side(grad_stream)
    branch_low = grad_branch.astype(BF16)
    grad_mixed = dot(branch_low, wo, 1, 1).astype(BF16)

    joined = back(p, q, k, v, o, lse, preu, grad_mixed.reshape(p.M, p.T, p.D))
    joined_low = joined.reshape(tokens_all, 3 * p.D)
    grad_normal = dot(joined_low, wq, 1, 1)
    _, pull_in = jax.vjp(normed, tokens, gains[0:1], shifts[0:1])
    grad_tokens, gain_zero, shift_zero = pull_in(grad_normal)
    input_grad = (grad_stream + grad_tokens).astype(BF16)

    def column_sum(values):
        return jnp.sum(values.astype(F32), axis=0, keepdims=True)

    du_sum = column_sum(upper_low).reshape(p.S, -1, width).transpose(1, 0, 2).reshape(-1, p.D)
    joined_sum = column_sum(joined_low)
    small = jnp.concatenate(
        [
            joined_sum[:, : p.D], joined_sum[:, 2 * p.D :],
            column_sum(branch_low), column_sum(lower_low),
            gain_zero, gain_one, gain_two, gain_three,
            shift_zero, shift_one, shift_two, shift_three,
            du_sum,
        ], axis=0,
    )
    small = jnp.pad(small.reshape(-1, p.S, width).transpose(1, 0, 2), ((0, 0), (0, 0), (0, spare)))
    grads = (
        dot(a_low, joined_low, 0, 0).astype(BF16),
        dot(mixed_low, branch_low, 0, 0).astype(BF16),
        dot(middle_low, upper_low, 0, 0).astype(BF16),
        dot(active_low, lower_low, 0, 0).astype(BF16),
    )
    full, tiny = summed(p, grads, small)
    tiny = tiny[:, :width]
    shaped = (p.M, 1, p.T, p.D)
    return (
        output.reshape(shaped),
        input_grad.reshape(shaped),
        full[0],
        tiny[0:2],
        full[1],
        tiny[2:4],
        full[2],
        tiny[12:].reshape(-1),
        full[3],
        tiny[4:8],
        tiny[8:12],
    )


def solution(mesh):
    sizes = {name: mesh.shape[name] for name in ("shard", "replica")}
    placed = (
        P(None, "replica", "shard", None),
        P(None, "replica", None),
        P("shard", None),
        P(None, "shard"),
        P("shard", None),
        P(None, "shard"),
        P("shard", None),
        P("shard"),
        P("shard", None),
        P(None, "shard"),
        P(None, "shard"),
        P(None, "replica", "shard", None),
    )
    return jax.shard_map(
        functools.partial(per_device, sizes),
        mesh=mesh,
        in_specs=placed,
        out_specs=(
            P(None, "replica", "shard", None),
            P(None, "replica", "shard", None),
            P("shard", None),
            P(None, "shard"),
            P("shard", None),
            P(None, "shard"),
            P("shard", None),
            P("shard"),
            P("shard", None),
            P(None, "shard"),
            P(None, "shard"),
        ),
        check_vma=False,
    )
```

```python
import functools
import math

import jax
import jax.numpy as jnp
from jax import lax
from jax.experimental import pallas as pl
from jax.experimental.pallas import tpu as pltpu
from jax.sharding import PartitionSpec as P

HEAD = 64
LEN = 2048
CORES = 2
PAIR = 2 * HEAD
BQ = 256
EPS = 1e-05
MASKED = -1e30
SCALE = HEAD ** (-0.5)
SCALE2 = SCALE * math.log2(math.e)
F32 = jnp.float32
BF16 = jnp.bfloat16
MESH = pl.DeviceIdType.MESH
VMEM_LIMIT = 66_000_000
LAG = 2
KEYS = 512
SIDE_FIRST = (False, True, True)
SUM_LAG = 2
COLUMN_FIRST = (True, True, True, False)


class Plan:
    def __init__(self, mesh_shape, inputs_shape):
        self.S = mesh_shape["shard"]
        self.R = mesh_shape["replica"]
        self.M, _, self.T, self.D = inputs_shape
        self.Q = self.T * self.S // LEN
        self.P = LEN // self.T
        self.U = self.M * self.Q * CORES
        self.cpu = self.S // self.U
        self.heads = self.D // HEAD
        self.W = self.D // (CORES * self.cpu)
        self.pairs = self.W // PAIR
        self.groups = CORES * self.cpu
        self.pieces = self.T // BQ
        self.nq = LEN // BQ
        self.near = self.P // self.cpu
        self.width = self.D // self.S
        assert self.cpu == 2 and self.pairs == 2 and self.T % BQ == 0 and LEN % self.T == 0


class Place:
    def __init__(self, plan):
        self.p = plan
        self.s = lax.axis_index("shard")
        self.r = lax.axis_index("replica")
        self.c = lax.rem(self.r, CORES)
        self.chip = self.r - self.c
        self.mate = self.chip + (1 - self.c)
        self.unit = self.s // plan.cpu
        self.lane = lax.rem(self.s, plan.cpu)
        self.group = self.c * plan.cpu + self.lane
        self.uc = lax.rem(self.unit, CORES)
        self.um = lax.rem(self.unit // CORES, plan.M)
        self.uq = self.unit // (CORES * plan.M)
        self.ring = self.to_ring(self.s)
        self.plane = self.r // CORES
        self.side = lax.rem(self.plane, 2)
        self.twin = self.r + CORES * (1 - 2 * self.side)
        self.row = self.s // 2
        self.col = lax.rem(self.s, 2)
        self.beside = 2 * self.row + 1 - self.col
        self.rows = plan.S // 2

    def unit_of(self, c, m, s):
        return ((s // self.p.P) * self.p.M + m) * CORES + c

    def to_ring(self, s):
        half = self.p.S // 2
        row, col = s // 2, lax.rem(s, 2)
        return row + col * (2 * half - 1 - 2 * row)

    def from_ring(self, i):
        n = self.p.S
        return jnp.where(i < n // 2, 2 * i, 2 * (n - 1 - i) + 1)


def remote(src, dst, send, recv, s, r):
    return pltpu.make_async_remote_copy(
        src_ref=src, dst_ref=dst, send_sem=send, recv_sem=recv, device_id=(s, r), device_id_type=MESH
    )


def launch(away, far, near):
    @pl.when(away)
    def _():
        far().start()

    @pl.when(jnp.logical_not(away))
    def _():
        pltpu.make_async_copy(*near).start()


def sent(away, far, near):
    @pl.when(away)
    def _():
        far().wait_send()


def greet(peers):
    barrier = pltpu.get_barrier_semaphore()
    for s, r in peers:
        pl.semaphore_signal(barrier, inc=1, device_id=(s, r), device_id_type=MESH)
    pl.semaphore_wait(barrier, len(peers))


def plane_peers(here):
    n = here.p.S * CORES
    own = here.s * CORES + here.c
    out = []
    for k in range(1, n):
        i = lax.rem(own + k, n)
        out.append((i // CORES, here.chip + lax.rem(i, CORES)))
    return out


def normed(values, gain, shift):
    centre = values - jnp.mean(values, axis=-1, keepdims=True)
    spread = jnp.mean(centre * centre, axis=-1, keepdims=True)
    return centre * lax.rsqrt(spread + EPS) * gain + shift


def dot(a, b, ca=1, cb=0):
    return lax.dot_general(a, b, (((ca,), (cb,)), ((), ())), preferred_element_type=F32)


def head_lanes(rows, which):
    lane = lax.broadcasted_iota(jnp.int32, (rows, PAIR), 1)
    return (lane < HEAD) if which == 0 else (lane >= HEAD)


def fore_kernel(
    plan, x, par, pre, wq, wo, wu, wd,
    wqf, wof, wuf, wdf, parf, ah, q_out, k_out, v_out, o_out, lse_out, preu, oh, a_all, wcol,
    parg, pre2,
    par_ss, par_rs, pre_sem, loc_sem, a_ss, a_rs, af_ss, z_ss, z_rs, wa_ss, wa_rs, wb_ss, wb_rs, wm_ss, wm_rs,
    o_ss, o_rs, col_sem,
):
    p = plan
    here = Place(p)
    s, c = here.s, here.c
    mine, full = (wq, wo, wu, wd), (wqf, wof, wuf, wdf)
    nw = len(mine)
    first = COLUMN_FIRST
    greet(plane_peers(here) + [(s, here.twin)])

    parg[s] = par[...]
    small = []
    for k in range(1, p.S):
        to = lax.rem(s + k, p.S)
        small.append(remote(par, parg.at[s], par_ss.at[k], par_rs.at[k], to, here.r))
        small[-1].start()
    swap = remote(pre, pre2, pre_sem.at[0], pre_sem.at[1], s, here.mate)
    swap.start()

    z, nz = here.row, here.rows

    def where(w, zr, fa, fb, core):
        fy, fx = (fa, fb) if first[w] else (fb, fa)
        col = here.col if fy == 0 else 1 - here.col
        side = here.side if fx == 0 else 1 - here.side
        n, width = mine[w].shape[0], mine[w].shape[1] // 2
        rows = pl.ds(pl.multiple_of((2 * zr + col) * n + core * (n // 2), n // 2), n // 2)
        return full[w].at[rows, pl.ds(pl.multiple_of(side * width, width), width)]

    def origin(w, fa):
        n, width = mine[w].shape[0], mine[w].shape[1] // 2
        side = here.side if fa == 0 else 1 - here.side
        rows = pl.ds(pl.multiple_of(c * (n // 2), n // 2), n // 2)
        return mine[w].at[rows, pl.ds(pl.multiple_of(side * width, width), width)]

    def peer(w, second):
        return (here.beside, here.r) if first[w] == (second == 0) else (s, here.twin)

    def z_send(w, d, k):
        sign = 1 - 2 * d
        part = where(w, z - sign * (k - 1), 0, 0, c)
        src = origin(w, 0) if isinstance(k, int) and k == 1 else part
        return remote(src, part, z_ss.at[w, d, k - 1], z_rs.at[w, d, k - 1], s + 2 * sign, here.r)

    def z_came(w, d, k):
        sign = 1 - 2 * d
        part = where(w, z - sign * k, 0, 0, c)
        return remote(part, part, z_ss.at[w, d, k - 1], z_rs.at[w, d, k - 1], s, here.r)

    def to_first(w, zr, src=None):
        part = where(w, zr, 0, 0, c)
        return remote(part if src is None else src, part, wa_ss.at[w, zr], wa_rs.at[w, zr], *peer(w, 0))

    def to_second(w, fa, zr, src=None):
        part = where(w, zr, fa, 0, c)
        return remote(part if src is None else src, part, wb_ss.at[w, fa, zr], wb_rs.at[w, fa, zr], *peer(w, 1))

    def to_mate(w, fa, fb, zr, core):
        part = where(w, zr, fa, fb, core)
        at = 2 * fa + fb
        return remote(part, part, wm_ss.at[w, at, zr], wm_rs.at[w, at, zr], s, here.mate)

    def first_came(w, zr):
        part = where(w, zr, 1, 0, c)
        return remote(part, part, wa_ss.at[w, zr], wa_rs.at[w, zr], s, here.r)

    def second_came(w, fa, zr):
        part = where(w, zr, fa, 1, c)
        return remote(part, part, wb_ss.at[w, fa, zr], wb_rs.at[w, fa, zr], s, here.r)

    def on_grid(d, k):
        return z >= k if d == 0 else z + k < nz

    def can_send(d):
        return z < nz - 1 if d == 0 else z > 0

    def gather_start(w):
        for d in (0, 1):

            @pl.when(can_send(d))
            def _():
                z_send(w, d, 1).start()

        if first[w]:
            to_first(w, z, origin(w, 0)).start()
        else:
            to_second(w, 0, z, origin(w, 0)).start()
            to_second(w, 1, z, origin(w, 1)).start()

    def gather_slot(w, k, lag):
        for d in (0, 1):
            sign = 1 - 2 * d

            @pl.when(jnp.logical_and(k >= 1, on_grid(d, k)))
            def _():
                at = jnp.maximum(k, 1)
                z_came(w, d, at).wait_recv()
                zr = z - sign * at

                @pl.when(can_send(d))
                def _():
                    z_send(w, d, at + 1).start()

                to_first(w, zr).start()
                to_second(w, 0, zr).start()
                to_mate(w, 0, 0, zr, c).start()

        def at_distance(j, least, body):
            for d in (0, 1):
                ok = jnp.logical_and(j >= max(least, d), on_grid(d, j))

                @pl.when(ok)
                def _():
                    body(z - (1 - 2 * d) * jnp.maximum(j, 0))

        def after_first(zr):
            first_came(w, zr).wait_recv()
            to_second(w, 1, zr).start()
            to_mate(w, 1, 0, zr, c).start()

        at_distance(k - 1, 0 if first[w] else 1, after_first)

        def after_second(fa):
            def body(zr):
                second_came(w, fa, zr).wait_recv()
                to_mate(w, fa, 1, zr, c).start()

            return body

        at_distance(k - 1 - lag, 1 if first[w] else 0, after_second(0))
        at_distance(k - 2 - lag, 0, after_second(1))

    def mate_pieces(w, zr, act):
        other = zr != z

        @pl.when(other)
        def _():
            act(0, 0)

        if first[w]:

            @pl.when(other)
            def _():
                act(0, 1)

            act(1, 0)
        else:

            @pl.when(other)
            def _():
                act(1, 0)

            act(0, 1)
        act(1, 1)

    def gather_wait(w):
        def one(zr, carry):
            mate_pieces(w, zr, lambda fa, fb: to_mate(w, fa, fb, zr, 1 - c).wait_recv())
            return carry

        lax.fori_loop(0, nz, one, 0)

    def gather_drain(w):
        def one(zr, carry):
            mate_pieces(w, zr, lambda fa, fb: to_mate(w, fa, fb, zr, c).wait_send())
            if first[w]:
                to_first(w, zr).wait_send()

                @pl.when(zr != z)
                def _():
                    to_second(w, 0, zr).wait_send()
            else:

                @pl.when(zr != z)
                def _():
                    to_first(w, zr).wait_send()

                to_second(w, 0, zr).wait_send()
            to_second(w, 1, zr).wait_send()
            for d in (0, 1):
                reach = zr <= z if d == 0 else zr < nz - z

                @pl.when(jnp.logical_and(can_send(d), reach))
                def _():
                    z_send(w, d, zr + 1).wait_send()

            return carry

        lax.fori_loop(0, nz, one, 0)

    gather_start(0)
    local = []
    for w in range(nw):
        n = mine[w].shape[0]
        local.append(
            pltpu.make_async_copy(mine[w], full[w].at[pl.ds(pl.multiple_of(s * n, n), n), :], loc_sem.at[w])
        )
        local[-1].start()

    for k in range(1, p.S):
        small[k - 1].wait_recv()
    parf[...] = jnp.concatenate([parg[k][:, : p.D // p.S] for k in range(p.S)], axis=1)
    gain = parf[4:5, :].astype(F32)
    shift = parf[8:9, :].astype(F32)
    rows_here = pl.ds(pl.multiple_of(lax.rem(s, p.P) * p.T, p.T), p.T)

    def first_hop(m):
        to = here.unit_of(c, m, s) * p.cpu + here.lane
        far = lambda: remote(ah.at[m], a_all.at[rows_here, :], a_ss.at[m], a_rs.at[lax.rem(s, p.P)], to, here.r)
        return to, far

    for m in range(p.M):
        ah[m] = normed(x[m].astype(F32), gain, shift).astype(BF16)
        to, far = first_hop(m)

        @pl.when(to != s)
        def _():
            far().start()

        @pl.when(to == s)
        def _():
            a_all[rows_here, :] = ah[m]

    primary = c == here.uc

    def a_rows(j):
        return pl.ds(pl.multiple_of(j * p.T, p.T), p.T)

    def a_forward(j, k):
        part = a_all.at[a_rows(j), :]
        if k == 0:
            return remote(part, part, af_ss.at[j, 0], a_rs.at[j], s, here.mate)
        to = here.unit * p.cpu + lax.rem(here.lane + k, p.cpu)
        return remote(part, part, af_ss.at[j, k], a_rs.at[j], to, here.r)

    def a_wait(j):
        part = a_all.at[a_rows(j), :]
        remote(part, part, af_ss.at[j, 0], a_rs.at[j], s, here.mate).wait_recv()

    near = p.near

    zi = here.unit - here.uq * near

    def a_at(k, body):
        for d in (0, 1):
            if k or not d:
                ok = zi >= k if d == 0 else zi + k < near

                @pl.when(jnp.logical_and(primary, ok))
                def _():
                    body(zi - (1 - 2 * d) * k)

    def a_near(jj):
        j = jj * p.cpu + here.lane

        @pl.when(here.uq * p.P + j != s)
        def _():
            a_wait(j)

        for k in list(range(1, p.cpu)) + [0]:
            a_forward(j, k).start()

    def a_far(jj):
        for k in range(1, p.cpu):
            j = jj * p.cpu + lax.rem(here.lane + k, p.cpu)
            a_wait(j)
            a_forward(j, 0).start()

    for k in range(max(nz + 2, near + 1)):
        if 1 <= k < nz + 2:
            gather_slot(0, k, 0)
        if k < near:
            a_at(k, a_near)
        if 1 <= k < near + 1:
            a_at(k - 1, a_far)
        if k == near - 1:
            for w in range(1, nw):
                gather_start(w)

    @pl.when(jnp.logical_not(primary))
    def _():
        for j in range(p.P):
            a_wait(j)

    swap.wait_recv()
    pre2[...] = jnp.where(primary, pre[...], pre2[...])
    row = here.um * p.Q + here.uq
    preu[...] = jnp.broadcast_to(pre2[pl.ds(row, 1), :], preu.shape)

    gather_wait(0)
    local[0].wait()
    cols = []
    for h in range(p.pairs):
        for k in range(3):
            start = pl.multiple_of(k * p.D + here.group * p.W + h * PAIR, PAIR)
            src = wqf.at[:, pl.ds(start, PAIR)]
            cols.append(pltpu.make_async_copy(src, wcol.at[h, :, pl.ds(k * PAIR, PAIR)], col_sem.at[h, k]))
            cols[-1].start()
    for copy in cols:
        copy.wait()
    own = pl.ds(pl.multiple_of(here.group * p.W, PAIR), p.W)
    q_bias = parf[0:1, own].astype(F32)
    v_bias = parf[1:2, own].astype(F32)

    def project(i, carry):
        rows = pl.ds(pl.multiple_of(i * BQ, BQ), BQ)
        part = a_all[rows, :]
        for h in range(p.pairs):
            lanes = slice(h * PAIR, (h + 1) * PAIR)
            got = dot(part, wcol[h])
            q_out[rows, lanes] = (got[:, :PAIR] + q_bias[:, lanes]).astype(BF16)
            k_out[rows, lanes] = got[:, PAIR : 2 * PAIR].astype(BF16)
            v_out[rows, lanes] = (got[:, 2 * PAIR :] + v_bias[:, lanes]).astype(BF16)
        return carry

    lax.fori_loop(0, p.nq, project, 0)

    prefix = preu[0:1, 0:1]
    slots = nz + 1 + LAG
    per = -(-slots // p.nq)

    def o_copy(i):
        rows = pl.ds(pl.multiple_of(i * BQ, BQ), BQ)
        home = here.uq * p.P + i // p.pieces
        piece = lax.rem(i, p.pieces)
        there = pl.ds(pl.multiple_of(piece * BQ, BQ), BQ)
        src = o_out.at[rows, :]
        dst = oh.at[here.um, there, own]
        away = jnp.logical_or(home != s, here.uc != c)
        recv = o_rs.at[here.um, here.group, piece]
        return away, lambda: remote(src, dst, o_ss.at[i], recv, home, here.chip + here.uc), (src, dst, recv)

    def attend(i, carry):
        rows = pl.ds(pl.multiple_of(i * BQ, BQ), BQ)
        row_pos = (lax.broadcasted_iota(jnp.int32, (BQ, 1), 0) + i * BQ + 1).astype(F32)
        bound = jnp.maximum(row_pos, prefix)
        key_pos = lax.broadcasted_iota(jnp.int32, (1, LEN), 1).astype(F32)
        seen = key_pos < bound

        def pair_step(h, inner):
            lanes = pl.ds(pl.multiple_of(h * PAIR, PAIR), PAIR)
            qp, kp, vp = q_out[rows, lanes], k_out[:, lanes], v_out[:, lanes]
            halves = []
            for e in (0, 1):
                logits = dot(jnp.where(head_lanes(BQ, e), qp, jnp.zeros_like(qp)), kp, 1, 1)
                logits = jnp.where(seen, logits, MASKED)
                top = jnp.max(logits, axis=1, keepdims=True)
                powers = jnp.exp2((logits - top) * SCALE2)
                total = jnp.sum(powers, axis=1, keepdims=True)
                halves.append(dot(powers.astype(BF16), vp) * (1.0 / total))
                level = top * SCALE2 + jnp.log2(total)
                turned = jnp.broadcast_to(level, (BQ, 128)).T
                lse_out[2 * h + e, :, pl.ds(pl.multiple_of(i * BQ, BQ), BQ)] = turned[0:8]
            o_out[rows, lanes] = jnp.where(head_lanes(BQ, 0), halves[0], halves[1]).astype(BF16)
            return inner

        lax.fori_loop(0, p.pairs, pair_step, 0)
        launch(*o_copy(i))

        for extra in range(per):
            for w in range(1, nw):
                gather_slot(w, i * per + extra + 1, LAG)

        return carry

    lax.fori_loop(0, p.nq, attend, 0)

    for m in range(p.M):
        for g in range(p.groups):
            for piece in range(p.pieces):
                src = o_out.at[pl.ds(0, BQ), :]
                dst = oh.at[m, pl.ds(piece * BQ, BQ), pl.ds(g * p.W, p.W)]
                pltpu.make_async_copy(src, dst, o_rs.at[m, g, piece]).wait()

    def o_sent(i, carry):
        sent(*o_copy(i))
        return carry

    lax.fori_loop(0, p.nq, o_sent, 0)
    for copy in small:
        copy.wait_send()
    swap.wait_send()
    for copy in local[1:]:
        copy.wait()
    for m in range(p.M):
        to, far = first_hop(m)

        @pl.when(to != s)
        def _():
            far().wait_send()

    @pl.when(primary)
    def _():
        for jj in range(near):
            for k in range(p.cpu):
                a_forward(jj * p.cpu + here.lane, k).wait_send()
            for k in range(1, p.cpu):
                a_forward(jj * p.cpu + lax.rem(here.lane + k, p.cpu), 0).wait_send()

    for w in range(nw):
        if w:
            gather_wait(w)
        gather_drain(w)


def fore(plan, x, par, pre, weights):
    p = plan
    nz = p.S // 2
    nw = len(weights)
    any_space = pl.BlockSpec(memory_space=pl.ANY)
    vmem = pl.BlockSpec(memory_space=pltpu.VMEM)
    shape = jax.ShapeDtypeStruct
    out_shape = (
        [shape((w.shape[0] * p.S, w.shape[1]), BF16) for w in weights]
        + [shape((par.shape[0], p.D), BF16), shape((p.M, p.T, p.D), BF16)]
        + [shape((LEN, p.W), BF16)] * 4
        + [shape((2 * p.pairs, 8, LEN), F32), shape((8, 128), F32), shape((p.M, p.T, p.D), BF16)]
        + [shape((LEN, p.D), BF16), shape((p.pairs, p.D, 3 * PAIR), BF16)]
    )
    dma = pltpu.SemaphoreType.DMA
    return pl.pallas_call(
        functools.partial(fore_kernel, p),
        out_shape=out_shape,
        in_specs=[vmem] * (3 + nw),
        out_specs=[any_space] * nw + [vmem] * 11,
        scratch_shapes=[
            pltpu.VMEM((p.S,) + par.shape, BF16),
            pltpu.VMEM((8, 128), F32),
            dma((p.S,)), dma((p.S,)), dma((2,)), dma((nw,)),
            dma((p.M,)), dma((p.P,)), dma((p.P, p.cpu)),
            dma((nw, 2, nz)), dma((nw, 2, nz)), dma((nw, nz)), dma((nw, nz)),
            dma((nw, 2, nz)), dma((nw, 2, nz)), dma((nw, 4, nz)), dma((nw, 4, nz)),
            dma((p.nq,)), dma((p.M, p.groups, p.pieces)), dma((p.pairs, 3)),
        ],
        compiler_params=pltpu.CompilerParams(
            collective_id=0, has_side_effects=True, vmem_limit_bytes=VMEM_LIMIT
        ),
        name="fore",
    )(x, par, pre, *weights)


class GridSum:
    def __init__(self, here, grads, outs, refs):
        self.here, self.grads, self.outs = here, grads, outs
        self.nw = nw = len(grads)
        self.nz = here.rows
        self.planes = here.p.R // CORES
        self.own, self.acc, self.one, self.two, self.far = (refs[k * nw : (k + 1) * nw] for k in range(5))
        (self.ld, self.m_s, self.m_r, self.a_s, self.a_r, self.b_s, self.b_r, self.z_s, self.z_r) = refs[5 * nw : 5 * nw + 9]
        (self.x_s, self.x_r, self.t_s, self.t_r, self.f_s, self.f_r) = refs[5 * nw + 9 :]
        self.side_first = SIDE_FIRST

    @staticmethod
    def scratch(plan, shapes):
        nw = len(shapes)
        planes = plan.R // CORES
        nz = plan.S // 2
        dma = pltpu.SemaphoreType.DMA
        return (
            [pltpu.VMEM((2,) + sh, BF16) for sh in shapes]
            + [pltpu.VMEM((plan.S,) + sh, BF16) for sh in shapes]
            + [
                pltpu.VMEM((plan.S, sh[0], sh[1] // 2) if sf else (nz,) + sh, BF16)
                for sh, sf in zip(shapes, SIDE_FIRST)
            ]
            + [pltpu.VMEM((nz, sh[0], sh[1] // 2), BF16) for sh in shapes]
            + [pltpu.VMEM((max(nz, planes // 2), sh[0], sh[1] // 2), BF16) for sh in shapes]
            + [dma((nw,))]
            + [dma((nw, nz))] * 8
            + [dma((nw, planes))] * 2
            + [dma((nw,))] * 2
            + [dma((nw, 2))] * 2
        )

    @staticmethod
    def count(nw):
        return 5 * nw + 15

    def zr(self, k):
        return lax.rem(self.here.row + 1 + k, self.nz)

    def half(self, w, side):
        n = self.acc[w].shape[2] // 2
        return pl.ds(pl.multiple_of(side * n, n), n)

    def load(self, w, k):
        src = self.grads[w].at[pl.ds(2 * self.zr(k), 2), self.here.c]
        return pltpu.make_async_copy(src, self.own[w], self.ld.at[w])

    def swap(self, w, k):
        here = self.here
        pair = pl.ds(2 * self.zr(k), 2)
        return remote(
            self.grads[w].at[pair, 1 - here.c], self.acc[w].at[pair], self.m_s.at[w, k], self.m_r.at[w, k], here.s, here.mate
        )

    def first(self, w, k):
        here, zr = self.here, self.zr(k)
        if self.side_first[w]:
            pair = pl.ds(2 * zr, 2)
            src = self.acc[w].at[pair, :, self.half(w, 1 - here.side)]
            return remote(src, self.one[w].at[pair], self.a_s.at[w, k], self.a_r.at[w, k], here.s, here.twin)
        src = self.acc[w].at[2 * zr + 1 - here.col]
        return remote(src, self.one[w].at[zr], self.a_s.at[w, k], self.a_r.at[w, k], here.beside, here.r)

    def second(self, w, k):
        here, zr = self.here, self.zr(k)
        if self.side_first[w]:
            src = self.acc[w].at[2 * zr + 1 - here.col, :, self.half(w, here.side)]
            to = (here.beside, here.r)
        else:
            src = self.acc[w].at[2 * zr + here.col, :, self.half(w, 1 - here.side)]
            to = (here.s, here.twin)
        return remote(src, self.two[w].at[zr], self.b_s.at[w, k], self.b_r.at[w, k], *to)

    def final(self, w, k):
        here, zr = self.here, self.zr(k)
        src = self.acc[w].at[2 * zr + here.col, :, self.half(w, here.side)]
        return remote(
            src, self.far[w].at[here.row], self.z_s.at[w, k], self.z_r.at[w, here.row], 2 * zr + here.col, here.r
        )

    def begin(self):
        for k in range(self.nz):
            for w in range(self.nw):
                self.swap(w, k).start()
                if k == 0:
                    self.load(w, 0).start()

    def event_one(self, w, k):
        zr = self.zr(k)
        pair = pl.ds(2 * zr, 2)
        self.load(w, k).wait()
        self.swap(w, k).wait_recv()
        self.acc[w][pair] = (self.acc[w][pair].astype(F32) + self.own[w][...].astype(F32)).astype(BF16)
        self.first(w, k).start()

        @pl.when(k < self.nz - 1)
        def _():
            self.load(w, jnp.minimum(k + 1, self.nz - 1)).start()

    def event_two(self, w, k):
        here, zr = self.here, self.zr(k)
        self.first(w, k).wait_recv()
        acc = self.acc[w]
        if self.side_first[w]:
            pair = pl.ds(2 * zr, 2)
            lanes = self.half(w, here.side)
            acc[pair, :, lanes] = (acc[pair, :, lanes].astype(F32) + self.one[w][pair].astype(F32)).astype(BF16)
        else:
            at = 2 * zr + here.col
            acc[at] = (acc[at].astype(F32) + self.one[w][zr].astype(F32)).astype(BF16)
        self.second(w, k).start()

    def event_three(self, w, k):
        here, zr = self.here, self.zr(k)
        self.second(w, k).wait_recv()
        at, lanes = 2 * zr + here.col, self.half(w, here.side)
        self.acc[w][at, :, lanes] = (self.acc[w][at, :, lanes].astype(F32) + self.two[w][zr].astype(F32)).astype(BF16)

        @pl.when(k < self.nz - 1)
        def _():
            self.final(w, k).start()

    def events(self):
        return self.nw * self.nz + 2 * SUM_LAG

    def event(self, n):
        for stage, body in enumerate((self.event_one, self.event_two, self.event_three)):
            e = n - stage * SUM_LAG
            for w in range(self.nw):
                ok = jnp.logical_and(e >= 0, e < self.nw * self.nz)

                @pl.when(jnp.logical_and(ok, lax.rem(e, self.nw) == w))
                def _():
                    body(w, jnp.maximum(e, 0) // self.nw)

    def over(self, w, k):
        here = self.here
        pairs = self.planes // 2
        to = 2 * lax.rem(here.plane // 2 + k, pairs) + here.side
        src = self.two[w].at[0]
        return remote(
            src, self.one_slot(w, here.plane // 2), self.x_s.at[w, k], self.x_r.at[w, here.plane // 2],
            here.s, to * CORES + here.c,
        )

    def one_slot(self, w, k):
        return self.acc[w].at[k, :, self.half(w, self.here.side)]

    def to_twin(self, w, side):
        part = self.outs[w].at[self.here.c, :, self.half(w, side)]
        return remote(part, part, self.t_s.at[w], self.t_r.at[w], self.here.s, self.here.twin)

    def to_mate(self, w, core, via):
        side = self.here.side if via == 0 else 1 - self.here.side
        part = self.outs[w].at[core, :, self.half(w, side)]
        return remote(part, part, self.f_s.at[w, via], self.f_r.at[w, via], self.here.s, self.here.mate)

    def finish(self):
        here = self.here
        for w in range(self.nw):
            self.far[w][here.row] = self.acc[w][here.s, :, self.half(w, here.side)]
            for k in range(self.nz - 1):
                off = lax.rem(here.row + 1 + k, self.nz)
                part = self.far[w].at[off]
                remote(part, part, self.z_s.at[w, k], self.z_r.at[w, off], here.s, here.r).wait_recv()
            total = self.far[w][0].astype(F32)
            for k in range(1, self.nz):
                total = total + self.far[w][k].astype(F32)
            self.outs[w][here.c, :, self.half(w, here.side)] = total.astype(BF16)
            self.to_twin(w, here.side).start()
            self.to_mate(w, here.c, 0).start()

    def twin_to_mate(self):
        for w in range(self.nw):
            self.to_twin(w, 1 - self.here.side).wait_recv()
            self.to_mate(w, self.here.c, 1).start()

    def drain(self):
        for w in range(self.nw):
            for via in (0, 1):
                self.to_mate(w, 1 - self.here.c, via).wait_recv()
                self.to_mate(w, self.here.c, via).wait_send()
            self.to_twin(w, self.here.side).wait_send()
            for k in range(self.nz):
                self.swap(w, k).wait_send()
                self.first(w, k).wait_send()
                self.second(w, k).wait_send()
                if k < self.nz - 1:
                    self.final(w, k).wait_send()


def sum_peers(here):
    p = here.p
    planes = p.R // CORES
    far = [(here.s, lax.rem(here.plane + k, planes) * CORES + j) for k in range(1, planes) for j in range(CORES)]
    twin_chip = here.twin - here.c
    return plane_peers(here) + far + [(here.beside, twin_chip + j) for j in range(CORES)]


def split_rows(p, grad):
    rows, cols = grad.shape
    return grad.reshape(p.S, CORES, rows // (p.S * CORES), cols)


def whole_shard(halves):
    return halves.reshape(CORES * halves.shape[1], halves.shape[2]).astype(F32)


def back_kernel(plan, nw, *refs):
    p = plan
    here = Place(p)
    s, c = here.s, here.c
    nz, near, width = here.rows, p.near, p.width
    (q, k, v, o, lse, preu, do_home, a_all, wcol, x, stream, par, small) = refs[:13]
    grads = refs[13 : 13 + nw]
    rest = refs[13 + nw :]
    input_grad, gq, small_out = rest[:3]
    outs = rest[3 : 3 + nw]
    rest = rest[3 + nw :]
    (do_all, low, dk_acc, dv_acc, k_turn, da_own, da_out, da_in, da_side) = rest[:9]
    x_buf, stream_buf, buf_sem, a_buf, a_sem = rest[-5:]
    rest = rest[:-5]
    da_home = input_grad
    (dw_out, dw_own, dw_in, dw_far, dw_end, small_acc, small_in, small_all) = rest[9:17]
    (do_ss, do_rs, dm_s, dm_r, dy_s, dy_r, dh_s, dh_r, wt_s, wt_r, wz_s, wz_r, wx_s, wx_r, wd_s, wd_r) = rest[17:33]
    (ss_s, ss_r, sa_s, sa_r) = rest[33:37]
    sums = GridSum(here, grads, outs, rest[37:])
    per = -(-sums.events() // (p.pairs * p.nq))
    greet(sum_peers(here))
    rows_here = pl.ds(pl.multiple_of(lax.rem(s, p.P) * p.T, p.T), p.T)

    def do_copy(m, g):
        core, lane = g // p.cpu, g % p.cpu
        to = here.unit_of(c, m, s) * p.cpu + lane
        src = do_home.at[m, :, pl.ds(g * p.W, p.W)]
        dst = do_all.at[rows_here, :]
        away = jnp.logical_or(to != s, c != core)
        recv = do_rs.at[lax.rem(s, p.P)]
        return away, lambda: remote(src, dst, do_ss.at[m, g], recv, to, here.chip + core), (src, dst, recv)

    for m in range(p.M):
        for g in range(p.groups):
            launch(*do_copy(m, g))
    sums.begin()
    small_acc[...] = small[...]
    prefix = preu[0:1, 0:1]

    def block_rows(i):
        return pl.ds(pl.multiple_of(i * BQ, BQ), BQ)

    def a_load(b):
        slot = lax.rem(b, 2)
        return pltpu.make_async_copy(
            a_all.at[:, pl.ds(pl.multiple_of(b * BQ, BQ), BQ)], a_buf.at[slot], a_sem.at[slot]
        )

    def weight_part(h, dst):
        def some(b, carry):
            slot = lax.rem(b, 2)

            @pl.when(b < p.D // BQ - 1)
            def _():
                a_load(b + 1).start()

            a_load(b).wait()
            dst[pl.ds(pl.multiple_of(b * BQ, BQ), BQ), :] = dot(a_buf[slot], low[h], 0, 0).astype(BF16)
            return carry

        lax.fori_loop(0, p.D // BQ, some, 0)

    def bias_part(h):
        folds = PAIR // width
        for row, lanes in ((0, slice(0, PAIR)), (1, slice(2 * PAIR, 3 * PAIR))):
            total = jnp.sum(low[h, :, lanes].astype(F32), axis=0, keepdims=True)
            for n in range(folds):
                at = (here.group * p.pairs + h) * folds + n
                small_acc[at, row : row + 1, 0:width] = total[:, n * width : (n + 1) * width]

    def to_twin_dw():
        return remote(dw_out, dw_in, wt_s.at[0], wt_r.at[0], s, here.twin)

    def pair_step(turn, carry):
        h = lax.rem(turn + 1 + here.side, 2)
        lanes = pl.ds(pl.multiple_of(h * PAIR, PAIR), PAIR)
        k_turn[...] = k[:, lanes].astype(F32).T.astype(BF16)
        dk_acc[...] = jnp.zeros_like(dk_acc)
        dv_acc[...] = jnp.zeros_like(dv_acc)

        def query_step(i, inner):
            rows = block_rows(i)

            @pl.when(jnp.logical_and(turn == 0, lax.rem(i, p.pieces) == 0))
            def _():
                j = i // p.pieces
                part = do_all.at[pl.ds(pl.multiple_of(j * p.T, p.T), p.T), :]
                pltpu.make_async_copy(part, part, do_rs.at[j]).wait()

            qp, dop, op = q[rows, lanes], do_all[rows, lanes], o[rows, lanes]
            turned = (dop.astype(F32) * op.astype(F32)).T
            pos = (lax.broadcasted_iota(jnp.int32, (1, BQ), 1) + i * BQ + 1).astype(F32)
            bound = jnp.maximum(pos, prefix)
            dq_t = []
            for e in (0, 1):
                lit = head_lanes(BQ, e)
                qe = jnp.where(lit, qp, jnp.zeros_like(qp))
                de = jnp.where(lit, dop, jnp.zeros_like(dop))
                level = lse[2 * h + e, 0:1, rows]
                inner_sum = jnp.sum(turned[e * HEAD : (e + 1) * HEAD], axis=0, keepdims=True)
                total = jnp.zeros((HEAD, BQ), F32)
                for start in range(0, LEN, KEYS):
                    keys = slice(start, start + KEYS)
                    key_pos = (lax.broadcasted_iota(jnp.int32, (KEYS, 1), 0) + start).astype(F32)
                    logits = dot(k[keys, lanes], qe, 1, 1)
                    probs = jnp.where(key_pos < bound, jnp.exp2(logits * SCALE2 - level), 0.0)
                    slope = dot(v[keys, lanes], de, 1, 1)
                    dlog = (probs * (slope - inner_sum)).astype(BF16)
                    dv_acc[keys, :] += dot(probs.astype(BF16), de)
                    dk_acc[keys, :] += dot(dlog, qe)
                    total = total + dot(k_turn[e * HEAD : (e + 1) * HEAD, keys], dlog)
                dq_t.append(total)
            low[h, rows, 0:PAIR] = (jnp.concatenate(dq_t, axis=0).T * SCALE).astype(BF16)
            for extra in range(per):
                sums.event((turn * p.nq + i) * per + extra)
            return inner

        lax.fori_loop(0, p.nq, query_step, 0)
        low[h, :, PAIR : 2 * PAIR] = (dk_acc[...] * SCALE).astype(BF16)
        low[h, :, 2 * PAIR :] = dv_acc[...].astype(BF16)
        bias_part(h)

        a_load(0).start()

        @pl.when(turn == 0)
        def _():
            weight_part(h, dw_out)
            to_twin_dw().start()

        return carry

    lax.fori_loop(0, p.pairs, pair_step, 0)

    half = p.D // CORES

    def block_of(n):
        lane = lax.rem(here.lane + 1 + n // (near * p.pieces), p.cpu)
        m = lax.rem(n, near * p.pieces)
        return ((m // p.pieces) * p.cpu + lane) * p.pieces + lax.rem(m, p.pieces)

    def da_half(rows, core):
        at = pl.ds(pl.multiple_of(core * half, half), half)
        total = dot(low[0, rows, :], wcol[0, at, :], 1, 1)
        for h in range(1, p.pairs):
            total = total + dot(low[h, rows, :], wcol[h, at, :], 1, 1)
        return total

    def da_mate(n, i):
        rows = block_rows(i)
        return remote(da_out.at[rows, :], da_in.at[rows, :], dm_s.at[n], dm_r.at[i], s, here.mate)

    def da_first(n, carry):
        i = block_of(n)
        rows = block_rows(i)
        da_out[rows, :] = da_half(rows, 1 - c).astype(BF16)
        da_mate(n, i).start()
        da_own[rows, :] = da_half(rows, c).astype(BF16)
        return carry

    lax.fori_loop(0, p.nq, da_first, 0)

    own_pair = here.side
    weight_part(own_pair, dw_own)
    to_twin_dw().wait_recv()
    dw_own[...] = (dw_own[...].astype(F32) + dw_in[...].astype(F32)).astype(BF16)
    span = 2 * width

    def dw_rows(zr):
        return pl.ds(pl.multiple_of(zr * span, span), span)

    def dw_send(n):
        zr = lax.rem(here.row + 1 + n, nz)
        return remote(
            dw_own.at[dw_rows(zr), :], dw_far.at[here.row], wz_s.at[n], wz_r.at[here.row], 2 * zr + here.col, here.r
        )

    for n in range(nz - 1):
        dw_send(n).start()

    far_blocks = (p.cpu - 1) * near * p.pieces

    def side_rows(i):
        return block_rows((i // p.pieces // p.cpu) * p.pieces + lax.rem(i, p.pieces))

    def da_over(n, i):
        return remote(da_own.at[block_rows(i), :], da_side.at[side_rows(i), :], dy_s.at[n], dy_r.at[i], here.beside, here.r)

    def da_back(n, i):
        rows = block_rows(i)
        home = here.uq * p.P + i // p.pieces
        piece = lax.rem(i, p.pieces)
        dst = da_home.at[here.um, block_rows(piece), pl.ds(pl.multiple_of(c * half, half), half)]
        src = da_own.at[rows, :]
        recv = dh_r.at[here.um, c, piece]
        away = jnp.logical_or(home != s, here.uc != c)
        return away, lambda: remote(src, dst, dh_s.at[n], recv, home, here.chip + here.uc), (src, dst, recv)

    def da_second(n, carry):
        i = block_of(n)
        rows = block_rows(i)
        da_mate(n, i).wait_recv()
        pair = da_own[rows, :].astype(F32) + da_in[rows, :].astype(F32)

        @pl.when(n < far_blocks)
        def _():
            da_own[rows, :] = pair.astype(BF16)
            da_over(n, i).start()

        @pl.when(n >= far_blocks)
        def _():
            da_over(n, i).wait_recv()
            da_own[rows, :] = (pair + da_side[side_rows(i), :].astype(F32)).astype(BF16)
            launch(*da_back(n, i))

        return carry

    lax.fori_loop(0, p.nq, da_second, 0)
    sums.finish()

    dw_far[here.row] = dw_own[dw_rows(here.row), :]
    for n in range(nz - 1):
        off = lax.rem(here.row + 1 + n, nz)
        remote(dw_far.at[off], dw_far.at[off], wz_s.at[n], wz_r.at[off], s, here.r).wait_recv()
    total = dw_far[0].astype(F32)
    for n in range(1, nz):
        total = total + dw_far[n].astype(F32)
    dw_end[...] = total.astype(BF16)
    slot = here.group * p.pairs + here.side
    twin_chip = here.twin - c

    def dw_give(n):
        fy, fx, fc = n // 4, n // 2 % 2, n % 2
        col = here.col if fy == 0 else 1 - here.col
        core = c if fc == 0 else 1 - c
        src = dw_end.at[pl.ds(pl.multiple_of(col * width, width), width), :]
        dst = gq.at[slot]
        to = (2 * here.row + col, (here.chip if fx == 0 else twin_chip) + core)
        return src, dst, to

    for n in range(1, 8):
        src, dst, to = dw_give(n)
        remote(src, dst, wd_s.at[n], wd_r.at[slot], *to).start()
    gq[slot] = dw_end[pl.ds(pl.multiple_of(here.col * width, width), width), :]

    def token_loads(m, piece):
        at = pl.ds(piece * BQ, BQ)
        return (
            pltpu.make_async_copy(x.at[m, at, :], x_buf, buf_sem.at[0]),
            pltpu.make_async_copy(stream.at[m, at, :], stream_buf, buf_sem.at[1]),
        )

    for copy in token_loads(0, 0):
        copy.start()
    gain = par[4:5, :].astype(F32)
    gain_sum = jnp.zeros((1, p.D), F32)
    shift_sum = jnp.zeros((1, p.D), F32)
    for m in range(p.M):
        for piece in range(p.pieces):
            at = slice(piece * BQ, (piece + 1) * BQ)
            for core in range(CORES):
                dst = da_home.at[m, pl.ds(piece * BQ, BQ), pl.ds(core * half, half)]
                pltpu.make_async_copy(dst, dst, dh_r.at[m, core, piece]).wait()
            for copy in token_loads(m, piece):
                copy.wait()
            values = x_buf[...].astype(F32)
            dy = da_home[m, at, :].astype(F32)
            centre = values - jnp.mean(values, axis=-1, keepdims=True)
            spread = jnp.mean(centre * centre, axis=-1, keepdims=True)
            scale = lax.rsqrt(spread + EPS)
            wn = centre * scale
            e = dy * gain
            dw = scale * (e - jnp.mean(e, axis=-1, keepdims=True) - wn * jnp.mean(e * wn, axis=-1, keepdims=True))
            input_grad[m, at, :] = (stream_buf[...] + dw).astype(BF16)
            if m * p.pieces + piece + 1 < p.M * p.pieces:
                follow = m * p.pieces + piece + 1
                for copy in token_loads(follow // p.pieces, follow % p.pieces):
                    copy.start()
            gain_sum = gain_sum + jnp.sum(dy * wn, axis=0, keepdims=True)
            shift_sum = shift_sum + jnp.sum(dy, axis=0, keepdims=True)
    for n in range(p.S):
        lanes = slice(n * width, (n + 1) * width)
        small_acc[n, 4:5, 0:width] = gain_sum[:, lanes]
        small_acc[n, 8:9, 0:width] = shift_sum[:, lanes]

    def tiny(n):
        to = lax.rem(s + n, p.S)
        return remote(small_acc.at[to], small_in.at[n], ss_s.at[n], ss_r.at[n], to, here.r)

    for n in range(1, p.S):
        tiny(n).start()
    sums.twin_to_mate()
    total = small_acc[s]
    for n in range(1, p.S):
        tiny(n).wait_recv()
        total = total + small_in[n]
    small_all[here.r] = total

    def every(n):
        to = lax.rem(here.r + n, p.R)
        return remote(small_all.at[here.r], small_all.at[here.r], sa_s.at[n], sa_r.at[here.r], s, to)

    for n in range(1, p.R):
        every(n).start()
    for n in range(1, p.R):
        off = lax.rem(here.r + n, p.R)
        remote(small_all.at[0], small_all.at[off], sa_s.at[n], sa_r.at[off], s, here.r).wait_recv()
    total = small_all[0]
    for n in range(1, p.R):
        total = total + small_all[n]
    small_out[...] = total

    for m in range(p.M):
        for g in range(p.groups):
            sent(*do_copy(m, g))

    def da_sent(n, carry):
        i = block_of(n)
        da_mate(n, i).wait_send()

        @pl.when(n < far_blocks)
        def _():
            da_over(n, i).wait_send()

        @pl.when(n >= far_blocks)
        def _():
            sent(*da_back(n, i))

        return carry

    lax.fori_loop(0, p.nq, da_sent, 0)
    to_twin_dw().wait_send()
    for n in range(nz - 1):
        dw_send(n).wait_send()
    for n in range(1, 8):
        src, dst, to = dw_give(n)
        remote(src, dst, wd_s.at[n], wd_r.at[slot], *to).wait_send()
    for n in range(p.groups * p.pairs):

        @pl.when(n != slot)
        def _():
            remote(gq.at[n], gq.at[n], wd_s.at[0], wd_r.at[n], s, here.r).wait_recv()

    for n in range(1, p.S):
        tiny(n).wait_send()
    for n in range(1, p.R):
        every(n).wait_send()
    sums.drain()


def back(plan, units, small, grads):
    p = plan
    nw = len(grads)
    nz = p.S // 2
    planes = p.R // CORES
    split = [split_rows(p, grad) for grad in grads]
    shapes = [h.shape[2:] for h in split]
    any_space = pl.BlockSpec(memory_space=pl.ANY)
    vmem = pl.BlockSpec(memory_space=pltpu.VMEM)
    dma = pltpu.SemaphoreType.DMA
    shape = jax.ShapeDtypeStruct
    half = p.D // CORES
    outs = pl.pallas_call(
        functools.partial(back_kernel, p, nw),
        out_shape=[
            shape((p.M, p.T, p.D), BF16),
            shape((p.groups * p.pairs, p.width, 3 * PAIR), BF16),
            shape(small.shape[1:], F32),
        ]
        + [shape((CORES,) + sh, BF16) for sh in shapes],
        in_specs=[vmem] * 6 + [any_space] * 2 + [vmem] + [any_space] * 2 + [vmem] * 2 + [any_space] * nw,
        out_specs=[vmem] * (3 + nw),
        scratch_shapes=[
            pltpu.VMEM((LEN, p.W), BF16),
            pltpu.VMEM((p.pairs, LEN, 3 * PAIR), BF16),
            pltpu.VMEM((LEN, PAIR), F32),
            pltpu.VMEM((LEN, PAIR), F32),
            pltpu.VMEM((PAIR, LEN), BF16),
            pltpu.VMEM((LEN, half), BF16),
            pltpu.VMEM((LEN, half), BF16),
            pltpu.VMEM((LEN, half), BF16),
            pltpu.VMEM((p.near * p.T, half), BF16),
            pltpu.VMEM((p.D, 3 * PAIR), BF16),
            pltpu.VMEM((p.D, 3 * PAIR), BF16),
            pltpu.VMEM((p.D, 3 * PAIR), BF16),
            pltpu.VMEM((nz, 2 * p.width, 3 * PAIR), BF16),
            pltpu.VMEM((2 * p.width, 3 * PAIR), BF16),
            pltpu.VMEM(small.shape, F32),
            pltpu.VMEM(small.shape, F32),
            pltpu.VMEM((p.R,) + small.shape[1:], F32),
            dma((p.M, p.groups)), dma((p.P,)),
            dma((p.nq,)), dma((p.nq,)), dma((p.nq,)), dma((p.nq,)),
            dma((p.nq,)), dma((p.M, CORES, p.pieces)),
            dma((1,)), dma((1,)), dma((nz,)), dma((nz,)), dma((planes,)), dma((planes,)), dma((8,)), dma((8,)),
            dma((p.S,)), dma((p.S,)), dma((p.R,)), dma((p.R,)),
        ]
        + GridSum.scratch(p, shapes)
        + [pltpu.VMEM((BQ, p.D), BF16), pltpu.VMEM((BQ, p.D), F32), dma((2,))]
        + [pltpu.VMEM((2, LEN, BQ), BF16), dma((2,))],
        compiler_params=pltpu.CompilerParams(
            collective_id=1, has_side_effects=True, vmem_limit_bytes=VMEM_LIMIT
        ),
        name="back",
    )(*units, small, *split)
    gq = outs[1].reshape(p.groups, p.pairs, p.width, 3, PAIR).transpose(2, 3, 0, 1, 4).reshape(p.width, 3 * p.D)
    return outs[0], gq.astype(F32), outs[2], [whole_shard(part) for part in outs[3:]]


def per_device(
    sizes,
    inputs,
    prefix,
    qkv_weight,
    qv_bias,
    out_weight,
    branch_bias,
    up_weight,
    up_bias,
    down_weight,
    norm_gain,
    norm_bias,
    cotangent,
):
    p = Plan(sizes, (inputs.shape[0], 1, inputs.shape[2], inputs.shape[3]))
    tokens_all = p.M * p.T
    x = inputs[:, 0]
    width = p.D // p.S
    spare = max(128 - width, 0)
    par = jnp.concatenate([qv_bias, branch_bias, norm_gain, norm_bias, up_bias.reshape(-1, width)], axis=0)
    par = jnp.pad(par, ((0, 0), (0, spare)))
    pre = jnp.broadcast_to(prefix[:, 0].reshape(-1, 1).astype(F32), (p.M * p.Q, 128))
    pre = jnp.pad(pre, ((0, 8 - p.M * p.Q), (0, 0)))
    (_, wo, wu, wd, parf, _, q, k, v, o, lse, preu, o_home, a_unit, w_unit) = fore(
        p, x, par, pre, (qkv_weight, out_weight, up_weight, down_weight)
    )
    par32 = parf.astype(F32)
    bias_branch = par32[2:4]
    gains, shifts = par32[4:8], par32[8:12]
    bias_up = par32[12:].reshape(-1, p.S, width).transpose(1, 0, 2).reshape(-1)

    tokens = x.reshape(tokens_all, p.D).astype(F32)
    upstream = cotangent[:, 0].reshape(tokens_all, p.D).astype(F32)
    mixed_low = o_home.reshape(tokens_all, p.D)
    branch = dot(mixed_low, wo) + bias_branch[0]
    side, pull_side = jax.vjp(normed, branch, gains[1:2], shifts[1:2])
    stream = tokens + side
    normal_mid, pull_mid = jax.vjp(normed, stream, gains[2:3], shifts[2:3])
    middle_low = normal_mid.astype(BF16)
    upper = dot(middle_low, wu) + bias_up
    below = 0.5 * (1.0 + lax.erf(upper * math.sqrt(0.5)))
    slope = below + upper * jnp.exp(-0.5 * upper * upper) * (1.0 / math.sqrt(2.0 * math.pi))
    active_low, slope = lax.optimization_barrier(((upper * below).astype(BF16), slope))
    lower = dot(active_low, wd) + bias_branch[1]
    closing, pull_close = jax.vjp(normed, lower, gains[3:4], shifts[3:4])
    output = (stream + closing).astype(BF16)
    grad_lower, gain_three, shift_three = pull_close(upstream)
    lower_low = grad_lower.astype(BF16)
    grad_active = dot(lower_low, wd, 1, 1)
    upper_low = (grad_active * slope).astype(BF16)
    grad_middle = dot(upper_low, wu, 1, 1)
    grad_mid_in, gain_two, shift_two = pull_mid(grad_middle)
    grad_stream = grad_mid_in + upstream
    grad_branch, gain_one, shift_one = pull_side(grad_stream)
    branch_low = grad_branch.astype(BF16)
    grad_mixed = dot(branch_low, wo, 1, 1).astype(BF16)

    grads = (
        dot(active_low, lower_low, 0, 0).astype(BF16),
        dot(middle_low, upper_low, 0, 0).astype(BF16),
        dot(mixed_low, branch_low, 0, 0).astype(BF16),
    )
    def column_sum(values):
        return jnp.sum(values.astype(F32), axis=0, keepdims=True)

    du_sum = column_sum(upper_low).reshape(p.S, -1, width).transpose(1, 0, 2).reshape(-1, p.D)
    none = jnp.zeros((1, p.D), F32)
    small = jnp.concatenate(
        [
            none, none, column_sum(branch_low), column_sum(lower_low),
            none, gain_one, gain_two, gain_three,
            none, shift_one, shift_two, shift_three,
            du_sum,
        ], axis=0,
    )
    small = jnp.pad(small.reshape(-1, p.S, width).transpose(1, 0, 2), ((0, 0), (0, 0), (0, spare)))
    by_token = (p.M, p.T, p.D)
    input_grad, sum_qkv, tiny, (sum_down, sum_up, sum_out) = back(
        p,
        (
            q, k, v, o, lse, preu, grad_mixed.reshape(by_token), a_unit, w_unit,
            x, grad_stream.reshape(by_token), parf,
        ),
        small, grads,
    )
    tiny = tiny[:, :width]
    shaped = (p.M, 1, p.T, p.D)
    return (
        output.reshape(shaped),
        input_grad.reshape(shaped),
        sum_qkv,
        tiny[0:2],
        sum_out,
        tiny[2:4],
        sum_up,
        tiny[12:].reshape(-1),
        sum_down,
        tiny[4:8],
        tiny[8:12],
    )


def solution(mesh):
    sizes = {name: mesh.shape[name] for name in ("shard", "replica")}
    placed = (
        P(None, "replica", "shard", None),
        P(None, "replica", None),
        P("shard", None),
        P(None, "shard"),
        P("shard", None),
        P(None, "shard"),
        P("shard", None),
        P("shard"),
        P("shard", None),
        P(None, "shard"),
        P(None, "shard"),
        P(None, "replica", "shard", None),
    )
    return jax.shard_map(
        functools.partial(per_device, sizes),
        mesh=mesh,
        in_specs=placed,
        out_specs=(
            P(None, "replica", "shard", None),
            P(None, "replica", "shard", None),
            P("shard", None),
            P(None, "shard"),
            P("shard", None),
            P(None, "shard"),
            P("shard", None),
            P("shard"),
            P("shard", None),
            P(None, "shard"),
            P(None, "shard"),
        ),
        check_vma=False,
    )
```

```python
import functools
import math

import jax
import jax.numpy as jnp
from jax import lax
from jax.experimental import pallas as pl
from jax.experimental.pallas import tpu as pltpu
from jax.sharding import PartitionSpec as P

HEAD = 64
LEN = 2048
CORES = 2
PAIR = 2 * HEAD
BQ = 256
EPS = 1e-05
MASKED = -1e30
SCALE = HEAD ** (-0.5)
SCALE2 = SCALE * math.log2(math.e)
F32 = jnp.float32
BF16 = jnp.bfloat16
MESH = pl.DeviceIdType.MESH
VMEM_LIMIT = 66_000_000
LAG = 2
KEYS = 512
SIDE_FIRST = (True, False, False)
SUM_LAG = 5
CADENCE = 1
COLUMN_FIRST = (True, True, False)
START = 1
EARLY = 1


class Plan:
    def __init__(self, mesh_shape, inputs_shape):
        self.S = mesh_shape["shard"]
        self.R = mesh_shape["replica"]
        self.M, _, self.T, self.D = inputs_shape
        self.Q = self.T * self.S // LEN
        self.P = LEN // self.T
        self.U = self.M * self.Q * CORES
        self.cpu = self.S // self.U
        self.heads = self.D // HEAD
        self.W = self.D // (CORES * self.cpu)
        self.pairs = self.W // PAIR
        self.groups = CORES * self.cpu
        self.pieces = self.T // BQ
        self.nq = LEN // BQ
        self.near = self.P // self.cpu
        self.width = self.D // self.S
        assert self.cpu == 2 and self.pairs == 2 and self.T % BQ == 0 and LEN % self.T == 0


class Place:
    def __init__(self, plan):
        self.p = plan
        self.s = lax.axis_index("shard")
        self.r = lax.axis_index("replica")
        self.c = lax.rem(self.r, CORES)
        self.chip = self.r - self.c
        self.mate = self.chip + (1 - self.c)
        self.unit = self.s // plan.cpu
        self.lane = lax.rem(self.s, plan.cpu)
        self.group = self.c * plan.cpu + self.lane
        self.uc = lax.rem(self.unit, CORES)
        self.um = lax.rem(self.unit // CORES, plan.M)
        self.uq = self.unit // (CORES * plan.M)
        self.ring = self.to_ring(self.s)
        self.plane = self.r // CORES
        self.side = lax.rem(self.plane, 2)
        self.twin = self.r + CORES * (1 - 2 * self.side)
        self.row = self.s // 2
        self.col = lax.rem(self.s, 2)
        self.beside = 2 * self.row + 1 - self.col
        self.rows = plan.S // 2

    def unit_of(self, c, m, s):
        return ((s // self.p.P) * self.p.M + m) * CORES + c

    def to_ring(self, s):
        half = self.p.S // 2
        row, col = s // 2, lax.rem(s, 2)
        return row + col * (2 * half - 1 - 2 * row)

    def from_ring(self, i):
        n = self.p.S
        return jnp.where(i < n // 2, 2 * i, 2 * (n - 1 - i) + 1)


def remote(src, dst, send, recv, s, r):
    return pltpu.make_async_remote_copy(
        src_ref=src, dst_ref=dst, send_sem=send, recv_sem=recv, device_id=(s, r), device_id_type=MESH
    )


def launch(away, far, near):
    @pl.when(away)
    def _():
        far().start()

    @pl.when(jnp.logical_not(away))
    def _():
        pltpu.make_async_copy(*near).start()


def sent(away, far, near):
    @pl.when(away)
    def _():
        far().wait_send()


def greet(peers):
    barrier = pltpu.get_barrier_semaphore()
    for s, r in peers:
        pl.semaphore_signal(barrier, inc=1, device_id=(s, r), device_id_type=MESH)
    pl.semaphore_wait(barrier, len(peers))


def plane_peers(here):
    n = here.p.S * CORES
    own = here.s * CORES + here.c
    out = []
    for k in range(1, n):
        i = lax.rem(own + k, n)
        out.append((i // CORES, here.chip + lax.rem(i, CORES)))
    return out


def normed(values, gain, shift):
    centre = values - jnp.mean(values, axis=-1, keepdims=True)
    spread = jnp.mean(centre * centre, axis=-1, keepdims=True)
    return centre * lax.rsqrt(spread + EPS) * gain + shift


def dot(a, b, ca=1, cb=0):
    return lax.dot_general(a, b, (((ca,), (cb,)), ((), ())), preferred_element_type=F32)


def head_lanes(rows, which):
    lane = lax.broadcasted_iota(jnp.int32, (rows, PAIR), 1)
    return (lane < HEAD) if which == 0 else (lane >= HEAD)


def fore_kernel(
    plan, x, par, pre, wq, wo, wu, wd,
    wof, wuf, wdf, parf, ah, q_out, k_out, v_out, o_out, lse_out, preu, oh, a_all, wcol,
    parg, pre2,
    par_ss, par_rs, pre_sem, loc_sem, a_ss, a_rs, af_ss, z_ss, z_rs, wa_ss, wa_rs, wb_ss, wb_rs, wm_ss, wm_rs,
    o_ss, o_rs, q_ss, q_rs, qt_ss, qt_rs, q_loc,
):
    p = plan
    here = Place(p)
    s, c = here.s, here.c
    mine, full = (wo, wu, wd), (wof, wuf, wdf)
    nw = len(mine)
    first = COLUMN_FIRST
    greet(plane_peers(here) + [(s, here.twin)])

    parg[s] = par[...]
    small = []
    for k in range(1, p.S):
        to = lax.rem(s + k, p.S)
        small.append(remote(par, parg.at[s], par_ss.at[k], par_rs.at[k], to, here.r))
        small[-1].start()
    swap = remote(pre, pre2, pre_sem.at[0], pre_sem.at[1], s, here.mate)
    swap.start()

    z, nz = here.row, here.rows

    def where(w, zr, fa, fb, core):
        fy, fx = (fa, fb) if first[w] else (fb, fa)
        col = here.col if fy == 0 else 1 - here.col
        side = here.side if fx == 0 else 1 - here.side
        n, width = mine[w].shape[0], mine[w].shape[1] // 2
        rows = pl.ds(pl.multiple_of((2 * zr + col) * n + core * (n // 2), n // 2), n // 2)
        return full[w].at[rows, pl.ds(pl.multiple_of(side * width, width), width)]

    def origin(w, fa):
        n, width = mine[w].shape[0], mine[w].shape[1] // 2
        side = here.side if fa == 0 else 1 - here.side
        rows = pl.ds(pl.multiple_of(c * (n // 2), n // 2), n // 2)
        return mine[w].at[rows, pl.ds(pl.multiple_of(side * width, width), width)]

    def peer(w, second):
        return (here.beside, here.r) if first[w] == (second == 0) else (s, here.twin)

    def z_send(w, d, k):
        sign = 1 - 2 * d
        part = where(w, z - sign * (k - 1), 0, 0, c)
        src = origin(w, 0) if isinstance(k, int) and k == 1 else part
        return remote(src, part, z_ss.at[w, d, k - 1], z_rs.at[w, d, k - 1], s + 2 * sign, here.r)

    def z_came(w, d, k):
        sign = 1 - 2 * d
        part = where(w, z - sign * k, 0, 0, c)
        return remote(part, part, z_ss.at[w, d, k - 1], z_rs.at[w, d, k - 1], s, here.r)

    def to_first(w, zr, src=None):
        part = where(w, zr, 0, 0, c)
        return remote(part if src is None else src, part, wa_ss.at[w, zr], wa_rs.at[w, zr], *peer(w, 0))

    def to_second(w, fa, zr, src=None):
        part = where(w, zr, fa, 0, c)
        return remote(part if src is None else src, part, wb_ss.at[w, fa, zr], wb_rs.at[w, fa, zr], *peer(w, 1))

    def to_mate(w, fa, fb, zr, core):
        part = where(w, zr, fa, fb, core)
        at = 2 * fa + fb
        return remote(part, part, wm_ss.at[w, at, zr], wm_rs.at[w, at, zr], s, here.mate)

    def first_came(w, zr):
        part = where(w, zr, 1, 0, c)
        return remote(part, part, wa_ss.at[w, zr], wa_rs.at[w, zr], s, here.r)

    def second_came(w, fa, zr):
        part = where(w, zr, fa, 1, c)
        return remote(part, part, wb_ss.at[w, fa, zr], wb_rs.at[w, fa, zr], s, here.r)

    def on_grid(d, k):
        return z >= k if d == 0 else z + k < nz

    def can_send(d):
        return z < nz - 1 if d == 0 else z > 0

    def gather_rows(w):
        for d in (0, 1):

            @pl.when(can_send(d))
            def _():
                z_send(w, d, 1).start()

    def gather_near(w):
        if first[w]:
            to_first(w, z, origin(w, 0)).start()
        else:
            to_second(w, 0, z, origin(w, 0)).start()
            to_second(w, 1, z, origin(w, 1)).start()

    def gather_slot(w, k, lag):
        for d in (0, 1):
            sign = 1 - 2 * d

            @pl.when(jnp.logical_and(k >= 1, on_grid(d, k)))
            def _():
                at = jnp.maximum(k, 1)
                z_came(w, d, at).wait_recv()
                zr = z - sign * at

                @pl.when(can_send(d))
                def _():
                    z_send(w, d, at + 1).start()

                to_first(w, zr).start()
                to_second(w, 0, zr).start()
                to_mate(w, 0, 0, zr, c).start()

        def at_distance(j, least, body):
            for d in (0, 1):
                ok = jnp.logical_and(j >= max(least, d), on_grid(d, j))

                @pl.when(ok)
                def _():
                    body(z - (1 - 2 * d) * jnp.maximum(j, 0))

        def after_first(zr):
            first_came(w, zr).wait_recv()
            to_second(w, 1, zr).start()
            to_mate(w, 1, 0, zr, c).start()

        at_distance(k - 1, 0 if first[w] else 1, after_first)

        def after_second(fa):
            def body(zr):
                second_came(w, fa, zr).wait_recv()
                to_mate(w, fa, 1, zr, c).start()

            return body

        at_distance(k - 1 - lag, 1 if first[w] else 0, after_second(0))
        at_distance(k - 2 - lag, 0, after_second(1))

    def mate_pieces(w, zr, act):
        other = zr != z

        @pl.when(other)
        def _():
            act(0, 0)

        if first[w]:

            @pl.when(other)
            def _():
                act(0, 1)

            act(1, 0)
        else:

            @pl.when(other)
            def _():
                act(1, 0)

            act(0, 1)
        act(1, 1)

    def gather_wait(w):
        def one(zr, carry):
            mate_pieces(w, zr, lambda fa, fb: to_mate(w, fa, fb, zr, 1 - c).wait_recv())
            return carry

        lax.fori_loop(0, nz, one, 0)

    def gather_drain(w):
        def one(zr, carry):
            mate_pieces(w, zr, lambda fa, fb: to_mate(w, fa, fb, zr, c).wait_send())
            if first[w]:
                to_first(w, zr).wait_send()

                @pl.when(zr != z)
                def _():
                    to_second(w, 0, zr).wait_send()
            else:

                @pl.when(zr != z)
                def _():
                    to_first(w, zr).wait_send()

                to_second(w, 0, zr).wait_send()
            to_second(w, 1, zr).wait_send()
            for d in (0, 1):
                reach = zr <= z if d == 0 else zr < nz - z

                @pl.when(jnp.logical_and(can_send(d), reach))
                def _():
                    z_send(w, d, zr + 1).wait_send()

            return carry

        lax.fori_loop(0, nz, one, 0)

    nq_rows = wq.shape[2]
    half_rows = nq_rows // 2

    def q_rows(k, side):
        return pl.ds(pl.multiple_of(k * nq_rows + side * half_rows, half_rows), half_rows)

    def q_send(k):
        to = lax.rem(s + k, p.S)
        group = c * p.cpu + lax.rem(to, p.cpu)
        rows = pl.ds(pl.multiple_of(here.side * half_rows, half_rows), half_rows)
        src = wq.at[group, :, rows, :]
        return remote(src, wcol.at[:, q_rows(s, here.side), :], q_ss.at[k], q_rs.at[s], to, here.r)

    def q_twin(k, side):
        part = wcol.at[:, q_rows(k, side), :]
        return remote(part, part, qt_ss.at[k], qt_rs.at[k], s, here.twin)

    def q_from(k):
        return lax.rem(s + p.S - k, p.S)

    for k in range(1, p.S):
        q_send(k).start()
    for w in range(nw):
        gather_near(w)
    q_own = pltpu.make_async_copy(
        wq.at[here.group], wcol.at[:, pl.ds(pl.multiple_of(s * nq_rows, nq_rows), nq_rows), :], q_loc.at[0]
    )
    q_own.start()
    local = []
    for w in range(nw):
        n = mine[w].shape[0]
        local.append(
            pltpu.make_async_copy(mine[w], full[w].at[pl.ds(pl.multiple_of(s * n, n), n), :], loc_sem.at[w])
        )
        local[-1].start()

    for k in range(1, p.S):
        small[k - 1].wait_recv()
    parf[...] = jnp.concatenate([parg[k][:, : p.D // p.S] for k in range(p.S)], axis=1)
    gain = parf[4:5, :].astype(F32)
    shift = parf[8:9, :].astype(F32)
    rows_here = pl.ds(pl.multiple_of(lax.rem(s, p.P) * p.T, p.T), p.T)

    def first_hop(m):
        to = here.unit_of(c, m, s) * p.cpu + here.lane
        far = lambda: remote(ah.at[m], a_all.at[rows_here, :], a_ss.at[m], a_rs.at[lax.rem(s, p.P)], to, here.r)
        return to, far

    for m in range(p.M):
        ah[m] = normed(x[m].astype(F32), gain, shift).astype(BF16)
        to, far = first_hop(m)

        @pl.when(to != s)
        def _():
            far().start()

        @pl.when(to == s)
        def _():
            a_all[rows_here, :] = ah[m]

    primary = c == here.uc

    def a_rows(j):
        return pl.ds(pl.multiple_of(j * p.T, p.T), p.T)

    def a_forward(j, k):
        part = a_all.at[a_rows(j), :]
        if k == 0:
            return remote(part, part, af_ss.at[j, 0], a_rs.at[j], s, here.mate)
        to = here.unit * p.cpu + lax.rem(here.lane + k, p.cpu)
        return remote(part, part, af_ss.at[j, k], a_rs.at[j], to, here.r)

    def a_wait(j):
        part = a_all.at[a_rows(j), :]
        remote(part, part, af_ss.at[j, 0], a_rs.at[j], s, here.mate).wait_recv()

    near = p.near

    zi = here.unit - here.uq * near

    def a_at(k, body):
        for d in (0, 1):
            if k or not d:
                ok = zi >= k if d == 0 else zi + k < near

                @pl.when(jnp.logical_and(primary, ok))
                def _():
                    body(zi - (1 - 2 * d) * k)

    def a_near(jj):
        j = jj * p.cpu + here.lane

        @pl.when(here.uq * p.P + j != s)
        def _():
            a_wait(j)

        for k in list(range(1, p.cpu)) + [0]:
            a_forward(j, k).start()

    def a_far(jj):
        for k in range(1, p.cpu):
            j = jj * p.cpu + lax.rem(here.lane + k, p.cpu)
            a_wait(j)
            a_forward(j, 0).start()

    each = -(-(p.S - 1) // near)
    for k in range(near + 1):
        if k < near:
            for n in range(1 + k * each, min(1 + (k + 1) * each, p.S)):
                part = wcol.at[:, q_rows(q_from(n), here.side), :]
                remote(part, part, q_ss.at[n], q_rs.at[q_from(n)], s, here.r).wait_recv()
                q_twin(q_from(n), here.side).start()
            a_at(k, a_near)
        if k == START:
            for w in range(nw):
                gather_rows(w)
        if k >= 1:
            a_at(k - 1, a_far)
        if k >= near + 1 - EARLY:
            for w in range(nw):
                gather_slot(w, k - (near - EARLY), LAG)

    @pl.when(jnp.logical_not(primary))
    def _():
        for j in range(p.P):
            a_wait(j)

    swap.wait_recv()
    pre2[...] = jnp.where(primary, pre[...], pre2[...])
    row = here.um * p.Q + here.uq
    preu[...] = jnp.broadcast_to(pre2[pl.ds(row, 1), :], preu.shape)

    for n in range(1, p.S):
        q_twin(q_from(n), 1 - here.side).wait_recv()
    q_own.wait()
    own = pl.ds(pl.multiple_of(here.group * p.W, PAIR), p.W)
    q_bias = parf[0:1, own].astype(F32)
    v_bias = parf[1:2, own].astype(F32)

    def project(i, carry):
        rows = pl.ds(pl.multiple_of(i * BQ, BQ), BQ)
        part = a_all[rows, :]
        for h in range(p.pairs):
            lanes = slice(h * PAIR, (h + 1) * PAIR)
            got = dot(part, wcol[h])
            q_out[rows, lanes] = (got[:, :PAIR] + q_bias[:, lanes]).astype(BF16)
            k_out[rows, lanes] = got[:, PAIR : 2 * PAIR].astype(BF16)
            v_out[rows, lanes] = (got[:, 2 * PAIR :] + v_bias[:, lanes]).astype(BF16)
        return carry

    lax.fori_loop(0, p.nq, project, 0)

    prefix = preu[0:1, 0:1]
    slots = nz + 1 + LAG - EARLY
    per = -(-slots // p.nq)

    def o_copy(i):
        rows = pl.ds(pl.multiple_of(i * BQ, BQ), BQ)
        home = here.uq * p.P + i // p.pieces
        piece = lax.rem(i, p.pieces)
        there = pl.ds(pl.multiple_of(piece * BQ, BQ), BQ)
        src = o_out.at[rows, :]
        dst = oh.at[here.um, there, own]
        away = jnp.logical_or(home != s, here.uc != c)
        recv = o_rs.at[here.um, here.group, piece]
        return away, lambda: remote(src, dst, o_ss.at[i], recv, home, here.chip + here.uc), (src, dst, recv)

    def attend(i, carry):
        rows = pl.ds(pl.multiple_of(i * BQ, BQ), BQ)
        row_pos = (lax.broadcasted_iota(jnp.int32, (BQ, 1), 0) + i * BQ + 1).astype(F32)
        bound = jnp.maximum(row_pos, prefix)
        key_pos = lax.broadcasted_iota(jnp.int32, (1, LEN), 1).astype(F32)
        seen = key_pos < bound

        def pair_step(h, inner):
            lanes = pl.ds(pl.multiple_of(h * PAIR, PAIR), PAIR)
            qp, kp, vp = q_out[rows, lanes], k_out[:, lanes], v_out[:, lanes]
            halves = []
            for e in (0, 1):
                logits = dot(jnp.where(head_lanes(BQ, e), qp, jnp.zeros_like(qp)), kp, 1, 1)
                logits = jnp.where(seen, logits, MASKED)
                top = jnp.max(logits, axis=1, keepdims=True)
                powers = jnp.exp2((logits - top) * SCALE2)
                total = jnp.sum(powers, axis=1, keepdims=True)
                halves.append(dot(powers.astype(BF16), vp) * (1.0 / total))
                level = top * SCALE2 + jnp.log2(total)
                turned = jnp.broadcast_to(level, (BQ, 128)).T
                lse_out[2 * h + e, :, pl.ds(pl.multiple_of(i * BQ, BQ), BQ)] = turned[0:8]
            o_out[rows, lanes] = jnp.where(head_lanes(BQ, 0), halves[0], halves[1]).astype(BF16)
            return inner

        lax.fori_loop(0, p.pairs, pair_step, 0)
        launch(*o_copy(i))

        for extra in range(per):
            for w in range(nw):
                gather_slot(w, i * per + extra + 1 + EARLY, LAG)

        return carry

    lax.fori_loop(0, p.nq, attend, 0)

    for m in range(p.M):
        for g in range(p.groups):
            for piece in range(p.pieces):
                src = o_out.at[pl.ds(0, BQ), :]
                dst = oh.at[m, pl.ds(piece * BQ, BQ), pl.ds(g * p.W, p.W)]
                pltpu.make_async_copy(src, dst, o_rs.at[m, g, piece]).wait()

    def o_sent(i, carry):
        sent(*o_copy(i))
        return carry

    lax.fori_loop(0, p.nq, o_sent, 0)
    for copy in small:
        copy.wait_send()
    swap.wait_send()
    for copy in local:
        copy.wait()
    for n in range(1, p.S):
        q_send(n).wait_send()
        q_twin(q_from(n), here.side).wait_send()
    for m in range(p.M):
        to, far = first_hop(m)

        @pl.when(to != s)
        def _():
            far().wait_send()

    @pl.when(primary)
    def _():
        for jj in range(near):
            for k in range(p.cpu):
                a_forward(jj * p.cpu + here.lane, k).wait_send()
            for k in range(1, p.cpu):
                a_forward(jj * p.cpu + lax.rem(here.lane + k, p.cpu), 0).wait_send()

    for w in range(nw):
        gather_wait(w)
        gather_drain(w)


def fore(plan, x, par, pre, qkv, weights):
    p = plan
    nz = p.S // 2
    nw = len(weights)
    any_space = pl.BlockSpec(memory_space=pl.ANY)
    vmem = pl.BlockSpec(memory_space=pltpu.VMEM)
    shape = jax.ShapeDtypeStruct
    out_shape = (
        [shape((w.shape[0] * p.S, w.shape[1]), BF16) for w in weights]
        + [shape((par.shape[0], p.D), BF16), shape((p.M, p.T, p.D), BF16)]
        + [shape((LEN, p.W), BF16)] * 4
        + [shape((2 * p.pairs, 8, LEN), F32), shape((8, 128), F32), shape((p.M, p.T, p.D), BF16)]
        + [shape((LEN, p.D), BF16), shape((p.pairs, p.D, 3 * PAIR), BF16)]
    )
    dma = pltpu.SemaphoreType.DMA
    return pl.pallas_call(
        functools.partial(fore_kernel, p),
        out_shape=out_shape,
        in_specs=[vmem] * (4 + nw),
        out_specs=[any_space] * nw + [vmem] * 11,
        scratch_shapes=[
            pltpu.VMEM((p.S,) + par.shape, BF16),
            pltpu.VMEM((8, 128), F32),
            dma((p.S,)), dma((p.S,)), dma((2,)), dma((nw,)),
            dma((p.M,)), dma((p.P,)), dma((p.P, p.cpu)),
            dma((nw, 2, nz)), dma((nw, 2, nz)), dma((nw, nz)), dma((nw, nz)),
            dma((nw, 2, nz)), dma((nw, 2, nz)), dma((nw, 4, nz)), dma((nw, 4, nz)),
            dma((p.nq,)), dma((p.M, p.groups, p.pieces)),
            dma((p.S,)), dma((p.S,)), dma((p.S,)), dma((p.S,)), dma((1,)),
        ],
        compiler_params=pltpu.CompilerParams(
            collective_id=0, has_side_effects=True, vmem_limit_bytes=VMEM_LIMIT
        ),
        name="fore",
    )(x, par, pre, qkv, *weights)


class GridSum:
    def __init__(self, here, grads, outs, refs):
        self.here, self.grads, self.outs = here, grads, outs
        self.nw = nw = len(grads)
        self.nz = here.rows
        self.planes = here.p.R // CORES
        self.own, self.acc, self.one, self.two, self.far = (refs[k * nw : (k + 1) * nw] for k in range(5))
        (self.ld, self.m_s, self.m_r, self.a_s, self.a_r, self.b_s, self.b_r, self.z_s, self.z_r) = refs[5 * nw : 5 * nw + 9]
        (self.x_s, self.x_r, self.t_s, self.t_r, self.f_s, self.f_r) = refs[5 * nw + 9 :]
        self.side_first = SIDE_FIRST

    @staticmethod
    def scratch(plan, shapes):
        nw = len(shapes)
        planes = plan.R // CORES
        nz = plan.S // 2
        dma = pltpu.SemaphoreType.DMA
        return (
            [pltpu.VMEM((2,) + sh, BF16) for sh in shapes]
            + [pltpu.VMEM((plan.S,) + sh, BF16) for sh in shapes]
            + [
                pltpu.VMEM((plan.S, sh[0], sh[1] // 2) if sf else (nz,) + sh, BF16)
                for sh, sf in zip(shapes, SIDE_FIRST)
            ]
            + [pltpu.VMEM((nz, sh[0], sh[1] // 2), BF16) for sh in shapes]
            + [pltpu.VMEM((max(nz, planes // 2), sh[0], sh[1] // 2), BF16) for sh in shapes]
            + [dma((nw,))]
            + [dma((nw, nz))] * 8
            + [dma((nw, planes))] * 2
            + [dma((nw,))] * 2
            + [dma((nw, 2))] * 2
        )

    @staticmethod
    def count(nw):
        return 5 * nw + 15

    def zr(self, k):
        return lax.rem(self.here.row + 1 + k, self.nz)

    def half(self, w, side):
        n = self.acc[w].shape[2] // 2
        return pl.ds(pl.multiple_of(side * n, n), n)

    def load(self, w, k):
        src = self.grads[w].at[pl.ds(2 * self.zr(k), 2), self.here.c]
        return pltpu.make_async_copy(src, self.own[w], self.ld.at[w])

    def swap(self, w, k):
        here = self.here
        pair = pl.ds(2 * self.zr(k), 2)
        return remote(
            self.grads[w].at[pair, 1 - here.c], self.acc[w].at[pair], self.m_s.at[w, k], self.m_r.at[w, k], here.s, here.mate
        )

    def first(self, w, k):
        here, zr = self.here, self.zr(k)
        if self.side_first[w]:
            pair = pl.ds(2 * zr, 2)
            src = self.acc[w].at[pair, :, self.half(w, 1 - here.side)]
            return remote(src, self.one[w].at[pair], self.a_s.at[w, k], self.a_r.at[w, k], here.s, here.twin)
        src = self.acc[w].at[2 * zr + 1 - here.col]
        return remote(src, self.one[w].at[zr], self.a_s.at[w, k], self.a_r.at[w, k], here.beside, here.r)

    def second(self, w, k):
        here, zr = self.here, self.zr(k)
        if self.side_first[w]:
            src = self.acc[w].at[2 * zr + 1 - here.col, :, self.half(w, here.side)]
            to = (here.beside, here.r)
        else:
            src = self.acc[w].at[2 * zr + here.col, :, self.half(w, 1 - here.side)]
            to = (here.s, here.twin)
        return remote(src, self.two[w].at[zr], self.b_s.at[w, k], self.b_r.at[w, k], *to)

    def final(self, w, k):
        here, zr = self.here, self.zr(k)
        src = self.acc[w].at[2 * zr + here.col, :, self.half(w, here.side)]
        return remote(
            src, self.far[w].at[here.row], self.z_s.at[w, k], self.z_r.at[w, here.row], 2 * zr + here.col, here.r
        )

    def begin(self):
        for k in range(self.nz):
            for w in range(self.nw):
                self.swap(w, k).start()
                if k == 0:
                    self.load(w, 0).start()

    def event_one(self, w, k):
        zr = self.zr(k)
        pair = pl.ds(2 * zr, 2)
        self.load(w, k).wait()
        self.swap(w, k).wait_recv()
        self.acc[w][pair] = (self.acc[w][pair].astype(F32) + self.own[w][...].astype(F32)).astype(BF16)
        self.first(w, k).start()

        @pl.when(k < self.nz - 1)
        def _():
            self.load(w, jnp.minimum(k + 1, self.nz - 1)).start()

    def event_two(self, w, k):
        here, zr = self.here, self.zr(k)
        self.first(w, k).wait_recv()
        acc = self.acc[w]
        if self.side_first[w]:
            pair = pl.ds(2 * zr, 2)
            lanes = self.half(w, here.side)
            acc[pair, :, lanes] = (acc[pair, :, lanes].astype(F32) + self.one[w][pair].astype(F32)).astype(BF16)
        else:
            at = 2 * zr + here.col
            acc[at] = (acc[at].astype(F32) + self.one[w][zr].astype(F32)).astype(BF16)
        self.second(w, k).start()

    def event_three(self, w, k):
        here, zr = self.here, self.zr(k)
        self.second(w, k).wait_recv()
        at, lanes = 2 * zr + here.col, self.half(w, here.side)
        self.acc[w][at, :, lanes] = (self.acc[w][at, :, lanes].astype(F32) + self.two[w][zr].astype(F32)).astype(BF16)

        @pl.when(k < self.nz - 1)
        def _():
            self.final(w, k).start()

    def slots(self):
        return CADENCE * (self.nw * self.nz + 2 * SUM_LAG)

    def slot(self, n):
        @pl.when(lax.rem(n, CADENCE) == 0)
        def _():
            self.event(n // CADENCE)

    def event(self, n):
        for stage, body in ((2, self.event_three), (1, self.event_two), (0, self.event_one)):
            e = n - stage * SUM_LAG
            for w in range(self.nw):
                ok = jnp.logical_and(e >= 0, e < self.nw * self.nz)

                @pl.when(jnp.logical_and(ok, lax.rem(e, self.nw) == w))
                def _():
                    body(w, jnp.maximum(e, 0) // self.nw)

    def over(self, w, k):
        here = self.here
        pairs = self.planes // 2
        to = 2 * lax.rem(here.plane // 2 + k, pairs) + here.side
        src = self.two[w].at[0]
        return remote(
            src, self.one_slot(w, here.plane // 2), self.x_s.at[w, k], self.x_r.at[w, here.plane // 2],
            here.s, to * CORES + here.c,
        )

    def one_slot(self, w, k):
        return self.acc[w].at[k, :, self.half(w, self.here.side)]

    def to_twin(self, w, side):
        part = self.outs[w].at[self.here.c, :, self.half(w, side)]
        return remote(part, part, self.t_s.at[w], self.t_r.at[w], self.here.s, self.here.twin)

    def to_mate(self, w, core, via):
        side = self.here.side if via == 0 else 1 - self.here.side
        part = self.outs[w].at[core, :, self.half(w, side)]
        return remote(part, part, self.f_s.at[w, via], self.f_r.at[w, via], self.here.s, self.here.mate)

    def finish(self):
        here = self.here
        for w in range(self.nw):
            self.far[w][here.row] = self.acc[w][here.s, :, self.half(w, here.side)]
            for k in range(self.nz - 1):
                off = lax.rem(here.row + 1 + k, self.nz)
                part = self.far[w].at[off]
                remote(part, part, self.z_s.at[w, k], self.z_r.at[w, off], here.s, here.r).wait_recv()
            total = self.far[w][0].astype(F32)
            for k in range(1, self.nz):
                total = total + self.far[w][k].astype(F32)
            self.outs[w][here.c, :, self.half(w, here.side)] = total.astype(BF16)
            self.to_twin(w, here.side).start()
            self.to_mate(w, here.c, 0).start()

    def twin_to_mate(self):
        for w in range(self.nw):
            self.to_twin(w, 1 - self.here.side).wait_recv()
            self.to_mate(w, self.here.c, 1).start()

    def drain(self):
        for w in range(self.nw):
            for via in (0, 1):
                self.to_mate(w, 1 - self.here.c, via).wait_recv()
                self.to_mate(w, self.here.c, via).wait_send()
            self.to_twin(w, self.here.side).wait_send()
            for k in range(self.nz):
                self.swap(w, k).wait_send()
                self.first(w, k).wait_send()
                self.second(w, k).wait_send()
                if k < self.nz - 1:
                    self.final(w, k).wait_send()


def sum_peers(here):
    p = here.p
    planes = p.R // CORES
    far = [(here.s, lax.rem(here.plane + k, planes) * CORES + j) for k in range(1, planes) for j in range(CORES)]
    twin_chip = here.twin - here.c
    return plane_peers(here) + far + [(here.beside, twin_chip + j) for j in range(CORES)]


def split_rows(p, grad):
    rows, cols = grad.shape
    return grad.reshape(p.S, CORES, rows // (p.S * CORES), cols)


def whole_shard(halves):
    return halves.reshape(CORES * halves.shape[1], halves.shape[2]).astype(F32)


def back_kernel(plan, nw, *refs):
    p = plan
    here = Place(p)
    s, c = here.s, here.c
    nz, near, width = here.rows, p.near, p.width
    (q, k, v, o, lse, preu, do_home, a_all, wcol, x, stream, par, small) = refs[:13]
    grads = refs[13 : 13 + nw]
    rest = refs[13 + nw :]
    input_grad, gq, small_out = rest[:3]
    outs = rest[3 : 3 + nw]
    rest = rest[3 + nw :]
    (do_all, low, dk_acc, dv_acc, k_turn, da_own, da_out, da_in, da_side) = rest[:9]
    x_buf, stream_buf, buf_sem, a_buf, a_sem = rest[-5:]
    rest = rest[:-5]
    da_home = input_grad
    (dw_out, dw_own, dw_in, dw_far, dw_end, small_acc, small_in, small_all) = rest[9:17]
    (do_ss, do_rs, dm_s, dm_r, dy_s, dy_r, dh_s, dh_r, wt_s, wt_r, wz_s, wz_r, wx_s, wx_r, wd_s, wd_r) = rest[17:33]
    (ss_s, ss_r, sa_s, sa_r) = rest[33:37]
    sums = GridSum(here, grads, outs, rest[37:])
    greet(sum_peers(here))
    rows_here = pl.ds(pl.multiple_of(lax.rem(s, p.P) * p.T, p.T), p.T)

    def do_copy(m, g):
        core, lane = g // p.cpu, g % p.cpu
        to = here.unit_of(c, m, s) * p.cpu + lane
        src = do_home.at[m, :, pl.ds(g * p.W, p.W)]
        dst = do_all.at[rows_here, :]
        away = jnp.logical_or(to != s, c != core)
        recv = do_rs.at[lax.rem(s, p.P)]
        return away, lambda: remote(src, dst, do_ss.at[m, g], recv, to, here.chip + core), (src, dst, recv)

    for m in range(p.M):
        for g in range(p.groups):
            launch(*do_copy(m, g))
    sums.begin()
    small_acc[...] = small[...]
    prefix = preu[0:1, 0:1]

    def block_rows(i):
        return pl.ds(pl.multiple_of(i * BQ, BQ), BQ)

    def a_load(b):
        slot = lax.rem(b, 2)
        return pltpu.make_async_copy(
            a_all.at[:, pl.ds(pl.multiple_of(b * BQ, BQ), BQ)], a_buf.at[slot], a_sem.at[slot]
        )

    def weight_part(h, dst, slot_from=None):
        def some(b, carry):
            slot = lax.rem(b, 2)

            @pl.when(b < p.D // BQ - 1)
            def _():
                a_load(b + 1).start()

            a_load(b).wait()
            dst[pl.ds(pl.multiple_of(b * BQ, BQ), BQ), :] = dot(a_buf[slot], low[h], 0, 0).astype(BF16)
            if slot_from is not None:
                sums.slot(slot_from + b)
            return carry

        lax.fori_loop(0, p.D // BQ, some, 0)

    def bias_part(h):
        folds = PAIR // width
        for row, lanes in ((0, slice(0, PAIR)), (1, slice(2 * PAIR, 3 * PAIR))):
            total = jnp.sum(low[h, :, lanes].astype(F32), axis=0, keepdims=True)
            for n in range(folds):
                at = (here.group * p.pairs + h) * folds + n
                small_acc[at, row : row + 1, 0:width] = total[:, n * width : (n + 1) * width]

    def to_twin_dw():
        return remote(dw_out, dw_in, wt_s.at[0], wt_r.at[0], s, here.twin)

    def pair_step(turn, carry):
        h = lax.rem(turn + 1 + here.side, 2)
        lanes = pl.ds(pl.multiple_of(h * PAIR, PAIR), PAIR)
        k_turn[...] = k[:, lanes].astype(F32).T.astype(BF16)
        dk_acc[...] = jnp.zeros_like(dk_acc)
        dv_acc[...] = jnp.zeros_like(dv_acc)

        def query_step(n, inner):
            j = lax.rem((here.unit - here.uq * near) * p.cpu + n // p.pieces, p.P)
            i = j * p.pieces + lax.rem(n, p.pieces)
            rows = block_rows(i)

            @pl.when(jnp.logical_and(turn == 0, lax.rem(n, p.pieces) == 0))
            def _():
                part = do_all.at[pl.ds(pl.multiple_of(j * p.T, p.T), p.T), :]
                pltpu.make_async_copy(part, part, do_rs.at[j]).wait()

            qp, dop, op = q[rows, lanes], do_all[rows, lanes], o[rows, lanes]
            turned = (dop.astype(F32) * op.astype(F32)).T
            pos = (lax.broadcasted_iota(jnp.int32, (1, BQ), 1) + i * BQ + 1).astype(F32)
            bound = jnp.maximum(pos, prefix)
            dq_t = []
            for e in (0, 1):
                lit = head_lanes(BQ, e)
                qe = jnp.where(lit, qp, jnp.zeros_like(qp))
                de = jnp.where(lit, dop, jnp.zeros_like(dop))
                level = lse[2 * h + e, 0:1, rows]
                inner_sum = jnp.sum(turned[e * HEAD : (e + 1) * HEAD], axis=0, keepdims=True)
                total = jnp.zeros((HEAD, BQ), F32)
                for start in range(0, LEN, KEYS):
                    keys = slice(start, start + KEYS)
                    key_pos = (lax.broadcasted_iota(jnp.int32, (KEYS, 1), 0) + start).astype(F32)
                    logits = dot(k[keys, lanes], qe, 1, 1)
                    probs = jnp.where(key_pos < bound, jnp.exp2(logits * SCALE2 - level), 0.0)
                    slope = dot(v[keys, lanes], de, 1, 1)
                    dlog = (probs * (slope - inner_sum)).astype(BF16)
                    dv_acc[keys, :] += dot(probs.astype(BF16), de)
                    dk_acc[keys, :] += dot(dlog, qe)
                    total = total + dot(k_turn[e * HEAD : (e + 1) * HEAD, keys], dlog)
                dq_t.append(total)
            low[h, rows, 0:PAIR] = (jnp.concatenate(dq_t, axis=0).T * SCALE).astype(BF16)
            sums.slot(turn * p.nq + n)
            return inner

        lax.fori_loop(0, p.nq, query_step, 0)
        low[h, :, PAIR : 2 * PAIR] = (dk_acc[...] * SCALE).astype(BF16)
        low[h, :, 2 * PAIR :] = dv_acc[...].astype(BF16)
        bias_part(h)

        a_load(0).start()

        @pl.when(turn == 0)
        def _():
            weight_part(h, dw_out)
            to_twin_dw().start()

        return carry

    lax.fori_loop(0, p.pairs, pair_step, 0)

    half = p.D // CORES

    def block_of(n):
        lane = lax.rem(here.lane + 1 + n // (near * p.pieces), p.cpu)
        m = lax.rem(n, near * p.pieces)
        return ((m // p.pieces) * p.cpu + lane) * p.pieces + lax.rem(m, p.pieces)

    def da_half(rows, core):
        at = pl.ds(pl.multiple_of(core * half, half), half)
        total = dot(low[0, rows, :], wcol[0, at, :], 1, 1)
        for h in range(1, p.pairs):
            total = total + dot(low[h, rows, :], wcol[h, at, :], 1, 1)
        return total

    def da_mate(n, i):
        rows = block_rows(i)
        return remote(da_out.at[rows, :], da_in.at[rows, :], dm_s.at[n], dm_r.at[i], s, here.mate)

    far_blocks = (p.cpu - 1) * near * p.pieces
    count = p.pairs * p.nq

    def side_rows(i):
        return block_rows((i // p.pieces // p.cpu) * p.pieces + lax.rem(i, p.pieces))

    def da_over(n, i):
        return remote(da_own.at[block_rows(i), :], da_side.at[side_rows(i), :], dy_s.at[n], dy_r.at[i], here.beside, here.r)

    def da_first(n, carry):
        @pl.when(n < p.nq)
        def _():
            i = block_of(n)
            rows = block_rows(i)
            da_out[rows, :] = da_half(rows, 1 - c).astype(BF16)
            da_mate(n, i).start()
            da_own[rows, :] = da_half(rows, c).astype(BF16)

        @pl.when(n > 0)
        def _():
            last = jnp.maximum(n - 1, 0)
            i = block_of(last)
            rows = block_rows(i)
            da_mate(last, i).wait_recv()
            da_own[rows, :] = (da_own[rows, :].astype(F32) + da_in[rows, :].astype(F32)).astype(BF16)

            @pl.when(last < far_blocks)
            def _():
                da_over(last, i).start()

        sums.slot(count + n)
        return carry

    lax.fori_loop(0, p.nq + 1, da_first, 0)
    count = count + p.nq + 1

    own_pair = here.side
    weight_part(own_pair, dw_own, count)
    count = count + p.D // BQ
    to_twin_dw().wait_recv()
    dw_own[...] = (dw_own[...].astype(F32) + dw_in[...].astype(F32)).astype(BF16)
    span = 2 * width

    def dw_rows(zr):
        return pl.ds(pl.multiple_of(zr * span, span), span)

    def dw_send(n):
        zr = lax.rem(here.row + 1 + n, nz)
        return remote(
            dw_own.at[dw_rows(zr), :], dw_far.at[here.row], wz_s.at[n], wz_r.at[here.row], 2 * zr + here.col, here.r
        )

    for n in range(nz - 1):
        dw_send(n).start()

    def da_back(n, i):
        rows = block_rows(i)
        home = here.uq * p.P + i // p.pieces
        piece = lax.rem(i, p.pieces)
        dst = da_home.at[here.um, block_rows(piece), pl.ds(pl.multiple_of(c * half, half), half)]
        src = da_own.at[rows, :]
        recv = dh_r.at[here.um, c, piece]
        away = jnp.logical_or(home != s, here.uc != c)
        return away, lambda: remote(src, dst, dh_s.at[n], recv, home, here.chip + here.uc), (src, dst, recv)

    def da_second(n, carry):
        i = block_of(n)
        rows = block_rows(i)
        da_over(n, i).wait_recv()
        da_own[rows, :] = (da_own[rows, :].astype(F32) + da_side[side_rows(i), :].astype(F32)).astype(BF16)
        launch(*da_back(n, i))
        sums.slot(count + n - far_blocks)
        return carry

    lax.fori_loop(far_blocks, p.nq, da_second, 0)
    count = count + p.nq - far_blocks

    def rest_of_sums(n, carry):
        sums.slot(n)
        return carry

    lax.fori_loop(count, max(count, sums.slots()), rest_of_sums, 0)
    sums.finish()

    dw_far[here.row] = dw_own[dw_rows(here.row), :]
    for n in range(nz - 1):
        off = lax.rem(here.row + 1 + n, nz)
        remote(dw_far.at[off], dw_far.at[off], wz_s.at[n], wz_r.at[off], s, here.r).wait_recv()
    total = dw_far[0].astype(F32)
    for n in range(1, nz):
        total = total + dw_far[n].astype(F32)
    dw_end[...] = total.astype(BF16)
    slot = here.group * p.pairs + here.side
    twin_chip = here.twin - c

    def dw_give(n):
        fy, fx, fc = n // 4, n // 2 % 2, n % 2
        col = here.col if fy == 0 else 1 - here.col
        core = c if fc == 0 else 1 - c
        src = dw_end.at[pl.ds(pl.multiple_of(col * width, width), width), :]
        dst = gq.at[slot]
        to = (2 * here.row + col, (here.chip if fx == 0 else twin_chip) + core)
        return src, dst, to

    for n in range(1, 8):
        src, dst, to = dw_give(n)
        remote(src, dst, wd_s.at[n], wd_r.at[slot], *to).start()
    gq[slot] = dw_end[pl.ds(pl.multiple_of(here.col * width, width), width), :]

    def token_loads(m, piece):
        at = pl.ds(piece * BQ, BQ)
        return (
            pltpu.make_async_copy(x.at[m, at, :], x_buf, buf_sem.at[0]),
            pltpu.make_async_copy(stream.at[m, at, :], stream_buf, buf_sem.at[1]),
        )

    for copy in token_loads(0, 0):
        copy.start()
    gain = par[4:5, :].astype(F32)
    gain_sum = jnp.zeros((1, p.D), F32)
    shift_sum = jnp.zeros((1, p.D), F32)
    for m in range(p.M):
        for piece in range(p.pieces):
            at = slice(piece * BQ, (piece + 1) * BQ)
            for core in range(CORES):
                dst = da_home.at[m, pl.ds(piece * BQ, BQ), pl.ds(core * half, half)]
                pltpu.make_async_copy(dst, dst, dh_r.at[m, core, piece]).wait()
            for copy in token_loads(m, piece):
                copy.wait()
            values = x_buf[...].astype(F32)
            dy = da_home[m, at, :].astype(F32)
            centre = values - jnp.mean(values, axis=-1, keepdims=True)
            spread = jnp.mean(centre * centre, axis=-1, keepdims=True)
            scale = lax.rsqrt(spread + EPS)
            wn = centre * scale
            e = dy * gain
            dw = scale * (e - jnp.mean(e, axis=-1, keepdims=True) - wn * jnp.mean(e * wn, axis=-1, keepdims=True))
            input_grad[m, at, :] = (stream_buf[...] + dw).astype(BF16)
            if m * p.pieces + piece + 1 < p.M * p.pieces:
                follow = m * p.pieces + piece + 1
                for copy in token_loads(follow // p.pieces, follow % p.pieces):
                    copy.start()
            gain_sum = gain_sum + jnp.sum(dy * wn, axis=0, keepdims=True)
            shift_sum = shift_sum + jnp.sum(dy, axis=0, keepdims=True)
    for n in range(p.S):
        lanes = slice(n * width, (n + 1) * width)
        small_acc[n, 4:5, 0:width] = gain_sum[:, lanes]
        small_acc[n, 8:9, 0:width] = shift_sum[:, lanes]

    def tiny(n):
        to = lax.rem(s + n, p.S)
        return remote(small_acc.at[to], small_in.at[n], ss_s.at[n], ss_r.at[n], to, here.r)

    for n in range(1, p.S):
        tiny(n).start()
    sums.twin_to_mate()
    total = small_acc[s]
    for n in range(1, p.S):
        tiny(n).wait_recv()
        total = total + small_in[n]
    small_all[here.r] = total

    def every(n):
        to = lax.rem(here.r + n, p.R)
        return remote(small_all.at[here.r], small_all.at[here.r], sa_s.at[n], sa_r.at[here.r], s, to)

    for n in range(1, p.R):
        every(n).start()
    for n in range(1, p.R):
        off = lax.rem(here.r + n, p.R)
        remote(small_all.at[0], small_all.at[off], sa_s.at[n], sa_r.at[off], s, here.r).wait_recv()
    total = small_all[0]
    for n in range(1, p.R):
        total = total + small_all[n]
    small_out[...] = total

    for m in range(p.M):
        for g in range(p.groups):
            sent(*do_copy(m, g))

    def da_sent(n, carry):
        i = block_of(n)
        da_mate(n, i).wait_send()

        @pl.when(n < far_blocks)
        def _():
            da_over(n, i).wait_send()

        @pl.when(n >= far_blocks)
        def _():
            sent(*da_back(n, i))

        return carry

    lax.fori_loop(0, p.nq, da_sent, 0)
    to_twin_dw().wait_send()
    for n in range(nz - 1):
        dw_send(n).wait_send()
    for n in range(1, 8):
        src, dst, to = dw_give(n)
        remote(src, dst, wd_s.at[n], wd_r.at[slot], *to).wait_send()
    for n in range(p.groups * p.pairs):

        @pl.when(n != slot)
        def _():
            remote(gq.at[n], gq.at[n], wd_s.at[0], wd_r.at[n], s, here.r).wait_recv()

    for n in range(1, p.S):
        tiny(n).wait_send()
    for n in range(1, p.R):
        every(n).wait_send()
    sums.drain()


def back(plan, units, small, grads):
    p = plan
    nw = len(grads)
    nz = p.S // 2
    planes = p.R // CORES
    split = [split_rows(p, grad) for grad in grads]
    shapes = [h.shape[2:] for h in split]
    any_space = pl.BlockSpec(memory_space=pl.ANY)
    vmem = pl.BlockSpec(memory_space=pltpu.VMEM)
    dma = pltpu.SemaphoreType.DMA
    shape = jax.ShapeDtypeStruct
    half = p.D // CORES
    outs = pl.pallas_call(
        functools.partial(back_kernel, p, nw),
        out_shape=[
            shape((p.M, p.T, p.D), BF16),
            shape((p.groups * p.pairs, p.width, 3 * PAIR), BF16),
            shape(small.shape[1:], F32),
        ]
        + [shape((CORES,) + sh, BF16) for sh in shapes],
        in_specs=[vmem] * 6 + [any_space] * 2 + [vmem] + [any_space] * 2 + [vmem] * 2 + [any_space] * nw,
        out_specs=[vmem] * (3 + nw),
        scratch_shapes=[
            pltpu.VMEM((LEN, p.W), BF16),
            pltpu.VMEM((p.pairs, LEN, 3 * PAIR), BF16),
            pltpu.VMEM((LEN, PAIR), F32),
            pltpu.VMEM((LEN, PAIR), F32),
            pltpu.VMEM((PAIR, LEN), BF16),
            pltpu.VMEM((LEN, half), BF16),
            pltpu.VMEM((LEN, half), BF16),
            pltpu.VMEM((LEN, half), BF16),
            pltpu.VMEM((p.near * p.T, half), BF16),
            pltpu.VMEM((p.D, 3 * PAIR), BF16),
            pltpu.VMEM((p.D, 3 * PAIR), BF16),
            pltpu.VMEM((p.D, 3 * PAIR), BF16),
            pltpu.VMEM((nz, 2 * p.width, 3 * PAIR), BF16),
            pltpu.VMEM((2 * p.width, 3 * PAIR), BF16),
            pltpu.VMEM(small.shape, F32),
            pltpu.VMEM(small.shape, F32),
            pltpu.VMEM((p.R,) + small.shape[1:], F32),
            dma((p.M, p.groups)), dma((p.P,)),
            dma((p.nq,)), dma((p.nq,)), dma((p.nq,)), dma((p.nq,)),
            dma((p.nq,)), dma((p.M, CORES, p.pieces)),
            dma((1,)), dma((1,)), dma((nz,)), dma((nz,)), dma((planes,)), dma((planes,)), dma((8,)), dma((8,)),
            dma((p.S,)), dma((p.S,)), dma((p.R,)), dma((p.R,)),
        ]
        + GridSum.scratch(p, shapes)
        + [pltpu.VMEM((BQ, p.D), BF16), pltpu.VMEM((BQ, p.D), F32), dma((2,))]
        + [pltpu.VMEM((2, LEN, BQ), BF16), dma((2,))],
        compiler_params=pltpu.CompilerParams(
            collective_id=1, has_side_effects=True, vmem_limit_bytes=VMEM_LIMIT
        ),
        name="back",
    )(*units, small, *split)
    gq = outs[1].reshape(p.groups, p.pairs, p.width, 3, PAIR).transpose(2, 3, 0, 1, 4).reshape(p.width, 3 * p.D)
    return outs[0], gq.astype(F32), outs[2], [whole_shard(part) for part in outs[3:]]


def per_device(
    sizes,
    inputs,
    prefix,
    qkv_weight,
    qv_bias,
    out_weight,
    branch_bias,
    up_weight,
    up_bias,
    down_weight,
    norm_gain,
    norm_bias,
    cotangent,
):
    p = Plan(sizes, (inputs.shape[0], 1, inputs.shape[2], inputs.shape[3]))
    tokens_all = p.M * p.T
    x = inputs[:, 0]
    width = p.D // p.S
    spare = max(128 - width, 0)
    par = jnp.concatenate([qv_bias, branch_bias, norm_gain, norm_bias, up_bias.reshape(-1, width)], axis=0)
    par = jnp.pad(par, ((0, 0), (0, spare)))
    by_group = qkv_weight.reshape(-1, 3, p.groups, p.pairs, PAIR).transpose(2, 3, 0, 1, 4)
    by_group = by_group.reshape(p.groups, p.pairs, -1, 3 * PAIR)
    pre = jnp.broadcast_to(prefix[:, 0].reshape(-1, 1).astype(F32), (p.M * p.Q, 128))
    pre = jnp.pad(pre, ((0, 8 - p.M * p.Q), (0, 0)))
    (wo, wu, wd, parf, _, q, k, v, o, lse, preu, o_home, a_unit, w_unit) = fore(
        p, x, par, pre, by_group, (out_weight, up_weight, down_weight)
    )
    par32 = parf.astype(F32)
    bias_branch = par32[2:4]
    gains, shifts = par32[4:8], par32[8:12]
    bias_up = par32[12:].reshape(-1, p.S, width).transpose(1, 0, 2).reshape(-1)

    tokens = x.reshape(tokens_all, p.D).astype(F32)
    upstream = cotangent[:, 0].reshape(tokens_all, p.D).astype(F32)
    mixed_low = o_home.reshape(tokens_all, p.D)
    branch = dot(mixed_low, wo) + bias_branch[0]
    side, pull_side = jax.vjp(normed, branch, gains[1:2], shifts[1:2])
    stream = tokens + side
    normal_mid, pull_mid = jax.vjp(normed, stream, gains[2:3], shifts[2:3])
    middle_low = normal_mid.astype(BF16)
    upper = dot(middle_low, wu) + bias_up
    below = 0.5 * (1.0 + lax.erf(upper * math.sqrt(0.5)))
    slope = below + upper * jnp.exp(-0.5 * upper * upper) * (1.0 / math.sqrt(2.0 * math.pi))
    active_low, slope = lax.optimization_barrier(((upper * below).astype(BF16), slope))
    lower = dot(active_low, wd) + bias_branch[1]
    closing, pull_close = jax.vjp(normed, lower, gains[3:4], shifts[3:4])
    output = (stream + closing).astype(BF16)
    grad_lower, gain_three, shift_three = pull_close(upstream)
    lower_low = grad_lower.astype(BF16)
    grad_active = dot(lower_low, wd, 1, 1)
    upper_low = (grad_active * slope).astype(BF16)
    grad_middle = dot(upper_low, wu, 1, 1)
    grad_mid_in, gain_two, shift_two = pull_mid(grad_middle)
    grad_stream = grad_mid_in + upstream
    grad_branch, gain_one, shift_one = pull_side(grad_stream)
    branch_low = grad_branch.astype(BF16)
    grad_mixed = dot(branch_low, wo, 1, 1).astype(BF16)

    grads = (
        dot(active_low, lower_low, 0, 0).astype(BF16),
        dot(middle_low, upper_low, 0, 0).astype(BF16),
        dot(mixed_low, branch_low, 0, 0).astype(BF16),
    )
    def column_sum(values):
        return jnp.sum(values.astype(F32), axis=0, keepdims=True)

    du_sum = column_sum(upper_low).reshape(p.S, -1, width).transpose(1, 0, 2).reshape(-1, p.D)
    none = jnp.zeros((1, p.D), F32)
    small = jnp.concatenate(
        [
            none, none, column_sum(branch_low), column_sum(lower_low),
            none, gain_one, gain_two, gain_three,
            none, shift_one, shift_two, shift_three,
            du_sum,
        ], axis=0,
    )
    small = jnp.pad(small.reshape(-1, p.S, width).transpose(1, 0, 2), ((0, 0), (0, 0), (0, spare)))
    by_token = (p.M, p.T, p.D)
    input_grad, sum_qkv, tiny, (sum_down, sum_up, sum_out) = back(
        p,
        (
            q, k, v, o, lse, preu, grad_mixed.reshape(by_token), a_unit, w_unit,
            x, grad_stream.reshape(by_token), parf,
        ),
        small, grads,
    )
    tiny = tiny[:, :width]
    shaped = (p.M, 1, p.T, p.D)
    return (
        output.reshape(shaped),
        input_grad.reshape(shaped),
        sum_qkv,
        tiny[0:2],
        sum_out,
        tiny[2:4],
        sum_up,
        tiny[12:].reshape(-1),
        sum_down,
        tiny[4:8],
        tiny[8:12],
    )


def solution(mesh):
    sizes = {name: mesh.shape[name] for name in ("shard", "replica")}
    placed = (
        P(None, "replica", "shard", None),
        P(None, "replica", None),
        P("shard", None),
        P(None, "shard"),
        P("shard", None),
        P(None, "shard"),
        P("shard", None),
        P("shard"),
        P("shard", None),
        P(None, "shard"),
        P(None, "shard"),
        P(None, "replica", "shard", None),
    )
    return jax.shard_map(
        functools.partial(per_device, sizes),
        mesh=mesh,
        in_specs=placed,
        out_specs=(
            P(None, "replica", "shard", None),
            P(None, "replica", "shard", None),
            P("shard", None),
            P(None, "shard"),
            P("shard", None),
            P(None, "shard"),
            P("shard", None),
            P("shard"),
            P("shard", None),
            P(None, "shard"),
            P(None, "shard"),
        ),
        check_vma=False,
    )
```

```python
import functools
import math

import jax
import jax.numpy as jnp
from jax import lax
from jax.experimental import pallas as pl
from jax.experimental.pallas import tpu as pltpu
from jax.sharding import PartitionSpec as P

HEAD = 64
LEN = 2048
CORES = 2
PAIR = 2 * HEAD
BQ = 256
EPS = 1e-05
MASKED = -1e30
SCALE = HEAD ** (-0.5)
SCALE2 = SCALE * math.log2(math.e)
F32 = jnp.float32
BF16 = jnp.bfloat16
MESH = pl.DeviceIdType.MESH
VMEM_LIMIT = 66_000_000
LAG = 2
KEYS = 512
SIDE_FIRST = (True, False, False)
SUM_LAG = 5
CADENCE = 1
COLUMN_FIRST = (False, True, False)
START = 1
EARLY = 1


class Plan:
    def __init__(self, mesh_shape, inputs_shape):
        self.S = mesh_shape["shard"]
        self.R = mesh_shape["replica"]
        self.M, _, self.T, self.D = inputs_shape
        self.Q = self.T * self.S // LEN
        self.P = LEN // self.T
        self.U = self.M * self.Q * CORES
        self.cpu = self.S // self.U
        self.heads = self.D // HEAD
        self.W = self.D // (CORES * self.cpu)
        self.pairs = self.W // PAIR
        self.groups = CORES * self.cpu
        self.pieces = self.T // BQ
        self.nq = LEN // BQ
        self.near = self.P // self.cpu
        self.width = self.D // self.S
        assert self.cpu == 2 and self.pairs == 2 and self.T % BQ == 0 and LEN % self.T == 0


class Place:
    def __init__(self, plan):
        self.p = plan
        self.s = lax.axis_index("shard")
        self.r = lax.axis_index("replica")
        self.c = lax.rem(self.r, CORES)
        self.chip = self.r - self.c
        self.mate = self.chip + (1 - self.c)
        self.unit = self.s // plan.cpu
        self.lane = lax.rem(self.s, plan.cpu)
        self.group = self.c * plan.cpu + self.lane
        self.uc = lax.rem(self.unit, CORES)
        self.um = lax.rem(self.unit // CORES, plan.M)
        self.uq = self.unit // (CORES * plan.M)
        self.ring = self.to_ring(self.s)
        self.plane = self.r // CORES
        self.side = lax.rem(self.plane, 2)
        self.twin = self.r + CORES * (1 - 2 * self.side)
        self.row = self.s // 2
        self.col = lax.rem(self.s, 2)
        self.beside = 2 * self.row + 1 - self.col
        self.rows = plan.S // 2

    def unit_of(self, c, m, s):
        return ((s // self.p.P) * self.p.M + m) * CORES + c

    def to_ring(self, s):
        half = self.p.S // 2
        row, col = s // 2, lax.rem(s, 2)
        return row + col * (2 * half - 1 - 2 * row)

    def from_ring(self, i):
        n = self.p.S
        return jnp.where(i < n // 2, 2 * i, 2 * (n - 1 - i) + 1)


def remote(src, dst, send, recv, s, r):
    return pltpu.make_async_remote_copy(
        src_ref=src, dst_ref=dst, send_sem=send, recv_sem=recv, device_id=(s, r), device_id_type=MESH
    )


def launch(away, far, near):
    @pl.when(away)
    def _():
        far().start()

    @pl.when(jnp.logical_not(away))
    def _():
        pltpu.make_async_copy(*near).start()


def sent(away, far, near):
    @pl.when(away)
    def _():
        far().wait_send()


def greet(peers):
    barrier = pltpu.get_barrier_semaphore()
    for s, r in peers:
        pl.semaphore_signal(barrier, inc=1, device_id=(s, r), device_id_type=MESH)
    pl.semaphore_wait(barrier, len(peers))


def plane_peers(here):
    n = here.p.S * CORES
    own = here.s * CORES + here.c
    out = []
    for k in range(1, n):
        i = lax.rem(own + k, n)
        out.append((i // CORES, here.chip + lax.rem(i, CORES)))
    return out


def normed(values, gain, shift):
    centre = values - jnp.mean(values, axis=-1, keepdims=True)
    spread = jnp.mean(centre * centre, axis=-1, keepdims=True)
    return centre * lax.rsqrt(spread + EPS) * gain + shift


def dot(a, b, ca=1, cb=0):
    return lax.dot_general(a, b, (((ca,), (cb,)), ((), ())), preferred_element_type=F32)


def head_lanes(rows, which):
    lane = lax.broadcasted_iota(jnp.int32, (rows, PAIR), 1)
    return (lane < HEAD) if which == 0 else (lane >= HEAD)


def fore_kernel(
    plan, x, biases, branches, gains, shifts, ups, prefixes, wq_in, wo, wu, wd,
    wof, wuf, wdf, parf, ah, q_out, k_out, v_out, o_out, lse_out, preu, oh, a_all, wcol,
    par, pre, wq, parg, pre2,
    par_ss, par_rs, pre_sem, loc_sem, a_ss, a_rs, af_ss, z_ss, z_rs, wa_ss, wa_rs, wb_ss, wb_rs, wm_ss, wm_rs,
    o_ss, o_rs, q_ss, q_rs, qt_ss, qt_rs, q_loc,
):
    p = plan
    here = Place(p)
    s, c = here.s, here.c
    mine, full = (wo, wu, wd), (wof, wuf, wdf)
    nw = len(mine)
    first = COLUMN_FIRST
    greet(plane_peers(here) + [(s, here.twin)])

    par[...] = jnp.zeros_like(par)
    at = 0
    for part in (biases, branches, gains, shifts, ups):
        par[at : at + part.shape[0], 0 : part.shape[1]] = part[...]
        at += part.shape[0]
    pre[...] = jnp.zeros_like(pre)
    for m in range(p.M):
        for n in range(p.Q):
            pre[m * p.Q + n : m * p.Q + n + 1, :] = jnp.full((1, 128), prefixes[m, n].astype(F32))
    for g in range(p.groups):
        for h in range(p.pairs):
            for k in range(3):
                at = k * p.D + g * p.W + h * PAIR
                wq[g, h, :, k * PAIR : (k + 1) * PAIR] = wq_in[:, at : at + PAIR]
    parg[s] = par[...]
    small = []
    for k in range(1, p.S):
        to = lax.rem(s + k, p.S)
        small.append(remote(par, parg.at[s], par_ss.at[k], par_rs.at[k], to, here.r))
        small[-1].start()
    swap = remote(pre, pre2, pre_sem.at[0], pre_sem.at[1], s, here.mate)
    swap.start()

    z, nz = here.row, here.rows

    def where(w, zr, fa, fb, core):
        fy, fx = (fa, fb) if first[w] else (fb, fa)
        col = here.col if fy == 0 else 1 - here.col
        side = here.side if fx == 0 else 1 - here.side
        n, width = mine[w].shape[0], mine[w].shape[1] // 2
        rows = pl.ds(pl.multiple_of((2 * zr + col) * n + core * (n // 2), n // 2), n // 2)
        return full[w].at[rows, pl.ds(pl.multiple_of(side * width, width), width)]

    def origin(w, fa):
        n, width = mine[w].shape[0], mine[w].shape[1] // 2
        side = here.side if fa == 0 else 1 - here.side
        rows = pl.ds(pl.multiple_of(c * (n // 2), n // 2), n // 2)
        return mine[w].at[rows, pl.ds(pl.multiple_of(side * width, width), width)]

    def peer(w, second):
        return (here.beside, here.r) if first[w] == (second == 0) else (s, here.twin)

    def z_send(w, d, k):
        sign = 1 - 2 * d
        part = where(w, z - sign * (k - 1), 0, 0, c)
        src = origin(w, 0) if isinstance(k, int) and k == 1 else part
        return remote(src, part, z_ss.at[w, d, k - 1], z_rs.at[w, d, k - 1], s + 2 * sign, here.r)

    def z_came(w, d, k):
        sign = 1 - 2 * d
        part = where(w, z - sign * k, 0, 0, c)
        return remote(part, part, z_ss.at[w, d, k - 1], z_rs.at[w, d, k - 1], s, here.r)

    def to_first(w, zr, src=None):
        part = where(w, zr, 0, 0, c)
        return remote(part if src is None else src, part, wa_ss.at[w, zr], wa_rs.at[w, zr], *peer(w, 0))

    def to_second(w, fa, zr, src=None):
        part = where(w, zr, fa, 0, c)
        return remote(part if src is None else src, part, wb_ss.at[w, fa, zr], wb_rs.at[w, fa, zr], *peer(w, 1))

    def to_mate(w, fa, fb, zr, core):
        part = where(w, zr, fa, fb, core)
        at = 2 * fa + fb
        return remote(part, part, wm_ss.at[w, at, zr], wm_rs.at[w, at, zr], s, here.mate)

    def first_came(w, zr):
        part = where(w, zr, 1, 0, c)
        return remote(part, part, wa_ss.at[w, zr], wa_rs.at[w, zr], s, here.r)

    def second_came(w, fa, zr):
        part = where(w, zr, fa, 1, c)
        return remote(part, part, wb_ss.at[w, fa, zr], wb_rs.at[w, fa, zr], s, here.r)

    def on_grid(d, k):
        return z >= k if d == 0 else z + k < nz

    def can_send(d):
        return z < nz - 1 if d == 0 else z > 0

    def gather_rows(w):
        for d in (0, 1):

            @pl.when(can_send(d))
            def _():
                z_send(w, d, 1).start()

    def gather_near(w):
        if first[w]:
            to_first(w, z, origin(w, 0)).start()
        else:
            to_second(w, 0, z, origin(w, 0)).start()
            to_second(w, 1, z, origin(w, 1)).start()

    def gather_slot(w, k, lag):
        for d in (0, 1):
            sign = 1 - 2 * d

            @pl.when(jnp.logical_and(k >= 1, on_grid(d, k)))
            def _():
                at = jnp.maximum(k, 1)
                z_came(w, d, at).wait_recv()
                zr = z - sign * at

                @pl.when(can_send(d))
                def _():
                    z_send(w, d, at + 1).start()

                to_first(w, zr).start()
                to_second(w, 0, zr).start()
                to_mate(w, 0, 0, zr, c).start()

        def at_distance(j, least, body):
            for d in (0, 1):
                ok = jnp.logical_and(j >= max(least, d), on_grid(d, j))

                @pl.when(ok)
                def _():
                    body(z - (1 - 2 * d) * jnp.maximum(j, 0))

        def after_first(zr):
            first_came(w, zr).wait_recv()
            to_second(w, 1, zr).start()
            to_mate(w, 1, 0, zr, c).start()

        at_distance(k - 1, 0 if first[w] else 1, after_first)

        def after_second(fa):
            def body(zr):
                second_came(w, fa, zr).wait_recv()
                to_mate(w, fa, 1, zr, c).start()

            return body

        at_distance(k - 1 - lag, 1 if first[w] else 0, after_second(0))
        at_distance(k - 2 - lag, 0, after_second(1))

    def mate_pieces(w, zr, act):
        other = zr != z

        @pl.when(other)
        def _():
            act(0, 0)

        if first[w]:

            @pl.when(other)
            def _():
                act(0, 1)

            act(1, 0)
        else:

            @pl.when(other)
            def _():
                act(1, 0)

            act(0, 1)
        act(1, 1)

    def gather_wait(w):
        def one(zr, carry):
            mate_pieces(w, zr, lambda fa, fb: to_mate(w, fa, fb, zr, 1 - c).wait_recv())
            return carry

        lax.fori_loop(0, nz, one, 0)

    def gather_drain(w):
        def one(zr, carry):
            mate_pieces(w, zr, lambda fa, fb: to_mate(w, fa, fb, zr, c).wait_send())
            if first[w]:
                to_first(w, zr).wait_send()

                @pl.when(zr != z)
                def _():
                    to_second(w, 0, zr).wait_send()
            else:

                @pl.when(zr != z)
                def _():
                    to_first(w, zr).wait_send()

                to_second(w, 0, zr).wait_send()
            to_second(w, 1, zr).wait_send()
            for d in (0, 1):
                reach = zr <= z if d == 0 else zr < nz - z

                @pl.when(jnp.logical_and(can_send(d), reach))
                def _():
                    z_send(w, d, zr + 1).wait_send()

            return carry

        lax.fori_loop(0, nz, one, 0)

    nq_rows = wq.shape[2]
    half_rows = nq_rows // 2

    def q_rows(k, side):
        return pl.ds(pl.multiple_of(k * nq_rows + side * half_rows, half_rows), half_rows)

    def q_send(k):
        to = lax.rem(s + k, p.S)
        group = c * p.cpu + lax.rem(to, p.cpu)
        rows = pl.ds(pl.multiple_of(here.side * half_rows, half_rows), half_rows)
        src = wq.at[group, :, rows, :]
        return remote(src, wcol.at[:, q_rows(s, here.side), :], q_ss.at[k], q_rs.at[s], to, here.r)

    def q_twin(k, side):
        part = wcol.at[:, q_rows(k, side), :]
        return remote(part, part, qt_ss.at[k], qt_rs.at[k], s, here.twin)

    def q_from(k):
        return lax.rem(s + p.S - k, p.S)

    for k in range(1, p.S):
        q_send(k).start()
    for w in range(nw):
        gather_near(w)
    q_own = pltpu.make_async_copy(
        wq.at[here.group], wcol.at[:, pl.ds(pl.multiple_of(s * nq_rows, nq_rows), nq_rows), :], q_loc.at[0]
    )
    q_own.start()
    local = []
    for w in range(nw):
        n = mine[w].shape[0]
        local.append(
            pltpu.make_async_copy(mine[w], full[w].at[pl.ds(pl.multiple_of(s * n, n), n), :], loc_sem.at[w])
        )
        local[-1].start()

    for k in range(1, p.S):
        small[k - 1].wait_recv()
    parf[...] = jnp.concatenate([parg[k][:, : p.D // p.S] for k in range(p.S)], axis=1)
    gain = parf[4:5, :].astype(F32)
    shift = parf[8:9, :].astype(F32)
    rows_here = pl.ds(pl.multiple_of(lax.rem(s, p.P) * p.T, p.T), p.T)

    def first_hop(m):
        to = here.unit_of(c, m, s) * p.cpu + here.lane
        far = lambda: remote(ah.at[m], a_all.at[rows_here, :], a_ss.at[m], a_rs.at[lax.rem(s, p.P)], to, here.r)
        return to, far

    for m in range(p.M):
        ah[m] = normed(x[m].astype(F32), gain, shift).astype(BF16)
        to, far = first_hop(m)

        @pl.when(to != s)
        def _():
            far().start()

        @pl.when(to == s)
        def _():
            a_all[rows_here, :] = ah[m]

    primary = c == here.uc

    def a_rows(j):
        return pl.ds(pl.multiple_of(j * p.T, p.T), p.T)

    def a_forward(j, k):
        part = a_all.at[a_rows(j), :]
        if k == 0:
            return remote(part, part, af_ss.at[j, 0], a_rs.at[j], s, here.mate)
        to = here.unit * p.cpu + lax.rem(here.lane + k, p.cpu)
        return remote(part, part, af_ss.at[j, k], a_rs.at[j], to, here.r)

    def a_wait(j):
        part = a_all.at[a_rows(j), :]
        remote(part, part, af_ss.at[j, 0], a_rs.at[j], s, here.mate).wait_recv()

    near = p.near

    zi = here.unit - here.uq * near

    def a_at(k, body):
        for d in (0, 1):
            if k or not d:
                ok = zi >= k if d == 0 else zi + k < near

                @pl.when(jnp.logical_and(primary, ok))
                def _():
                    body(zi - (1 - 2 * d) * k)

    def a_near(jj):
        j = jj * p.cpu + here.lane

        @pl.when(here.uq * p.P + j != s)
        def _():
            a_wait(j)

        for k in list(range(1, p.cpu)) + [0]:
            a_forward(j, k).start()

    def a_far(jj):
        for k in range(1, p.cpu):
            j = jj * p.cpu + lax.rem(here.lane + k, p.cpu)
            a_wait(j)
            a_forward(j, 0).start()

    each = -(-(p.S - 1) // near)
    for k in range(near + 1):
        if k < near:
            for n in range(1 + k * each, min(1 + (k + 1) * each, p.S)):
                part = wcol.at[:, q_rows(q_from(n), here.side), :]
                remote(part, part, q_ss.at[n], q_rs.at[q_from(n)], s, here.r).wait_recv()
                q_twin(q_from(n), here.side).start()
            a_at(k, a_near)
        if k == START:
            for w in range(nw):
                gather_rows(w)
        if k >= 1:
            a_at(k - 1, a_far)
        if k >= near + 1 - EARLY:
            for w in range(nw):
                gather_slot(w, k - (near - EARLY), LAG)

    @pl.when(jnp.logical_not(primary))
    def _():
        for j in range(p.P):
            a_wait(j)

    swap.wait_recv()
    pre2[...] = jnp.where(primary, pre[...], pre2[...])
    row = here.um * p.Q + here.uq
    preu[...] = jnp.broadcast_to(pre2[pl.ds(row, 1), :], preu.shape)

    for n in range(1, p.S):
        q_twin(q_from(n), 1 - here.side).wait_recv()
    q_own.wait()
    own = pl.ds(pl.multiple_of(here.group * p.W, PAIR), p.W)
    q_bias = parf[0:1, own].astype(F32)
    v_bias = parf[1:2, own].astype(F32)

    def project(i, carry):
        rows = pl.ds(pl.multiple_of(i * BQ, BQ), BQ)
        part = a_all[rows, :]
        for h in range(p.pairs):
            lanes = slice(h * PAIR, (h + 1) * PAIR)
            got = dot(part, wcol[h])
            q_out[rows, lanes] = (got[:, :PAIR] + q_bias[:, lanes]).astype(BF16)
            k_out[rows, lanes] = got[:, PAIR : 2 * PAIR].astype(BF16)
            v_out[rows, lanes] = (got[:, 2 * PAIR :] + v_bias[:, lanes]).astype(BF16)
        return carry

    lax.fori_loop(0, p.nq, project, 0)

    prefix = preu[0:1, 0:1]
    slots = nz + 1 + LAG - EARLY
    per = -(-slots // p.nq)

    def o_copy(i):
        rows = pl.ds(pl.multiple_of(i * BQ, BQ), BQ)
        home = here.uq * p.P + i // p.pieces
        piece = lax.rem(i, p.pieces)
        there = pl.ds(pl.multiple_of(piece * BQ, BQ), BQ)
        src = o_out.at[rows, :]
        dst = oh.at[here.um, there, own]
        away = jnp.logical_or(home != s, here.uc != c)
        recv = o_rs.at[here.um, here.group, piece]
        return away, lambda: remote(src, dst, o_ss.at[i], recv, home, here.chip + here.uc), (src, dst, recv)

    def attend(i, carry):
        rows = pl.ds(pl.multiple_of(i * BQ, BQ), BQ)
        row_pos = (lax.broadcasted_iota(jnp.int32, (BQ, 1), 0) + i * BQ + 1).astype(F32)
        bound = jnp.maximum(row_pos, prefix)
        key_pos = lax.broadcasted_iota(jnp.int32, (1, LEN), 1).astype(F32)
        seen = key_pos < bound

        def pair_step(h, inner):
            lanes = pl.ds(pl.multiple_of(h * PAIR, PAIR), PAIR)
            qp, kp, vp = q_out[rows, lanes], k_out[:, lanes], v_out[:, lanes]
            halves = []
            for e in (0, 1):
                logits = dot(jnp.where(head_lanes(BQ, e), qp, jnp.zeros_like(qp)), kp, 1, 1)
                logits = jnp.where(seen, logits, MASKED)
                top = jnp.max(logits, axis=1, keepdims=True)
                powers = jnp.exp2((logits - top) * SCALE2)
                total = jnp.sum(powers, axis=1, keepdims=True)
                halves.append(dot(powers.astype(BF16), vp) * (1.0 / total))
                level = top * SCALE2 + jnp.log2(total)
                turned = jnp.broadcast_to(level, (BQ, 128)).T
                lse_out[2 * h + e, :, pl.ds(pl.multiple_of(i * BQ, BQ), BQ)] = turned[0:8]
            o_out[rows, lanes] = jnp.where(head_lanes(BQ, 0), halves[0], halves[1]).astype(BF16)
            return inner

        lax.fori_loop(0, p.pairs, pair_step, 0)
        launch(*o_copy(i))

        for extra in range(per):
            for w in range(nw):
                gather_slot(w, i * per + extra + 1 + EARLY, LAG)

        return carry

    lax.fori_loop(0, p.nq, attend, 0)

    for m in range(p.M):
        for g in range(p.groups):
            for piece in range(p.pieces):
                src = o_out.at[pl.ds(0, BQ), :]
                dst = oh.at[m, pl.ds(piece * BQ, BQ), pl.ds(g * p.W, p.W)]
                pltpu.make_async_copy(src, dst, o_rs.at[m, g, piece]).wait()

    def o_sent(i, carry):
        sent(*o_copy(i))
        return carry

    lax.fori_loop(0, p.nq, o_sent, 0)
    for copy in small:
        copy.wait_send()
    swap.wait_send()
    for copy in local:
        copy.wait()
    for n in range(1, p.S):
        q_send(n).wait_send()
        q_twin(q_from(n), here.side).wait_send()
    for m in range(p.M):
        to, far = first_hop(m)

        @pl.when(to != s)
        def _():
            far().wait_send()

    @pl.when(primary)
    def _():
        for jj in range(near):
            for k in range(p.cpu):
                a_forward(jj * p.cpu + here.lane, k).wait_send()
            for k in range(1, p.cpu):
                a_forward(jj * p.cpu + lax.rem(here.lane + k, p.cpu), 0).wait_send()

    for w in range(nw):
        gather_wait(w)
        gather_drain(w)


def fore(plan, x, small, prefixes, qkv, weights):
    p = plan
    par = (sum(part.shape[0] for part in small), max(p.width, 128))
    nz = p.S // 2
    nw = len(weights)
    any_space = pl.BlockSpec(memory_space=pl.ANY)
    vmem = pl.BlockSpec(memory_space=pltpu.VMEM)
    shape = jax.ShapeDtypeStruct
    out_shape = (
        [shape((w.shape[0] * p.S, w.shape[1]), BF16) for w in weights]
        + [shape((par[0], p.D), BF16), shape((p.M, p.T, p.D), BF16)]
        + [shape((LEN, p.W), BF16)] * 4
        + [shape((2 * p.pairs, 8, LEN), F32), shape((8, 128), F32), shape((p.M, p.T, p.D), BF16)]
        + [shape((LEN, p.D), BF16), shape((p.pairs, p.D, 3 * PAIR), BF16)]
    )
    dma = pltpu.SemaphoreType.DMA
    return pl.pallas_call(
        functools.partial(fore_kernel, p),
        out_shape=out_shape,
        in_specs=[vmem] * 6 + [pl.BlockSpec(memory_space=pltpu.SMEM)] + [vmem] * (1 + nw),
        out_specs=[any_space] * nw + [vmem] * 11,
        scratch_shapes=[
            pltpu.VMEM(par, BF16),
            pltpu.VMEM((8, 128), F32),
            pltpu.VMEM((p.groups, p.pairs, qkv.shape[0], 3 * PAIR), BF16),
            pltpu.VMEM((p.S,) + par, BF16),
            pltpu.VMEM((8, 128), F32),
            dma((p.S,)), dma((p.S,)), dma((2,)), dma((nw,)),
            dma((p.M,)), dma((p.P,)), dma((p.P, p.cpu)),
            dma((nw, 2, nz)), dma((nw, 2, nz)), dma((nw, nz)), dma((nw, nz)),
            dma((nw, 2, nz)), dma((nw, 2, nz)), dma((nw, 4, nz)), dma((nw, 4, nz)),
            dma((p.nq,)), dma((p.M, p.groups, p.pieces)),
            dma((p.S,)), dma((p.S,)), dma((p.S,)), dma((p.S,)), dma((1,)),
        ],
        compiler_params=pltpu.CompilerParams(
            collective_id=0, has_side_effects=True, vmem_limit_bytes=VMEM_LIMIT
        ),
        name="fore",
    )(x, *small, prefixes, qkv, *weights)


class GridSum:
    def __init__(self, here, grads, outs, refs):
        self.here, self.grads, self.outs = here, grads, outs
        self.nw = nw = len(grads)
        self.nz = here.rows
        self.planes = here.p.R // CORES
        self.own, self.acc, self.one, self.two, self.far = (refs[k * nw : (k + 1) * nw] for k in range(5))
        (self.ld, self.m_s, self.m_r, self.a_s, self.a_r, self.b_s, self.b_r, self.z_s, self.z_r) = refs[5 * nw : 5 * nw + 9]
        (self.x_s, self.x_r, self.t_s, self.t_r, self.f_s, self.f_r) = refs[5 * nw + 9 :]
        self.side_first = SIDE_FIRST

    @staticmethod
    def scratch(plan, shapes):
        nw = len(shapes)
        planes = plan.R // CORES
        nz = plan.S // 2
        dma = pltpu.SemaphoreType.DMA
        return (
            [pltpu.VMEM((2,) + sh, BF16) for sh in shapes]
            + [pltpu.VMEM((plan.S,) + sh, BF16) for sh in shapes]
            + [
                pltpu.VMEM((plan.S, sh[0], sh[1] // 2) if sf else (nz,) + sh, BF16)
                for sh, sf in zip(shapes, SIDE_FIRST)
            ]
            + [pltpu.VMEM((nz, sh[0], sh[1] // 2), BF16) for sh in shapes]
            + [pltpu.VMEM((max(nz, planes // 2), sh[0], sh[1] // 2), BF16) for sh in shapes]
            + [dma((nw,))]
            + [dma((nw, nz))] * 8
            + [dma((nw, planes))] * 2
            + [dma((nw,))] * 2
            + [dma((nw, 2))] * 2
        )

    @staticmethod
    def count(nw):
        return 5 * nw + 15

    def zr(self, k):
        return lax.rem(self.here.row + 1 + k, self.nz)

    def half(self, w, side):
        n = self.acc[w].shape[2] // 2
        return pl.ds(pl.multiple_of(side * n, n), n)

    def load(self, w, k):
        src = self.grads[w].at[pl.ds(2 * self.zr(k), 2), self.here.c]
        return pltpu.make_async_copy(src, self.own[w], self.ld.at[w])

    def swap(self, w, k):
        here = self.here
        pair = pl.ds(2 * self.zr(k), 2)
        return remote(
            self.grads[w].at[pair, 1 - here.c], self.acc[w].at[pair], self.m_s.at[w, k], self.m_r.at[w, k], here.s, here.mate
        )

    def first(self, w, k):
        here, zr = self.here, self.zr(k)
        if self.side_first[w]:
            pair = pl.ds(2 * zr, 2)
            src = self.acc[w].at[pair, :, self.half(w, 1 - here.side)]
            return remote(src, self.one[w].at[pair], self.a_s.at[w, k], self.a_r.at[w, k], here.s, here.twin)
        src = self.acc[w].at[2 * zr + 1 - here.col]
        return remote(src, self.one[w].at[zr], self.a_s.at[w, k], self.a_r.at[w, k], here.beside, here.r)

    def second(self, w, k):
        here, zr = self.here, self.zr(k)
        if self.side_first[w]:
            src = self.acc[w].at[2 * zr + 1 - here.col, :, self.half(w, here.side)]
            to = (here.beside, here.r)
        else:
            src = self.acc[w].at[2 * zr + here.col, :, self.half(w, 1 - here.side)]
            to = (here.s, here.twin)
        return remote(src, self.two[w].at[zr], self.b_s.at[w, k], self.b_r.at[w, k], *to)

    def final(self, w, k):
        here, zr = self.here, self.zr(k)
        src = self.acc[w].at[2 * zr + here.col, :, self.half(w, here.side)]
        return remote(
            src, self.far[w].at[here.row], self.z_s.at[w, k], self.z_r.at[w, here.row], 2 * zr + here.col, here.r
        )

    def begin(self):
        for k in range(self.nz):
            for w in range(self.nw):
                self.swap(w, k).start()
                if k == 0:
                    self.load(w, 0).start()

    def strips(self, w, body):
        def one(r, carry):
            body(pl.ds(pl.multiple_of(r * 16, 16), 16))
            return carry

        lax.fori_loop(0, self.acc[w].shape[1] // 16, one, 0)

    def event_one(self, w, k):
        zr = self.zr(k)
        pair = pl.ds(2 * zr, 2)
        self.load(w, k).wait()
        self.swap(w, k).wait_recv()
        acc, own = self.acc[w], self.own[w]

        def strip(at):
            acc[pair, at, :] = (acc[pair, at, :].astype(F32) + own[:, at, :].astype(F32)).astype(BF16)

        self.strips(w, strip)
        self.first(w, k).start()

        @pl.when(k < self.nz - 1)
        def _():
            self.load(w, jnp.minimum(k + 1, self.nz - 1)).start()

    def event_two(self, w, k):
        here, zr = self.here, self.zr(k)
        self.first(w, k).wait_recv()
        acc, one = self.acc[w], self.one[w]
        if self.side_first[w]:
            pair = pl.ds(2 * zr, 2)
            lanes = self.half(w, here.side)

            def strip(at):
                acc[pair, at, lanes] = (acc[pair, at, lanes].astype(F32) + one[pair, at, :].astype(F32)).astype(BF16)

        else:
            shard = 2 * zr + here.col

            def strip(at):
                acc[shard, at, :] = (acc[shard, at, :].astype(F32) + one[zr, at, :].astype(F32)).astype(BF16)

        self.strips(w, strip)
        self.second(w, k).start()

    def event_three(self, w, k):
        here, zr = self.here, self.zr(k)
        self.second(w, k).wait_recv()
        shard, lanes = 2 * zr + here.col, self.half(w, here.side)
        acc, two = self.acc[w], self.two[w]

        def strip(at):
            acc[shard, at, lanes] = (acc[shard, at, lanes].astype(F32) + two[zr, at, :].astype(F32)).astype(BF16)

        self.strips(w, strip)

        @pl.when(k < self.nz - 1)
        def _():
            self.final(w, k).start()

    def slots(self):
        return CADENCE * (self.nw * self.nz + 2 * SUM_LAG)

    def slot(self, n):
        @pl.when(lax.rem(n, CADENCE) == 0)
        def _():
            self.event(n // CADENCE)

    def event(self, n):
        for stage, body in ((2, self.event_three), (1, self.event_two), (0, self.event_one)):
            e = n - stage * SUM_LAG
            for w in range(self.nw):
                ok = jnp.logical_and(e >= 0, e < self.nw * self.nz)

                @pl.when(jnp.logical_and(ok, lax.rem(e, self.nw) == w))
                def _():
                    body(w, jnp.maximum(e, 0) // self.nw)

    def over(self, w, k):
        here = self.here
        pairs = self.planes // 2
        to = 2 * lax.rem(here.plane // 2 + k, pairs) + here.side
        src = self.two[w].at[0]
        return remote(
            src, self.one_slot(w, here.plane // 2), self.x_s.at[w, k], self.x_r.at[w, here.plane // 2],
            here.s, to * CORES + here.c,
        )

    def one_slot(self, w, k):
        return self.acc[w].at[k, :, self.half(w, self.here.side)]

    def to_twin(self, w, side):
        part = self.outs[w].at[self.here.c, :, self.half(w, side)]
        return remote(part, part, self.t_s.at[w], self.t_r.at[w], self.here.s, self.here.twin)

    def to_mate(self, w, core, via):
        side = self.here.side if via == 0 else 1 - self.here.side
        part = self.outs[w].at[core, :, self.half(w, side)]
        return remote(part, part, self.f_s.at[w, via], self.f_r.at[w, via], self.here.s, self.here.mate)

    def finish(self):
        here = self.here
        for w in range(self.nw):
            self.far[w][here.row] = self.acc[w][here.s, :, self.half(w, here.side)]
            for k in range(self.nz - 1):
                off = lax.rem(here.row + 1 + k, self.nz)
                part = self.far[w].at[off]
                remote(part, part, self.z_s.at[w, k], self.z_r.at[w, off], here.s, here.r).wait_recv()
            far, out, lanes = self.far[w], self.outs[w], self.half(w, here.side)

            def strip(at):
                total = far[0, at, :].astype(F32)
                for k in range(1, self.nz):
                    total = total + far[k, at, :].astype(F32)
                out[here.c, at, lanes] = total.astype(BF16)

            self.strips(w, strip)
            self.to_twin(w, here.side).start()
            self.to_mate(w, here.c, 0).start()

    def twin_to_mate(self):
        for w in range(self.nw):
            self.to_twin(w, 1 - self.here.side).wait_recv()
            self.to_mate(w, self.here.c, 1).start()

    def drain(self):
        for w in range(self.nw):
            for via in (0, 1):
                self.to_mate(w, 1 - self.here.c, via).wait_recv()
                self.to_mate(w, self.here.c, via).wait_send()
            self.to_twin(w, self.here.side).wait_send()
            for k in range(self.nz):
                self.swap(w, k).wait_send()
                self.first(w, k).wait_send()
                self.second(w, k).wait_send()
                if k < self.nz - 1:
                    self.final(w, k).wait_send()


def sum_peers(here):
    p = here.p
    planes = p.R // CORES
    far = [(here.s, lax.rem(here.plane + k, planes) * CORES + j) for k in range(1, planes) for j in range(CORES)]
    twin_chip = here.twin - here.c
    return plane_peers(here) + far + [(here.beside, twin_chip + j) for j in range(CORES)]


def split_rows(p, grad):
    rows, cols = grad.shape
    return grad.reshape(p.S, CORES, rows // (p.S * CORES), cols)


def whole_shard(halves):
    return halves.reshape(CORES * halves.shape[1], halves.shape[2]).astype(F32)


def back_kernel(plan, nw, *refs):
    p = plan
    here = Place(p)
    s, c = here.s, here.c
    nz, near, width = here.rows, p.near, p.width
    (q, k, v, o, lse, preu, do_home, a_all, wcol, x, stream, par, small) = refs[:13]
    grads = refs[13 : 13 + nw]
    rest = refs[13 + nw :]
    input_grad, g_out, small_out = rest[:3]
    outs = rest[3 : 3 + nw]
    rest = rest[3 + nw :]
    (do_all, low, dk_acc, dv_acc, k_turn, da_own, da_out, da_in, da_side) = rest[:9]
    x_buf, stream_buf, buf_sem, a_buf, a_sem, gq = rest[-6:]
    rest = rest[:-6]
    da_home = input_grad
    (dw_out, dw_own, dw_in, dw_far, dw_end, small_acc, small_in, small_all) = rest[9:17]
    (do_ss, do_rs, dm_s, dm_r, dy_s, dy_r, dh_s, dh_r, wt_s, wt_r, wz_s, wz_r, wx_s, wx_r, wd_s, wd_r) = rest[17:33]
    (ss_s, ss_r, sa_s, sa_r) = rest[33:37]
    sums = GridSum(here, grads, outs, rest[37:])
    greet(sum_peers(here))
    rows_here = pl.ds(pl.multiple_of(lax.rem(s, p.P) * p.T, p.T), p.T)

    def do_copy(m, g):
        core, lane = g // p.cpu, g % p.cpu
        to = here.unit_of(c, m, s) * p.cpu + lane
        src = do_home.at[m, :, pl.ds(g * p.W, p.W)]
        dst = do_all.at[rows_here, :]
        away = jnp.logical_or(to != s, c != core)
        recv = do_rs.at[lax.rem(s, p.P)]
        return away, lambda: remote(src, dst, do_ss.at[m, g], recv, to, here.chip + core), (src, dst, recv)

    for m in range(p.M):
        for g in range(p.groups):
            launch(*do_copy(m, g))
    sums.begin()
    small_acc[...] = small[...]
    prefix = preu[0:1, 0:1]

    def block_rows(i):
        return pl.ds(pl.multiple_of(i * BQ, BQ), BQ)

    def a_load(b):
        slot = lax.rem(b, 2)
        return pltpu.make_async_copy(
            a_all.at[:, pl.ds(pl.multiple_of(b * BQ, BQ), BQ)], a_buf.at[slot], a_sem.at[slot]
        )

    def weight_part(h, dst, slot_from=None):
        def some(b, carry):
            slot = lax.rem(b, 2)

            @pl.when(b < p.D // BQ - 1)
            def _():
                a_load(b + 1).start()

            a_load(b).wait()
            dst[pl.ds(pl.multiple_of(b * BQ, BQ), BQ), :] = dot(a_buf[slot], low[h], 0, 0).astype(BF16)
            if slot_from is not None:
                sums.slot(slot_from + b)
            return carry

        lax.fori_loop(0, p.D // BQ, some, 0)

    def bias_part(h):
        folds = PAIR // width
        for row, lanes in ((0, slice(0, PAIR)), (1, slice(2 * PAIR, 3 * PAIR))):
            total = jnp.sum(low[h, :, lanes].astype(F32), axis=0, keepdims=True)
            for n in range(folds):
                at = (here.group * p.pairs + h) * folds + n
                small_acc[at, row : row + 1, 0:width] = total[:, n * width : (n + 1) * width]

    def to_twin_dw():
        return remote(dw_out, dw_in, wt_s.at[0], wt_r.at[0], s, here.twin)

    def pair_step(turn, carry):
        h = lax.rem(turn + 1 + here.side, 2)
        lanes = pl.ds(pl.multiple_of(h * PAIR, PAIR), PAIR)
        k_turn[...] = k[:, lanes].astype(F32).T.astype(BF16)
        dk_acc[...] = jnp.zeros_like(dk_acc)
        dv_acc[...] = jnp.zeros_like(dv_acc)

        def query_step(n, inner):
            j = lax.rem((here.unit - here.uq * near) * p.cpu + n // p.pieces, p.P)
            i = j * p.pieces + lax.rem(n, p.pieces)
            rows = block_rows(i)

            @pl.when(jnp.logical_and(turn == 0, lax.rem(n, p.pieces) == 0))
            def _():
                part = do_all.at[pl.ds(pl.multiple_of(j * p.T, p.T), p.T), :]
                pltpu.make_async_copy(part, part, do_rs.at[j]).wait()

            qp, dop, op = q[rows, lanes], do_all[rows, lanes], o[rows, lanes]
            turned = (dop.astype(F32) * op.astype(F32)).T
            pos = (lax.broadcasted_iota(jnp.int32, (1, BQ), 1) + i * BQ + 1).astype(F32)
            bound = jnp.maximum(pos, prefix)
            dq_t = []
            for e in (0, 1):
                lit = head_lanes(BQ, e)
                qe = jnp.where(lit, qp, jnp.zeros_like(qp))
                de = jnp.where(lit, dop, jnp.zeros_like(dop))
                level = lse[2 * h + e, 0:1, rows]
                inner_sum = jnp.sum(turned[e * HEAD : (e + 1) * HEAD], axis=0, keepdims=True)
                total = jnp.zeros((HEAD, BQ), F32)
                for start in range(0, LEN, KEYS):
                    keys = slice(start, start + KEYS)
                    key_pos = (lax.broadcasted_iota(jnp.int32, (KEYS, 1), 0) + start).astype(F32)
                    logits = dot(k[keys, lanes], qe, 1, 1)
                    probs = jnp.where(key_pos < bound, jnp.exp2(logits * SCALE2 - level), 0.0)
                    slope = dot(v[keys, lanes], de, 1, 1)
                    dlog = (probs * (slope - inner_sum)).astype(BF16)
                    dv_acc[keys, :] += dot(probs.astype(BF16), de)
                    dk_acc[keys, :] += dot(dlog, qe)
                    total = total + dot(k_turn[e * HEAD : (e + 1) * HEAD, keys], dlog)
                dq_t.append(total)
            low[h, rows, 0:PAIR] = (jnp.concatenate(dq_t, axis=0).T * SCALE).astype(BF16)
            sums.slot(turn * p.nq + n)
            return inner

        lax.fori_loop(0, p.nq, query_step, 0)
        low[h, :, PAIR : 2 * PAIR] = (dk_acc[...] * SCALE).astype(BF16)
        low[h, :, 2 * PAIR :] = dv_acc[...].astype(BF16)
        bias_part(h)

        a_load(0).start()

        @pl.when(turn == 0)
        def _():
            weight_part(h, dw_out)
            to_twin_dw().start()

        return carry

    lax.fori_loop(0, p.pairs, pair_step, 0)

    half = p.D // CORES

    def block_of(n):
        lane = lax.rem(here.lane + 1 + n // (near * p.pieces), p.cpu)
        m = lax.rem(n, near * p.pieces)
        return ((m // p.pieces) * p.cpu + lane) * p.pieces + lax.rem(m, p.pieces)

    def da_half(rows, core):
        at = pl.ds(pl.multiple_of(core * half, half), half)
        total = dot(low[0, rows, :], wcol[0, at, :], 1, 1)
        for h in range(1, p.pairs):
            total = total + dot(low[h, rows, :], wcol[h, at, :], 1, 1)
        return total

    def da_mate(n, i):
        rows = block_rows(i)
        return remote(da_out.at[rows, :], da_in.at[rows, :], dm_s.at[n], dm_r.at[i], s, here.mate)

    far_blocks = (p.cpu - 1) * near * p.pieces
    count = p.pairs * p.nq

    def side_rows(i):
        return block_rows((i // p.pieces // p.cpu) * p.pieces + lax.rem(i, p.pieces))

    def da_over(n, i):
        return remote(da_own.at[block_rows(i), :], da_side.at[side_rows(i), :], dy_s.at[n], dy_r.at[i], here.beside, here.r)

    def da_first(n, carry):
        @pl.when(n < p.nq)
        def _():
            i = block_of(n)
            rows = block_rows(i)
            da_out[rows, :] = da_half(rows, 1 - c).astype(BF16)
            da_mate(n, i).start()
            da_own[rows, :] = da_half(rows, c).astype(BF16)

        @pl.when(n > 0)
        def _():
            last = jnp.maximum(n - 1, 0)
            i = block_of(last)
            rows = block_rows(i)
            da_mate(last, i).wait_recv()
            da_own[rows, :] = (da_own[rows, :].astype(F32) + da_in[rows, :].astype(F32)).astype(BF16)

            @pl.when(last < far_blocks)
            def _():
                da_over(last, i).start()

        sums.slot(count + n)
        return carry

    lax.fori_loop(0, p.nq + 1, da_first, 0)
    count = count + p.nq + 1

    own_pair = here.side
    weight_part(own_pair, dw_own, count)
    count = count + p.D // BQ
    to_twin_dw().wait_recv()
    dw_own[...] = (dw_own[...].astype(F32) + dw_in[...].astype(F32)).astype(BF16)
    span = 2 * width

    def dw_rows(zr):
        return pl.ds(pl.multiple_of(zr * span, span), span)

    def dw_send(n):
        zr = lax.rem(here.row + 1 + n, nz)
        return remote(
            dw_own.at[dw_rows(zr), :], dw_far.at[here.row], wz_s.at[n], wz_r.at[here.row], 2 * zr + here.col, here.r
        )

    for n in range(nz - 1):
        dw_send(n).start()

    def da_back(n, i):
        rows = block_rows(i)
        home = here.uq * p.P + i // p.pieces
        piece = lax.rem(i, p.pieces)
        dst = da_home.at[here.um, block_rows(piece), pl.ds(pl.multiple_of(c * half, half), half)]
        src = da_own.at[rows, :]
        recv = dh_r.at[here.um, c, piece]
        away = jnp.logical_or(home != s, here.uc != c)
        return away, lambda: remote(src, dst, dh_s.at[n], recv, home, here.chip + here.uc), (src, dst, recv)

    def da_second(n, carry):
        i = block_of(n)
        rows = block_rows(i)
        da_over(n, i).wait_recv()
        da_own[rows, :] = (da_own[rows, :].astype(F32) + da_side[side_rows(i), :].astype(F32)).astype(BF16)
        launch(*da_back(n, i))
        sums.slot(count + n - far_blocks)
        return carry

    lax.fori_loop(far_blocks, p.nq, da_second, 0)
    count = count + p.nq - far_blocks

    def rest_of_sums(n, carry):
        sums.slot(n)
        return carry

    lax.fori_loop(count, max(count, sums.slots()), rest_of_sums, 0)
    sums.finish()

    dw_far[here.row] = dw_own[dw_rows(here.row), :]
    for n in range(nz - 1):
        off = lax.rem(here.row + 1 + n, nz)
        remote(dw_far.at[off], dw_far.at[off], wz_s.at[n], wz_r.at[off], s, here.r).wait_recv()
    total = dw_far[0].astype(F32)
    for n in range(1, nz):
        total = total + dw_far[n].astype(F32)
    dw_end[...] = total.astype(BF16)
    slot = here.group * p.pairs + here.side
    twin_chip = here.twin - c

    def dw_give(n):
        fy, fx, fc = n // 4, n // 2 % 2, n % 2
        col = here.col if fy == 0 else 1 - here.col
        core = c if fc == 0 else 1 - c
        src = dw_end.at[pl.ds(pl.multiple_of(col * width, width), width), :]
        dst = gq.at[slot]
        to = (2 * here.row + col, (here.chip if fx == 0 else twin_chip) + core)
        return src, dst, to

    for n in range(1, 8):
        src, dst, to = dw_give(n)
        remote(src, dst, wd_s.at[n], wd_r.at[slot], *to).start()
    gq[slot] = dw_end[pl.ds(pl.multiple_of(here.col * width, width), width), :]

    def token_loads(m, piece):
        at = pl.ds(piece * BQ, BQ)
        return (
            pltpu.make_async_copy(x.at[m, at, :], x_buf, buf_sem.at[0]),
            pltpu.make_async_copy(stream.at[m, at, :], stream_buf, buf_sem.at[1]),
        )

    for copy in token_loads(0, 0):
        copy.start()
    gain = par[4:5, :].astype(F32)
    gain_sum = jnp.zeros((1, p.D), F32)
    shift_sum = jnp.zeros((1, p.D), F32)
    for m in range(p.M):
        for piece in range(p.pieces):
            at = slice(piece * BQ, (piece + 1) * BQ)
            for core in range(CORES):
                dst = da_home.at[m, pl.ds(piece * BQ, BQ), pl.ds(core * half, half)]
                pltpu.make_async_copy(dst, dst, dh_r.at[m, core, piece]).wait()
            for copy in token_loads(m, piece):
                copy.wait()
            values = x_buf[...].astype(F32)
            dy = da_home[m, at, :].astype(F32)
            centre = values - jnp.mean(values, axis=-1, keepdims=True)
            spread = jnp.mean(centre * centre, axis=-1, keepdims=True)
            scale = lax.rsqrt(spread + EPS)
            wn = centre * scale
            e = dy * gain
            dw = scale * (e - jnp.mean(e, axis=-1, keepdims=True) - wn * jnp.mean(e * wn, axis=-1, keepdims=True))
            input_grad[m, at, :] = (stream_buf[...] + dw).astype(BF16)
            if m * p.pieces + piece + 1 < p.M * p.pieces:
                follow = m * p.pieces + piece + 1
                for copy in token_loads(follow // p.pieces, follow % p.pieces):
                    copy.start()
            gain_sum = gain_sum + jnp.sum(dy * wn, axis=0, keepdims=True)
            shift_sum = shift_sum + jnp.sum(dy, axis=0, keepdims=True)
    for n in range(p.S):
        lanes = slice(n * width, (n + 1) * width)
        small_acc[n, 4:5, 0:width] = gain_sum[:, lanes]
        small_acc[n, 8:9, 0:width] = shift_sum[:, lanes]

    def tiny(n):
        to = lax.rem(s + n, p.S)
        return remote(small_acc.at[to], small_in.at[n], ss_s.at[n], ss_r.at[n], to, here.r)

    for n in range(1, p.S):
        tiny(n).start()
    sums.twin_to_mate()
    total = small_acc[s]
    for n in range(1, p.S):
        tiny(n).wait_recv()
        total = total + small_in[n]
    small_all[here.r] = total

    def every(n):
        to = lax.rem(here.r + n, p.R)
        return remote(small_all.at[here.r], small_all.at[here.r], sa_s.at[n], sa_r.at[here.r], s, to)

    for n in range(1, p.R):
        every(n).start()
    for n in range(1, p.R):
        off = lax.rem(here.r + n, p.R)
        remote(small_all.at[0], small_all.at[off], sa_s.at[n], sa_r.at[off], s, here.r).wait_recv()
    total = small_all[0]
    for n in range(1, p.R):
        total = total + small_all[n]
    small_out[...] = total

    for m in range(p.M):
        for g in range(p.groups):
            sent(*do_copy(m, g))

    def da_sent(n, carry):
        i = block_of(n)
        da_mate(n, i).wait_send()

        @pl.when(n < far_blocks)
        def _():
            da_over(n, i).wait_send()

        @pl.when(n >= far_blocks)
        def _():
            sent(*da_back(n, i))

        return carry

    lax.fori_loop(0, p.nq, da_sent, 0)
    to_twin_dw().wait_send()
    for n in range(nz - 1):
        dw_send(n).wait_send()
    for n in range(1, 8):
        src, dst, to = dw_give(n)
        remote(src, dst, wd_s.at[n], wd_r.at[slot], *to).wait_send()
    for n in range(p.groups * p.pairs):

        @pl.when(n != slot)
        def _():
            remote(gq.at[n], gq.at[n], wd_s.at[0], wd_r.at[n], s, here.r).wait_recv()

        for k in range(3):
            at = k * p.D + n * PAIR
            g_out[:, at : at + PAIR] = gq[n, :, k * PAIR : (k + 1) * PAIR]

    for n in range(1, p.S):
        tiny(n).wait_send()
    for n in range(1, p.R):
        every(n).wait_send()
    sums.drain()


def back(plan, units, small, grads):
    p = plan
    nw = len(grads)
    nz = p.S // 2
    planes = p.R // CORES
    split = [split_rows(p, grad) for grad in grads]
    shapes = [h.shape[2:] for h in split]
    any_space = pl.BlockSpec(memory_space=pl.ANY)
    vmem = pl.BlockSpec(memory_space=pltpu.VMEM)
    dma = pltpu.SemaphoreType.DMA
    shape = jax.ShapeDtypeStruct
    half = p.D // CORES
    outs = pl.pallas_call(
        functools.partial(back_kernel, p, nw),
        out_shape=[
            shape((p.M, p.T, p.D), BF16),
            shape((p.width, 3 * p.D), BF16),
            shape(small.shape[1:], F32),
        ]
        + [shape((CORES,) + sh, BF16) for sh in shapes],
        in_specs=[vmem] * 6 + [any_space] * 2 + [vmem] + [any_space] * 2 + [vmem] * 2 + [any_space] * nw,
        out_specs=[vmem] * (3 + nw),
        scratch_shapes=[
            pltpu.VMEM((LEN, p.W), BF16),
            pltpu.VMEM((p.pairs, LEN, 3 * PAIR), BF16),
            pltpu.VMEM((LEN, PAIR), F32),
            pltpu.VMEM((LEN, PAIR), F32),
            pltpu.VMEM((PAIR, LEN), BF16),
            pltpu.VMEM((LEN, half), BF16),
            pltpu.VMEM((LEN, half), BF16),
            pltpu.VMEM((LEN, half), BF16),
            pltpu.VMEM((p.near * p.T, half), BF16),
            pltpu.VMEM((p.D, 3 * PAIR), BF16),
            pltpu.VMEM((p.D, 3 * PAIR), BF16),
            pltpu.VMEM((p.D, 3 * PAIR), BF16),
            pltpu.VMEM((nz, 2 * p.width, 3 * PAIR), BF16),
            pltpu.VMEM((2 * p.width, 3 * PAIR), BF16),
            pltpu.VMEM(small.shape, F32),
            pltpu.VMEM(small.shape, F32),
            pltpu.VMEM((p.R,) + small.shape[1:], F32),
            dma((p.M, p.groups)), dma((p.P,)),
            dma((p.nq,)), dma((p.nq,)), dma((p.nq,)), dma((p.nq,)),
            dma((p.nq,)), dma((p.M, CORES, p.pieces)),
            dma((1,)), dma((1,)), dma((nz,)), dma((nz,)), dma((planes,)), dma((planes,)), dma((8,)), dma((8,)),
            dma((p.S,)), dma((p.S,)), dma((p.R,)), dma((p.R,)),
        ]
        + GridSum.scratch(p, shapes)
        + [pltpu.VMEM((BQ, p.D), BF16), pltpu.VMEM((BQ, p.D), F32), dma((2,))]
        + [pltpu.VMEM((2, LEN, BQ), BF16), dma((2,))]
        + [pltpu.VMEM((p.groups * p.pairs, p.width, 3 * PAIR), BF16)],
        compiler_params=pltpu.CompilerParams(
            collective_id=1, has_side_effects=True, vmem_limit_bytes=VMEM_LIMIT
        ),
        name="back",
    )(*units, small, *split)
    return outs[0], outs[1].astype(F32), outs[2], [whole_shard(part) for part in outs[3:]]


def per_device(
    sizes,
    inputs,
    prefix,
    qkv_weight,
    qv_bias,
    out_weight,
    branch_bias,
    up_weight,
    up_bias,
    down_weight,
    norm_gain,
    norm_bias,
    cotangent,
):
    p = Plan(sizes, (inputs.shape[0], 1, inputs.shape[2], inputs.shape[3]))
    tokens_all = p.M * p.T
    x = inputs[:, 0]
    width = p.D // p.S
    spare = max(128 - width, 0)
    small_in = (qv_bias, branch_bias, norm_gain, norm_bias, up_bias.reshape(-1, width))
    (wo, wu, wd, parf, _, q, k, v, o, lse, preu, o_home, a_unit, w_unit) = fore(
        p, x, small_in, prefix[:, 0], qkv_weight, (out_weight, up_weight, down_weight)
    )
    par32 = parf.astype(F32)
    bias_branch = par32[2:4]
    gains, shifts = par32[4:8], par32[8:12]
    bias_up = par32[12:].reshape(-1, p.S, width).transpose(1, 0, 2).reshape(-1)

    tokens = x.reshape(tokens_all, p.D).astype(F32)
    upstream = cotangent[:, 0].reshape(tokens_all, p.D).astype(F32)
    mixed_low = o_home.reshape(tokens_all, p.D)
    branch = dot(mixed_low, wo) + bias_branch[0]
    side, pull_side = jax.vjp(normed, branch, gains[1:2], shifts[1:2])
    stream = tokens + side
    normal_mid, pull_mid = jax.vjp(normed, stream, gains[2:3], shifts[2:3])
    middle_low = normal_mid.astype(BF16)
    upper = dot(middle_low, wu) + bias_up
    below = 0.5 * (1.0 + lax.erf(upper * math.sqrt(0.5)))
    slope = below + upper * jnp.exp(-0.5 * upper * upper) * (1.0 / math.sqrt(2.0 * math.pi))
    active_low, slope = lax.optimization_barrier(((upper * below).astype(BF16), slope))
    lower = dot(active_low, wd) + bias_branch[1]
    closing, pull_close = jax.vjp(normed, lower, gains[3:4], shifts[3:4])
    output = (stream + closing).astype(BF16)
    grad_lower, gain_three, shift_three = pull_close(upstream)
    lower_low = grad_lower.astype(BF16)
    grad_active = dot(lower_low, wd, 1, 1)
    upper_low = (grad_active * slope).astype(BF16)
    grad_middle = dot(upper_low, wu, 1, 1)
    grad_mid_in, gain_two, shift_two = pull_mid(grad_middle)
    grad_stream = grad_mid_in + upstream
    grad_branch, gain_one, shift_one = pull_side(grad_stream)
    branch_low = grad_branch.astype(BF16)
    grad_mixed = dot(branch_low, wo, 1, 1).astype(BF16)

    grads = (
        dot(active_low, lower_low, 0, 0).astype(BF16),
        dot(middle_low, upper_low, 0, 0).astype(BF16),
        dot(mixed_low, branch_low, 0, 0).astype(BF16),
    )
    def column_sum(values):
        return jnp.sum(values.astype(F32), axis=0, keepdims=True)

    du_sum = column_sum(upper_low).reshape(p.S, -1, width).transpose(1, 0, 2).reshape(-1, p.D)
    none = jnp.zeros((1, p.D), F32)
    small = jnp.concatenate(
        [
            none, none, column_sum(branch_low), column_sum(lower_low),
            none, gain_one, gain_two, gain_three,
            none, shift_one, shift_two, shift_three,
            du_sum,
        ], axis=0,
    )
    small = jnp.pad(small.reshape(-1, p.S, width).transpose(1, 0, 2), ((0, 0), (0, 0), (0, spare)))
    by_token = (p.M, p.T, p.D)
    input_grad, sum_qkv, tiny, (sum_down, sum_up, sum_out) = back(
        p,
        (
            q, k, v, o, lse, preu, grad_mixed.reshape(by_token), a_unit, w_unit,
            x, grad_stream.reshape(by_token), parf,
        ),
        small, grads,
    )
    tiny = tiny[:, :width]
    shaped = (p.M, 1, p.T, p.D)
    return (
        output.reshape(shaped),
        input_grad.reshape(shaped),
        sum_qkv,
        tiny[0:2],
        sum_out,
        tiny[2:4],
        sum_up,
        tiny[12:].reshape(-1),
        sum_down,
        tiny[4:8],
        tiny[8:12],
    )


def solution(mesh):
    sizes = {name: mesh.shape[name] for name in ("shard", "replica")}
    placed = (
        P(None, "replica", "shard", None),
        P(None, "replica", None),
        P("shard", None),
        P(None, "shard"),
        P("shard", None),
        P(None, "shard"),
        P("shard", None),
        P("shard"),
        P("shard", None),
        P(None, "shard"),
        P(None, "shard"),
        P(None, "replica", "shard", None),
    )
    return jax.shard_map(
        functools.partial(per_device, sizes),
        mesh=mesh,
        in_specs=placed,
        out_specs=(
            P(None, "replica", "shard", None),
            P(None, "replica", "shard", None),
            P("shard", None),
            P(None, "shard"),
            P("shard", None),
            P(None, "shard"),
            P("shard", None),
            P("shard"),
            P("shard", None),
            P(None, "shard"),
            P(None, "shard"),
        ),
        check_vma=False,
    )
```

```python
import functools
import math

import jax
import jax.numpy as jnp
from jax import lax
from jax.experimental import pallas as pl
from jax.experimental.pallas import tpu as pltpu
from jax.sharding import PartitionSpec as P

HEAD = 64
LEN = 2048
CORES = 2
PAIR = 2 * HEAD
BQ = 256
EPS = 1e-05
MASKED = -1e30
SCALE = HEAD ** (-0.5)
SCALE2 = SCALE * math.log2(math.e)
F32 = jnp.float32
BF16 = jnp.bfloat16
MESH = pl.DeviceIdType.MESH
VMEM_LIMIT = 66_000_000
LAG = 2
KEYS = 512
SIDE_FIRST = (True, False, False)
SUM_LAG = 5
CADENCE = 1
COLUMN_FIRST = (False, True, False)
START = 1
EARLY = 1


class Plan:
    def __init__(self, mesh_shape, inputs_shape):
        self.S = mesh_shape["shard"]
        self.R = mesh_shape["replica"]
        self.M, _, self.T, self.D = inputs_shape
        self.Q = self.T * self.S // LEN
        self.P = LEN // self.T
        self.U = self.M * self.Q * CORES
        self.cpu = self.S // self.U
        self.heads = self.D // HEAD
        self.W = self.D // (CORES * self.cpu)
        self.pairs = self.W // PAIR
        self.groups = CORES * self.cpu
        self.pieces = self.T // BQ
        self.nq = LEN // BQ
        self.near = self.P // self.cpu
        self.width = self.D // self.S
        assert self.cpu == 2 and self.pairs == 2 and self.T % BQ == 0 and LEN % self.T == 0


class Place:
    def __init__(self, plan):
        self.p = plan
        self.s = lax.axis_index("shard")
        self.r = lax.axis_index("replica")
        self.c = lax.rem(self.r, CORES)
        self.chip = self.r - self.c
        self.mate = self.chip + (1 - self.c)
        self.unit = self.s // plan.cpu
        self.lane = lax.rem(self.s, plan.cpu)
        self.group = self.c * plan.cpu + self.lane
        self.uc = lax.rem(self.unit, CORES)
        self.um = lax.rem(self.unit // CORES, plan.M)
        self.uq = self.unit // (CORES * plan.M)
        self.ring = self.to_ring(self.s)
        self.plane = self.r // CORES
        self.side = lax.rem(self.plane, 2)
        self.twin = self.r + CORES * (1 - 2 * self.side)
        self.row = self.s // 2
        self.col = lax.rem(self.s, 2)
        self.beside = 2 * self.row + 1 - self.col
        self.rows = plan.S // 2

    def unit_of(self, c, m, s):
        return ((s // self.p.P) * self.p.M + m) * CORES + c

    def to_ring(self, s):
        half = self.p.S // 2
        row, col = s // 2, lax.rem(s, 2)
        return row + col * (2 * half - 1 - 2 * row)

    def from_ring(self, i):
        n = self.p.S
        return jnp.where(i < n // 2, 2 * i, 2 * (n - 1 - i) + 1)


def remote(src, dst, send, recv, s, r):
    return pltpu.make_async_remote_copy(
        src_ref=src, dst_ref=dst, send_sem=send, recv_sem=recv, device_id=(s, r), device_id_type=MESH
    )


def launch(away, far, near):
    @pl.when(away)
    def _():
        far().start()

    @pl.when(jnp.logical_not(away))
    def _():
        pltpu.make_async_copy(*near).start()


def sent(away, far, near):
    @pl.when(away)
    def _():
        far().wait_send()


def greet(peers):
    barrier = pltpu.get_barrier_semaphore()
    for s, r in peers:
        pl.semaphore_signal(barrier, inc=1, device_id=(s, r), device_id_type=MESH)
    pl.semaphore_wait(barrier, len(peers))


def plane_peers(here):
    n = here.p.S * CORES
    own = here.s * CORES + here.c
    out = []
    for k in range(1, n):
        i = lax.rem(own + k, n)
        out.append((i // CORES, here.chip + lax.rem(i, CORES)))
    return out


def normed(values, gain, shift):
    centre = values - jnp.mean(values, axis=-1, keepdims=True)
    spread = jnp.mean(centre * centre, axis=-1, keepdims=True)
    return centre * lax.rsqrt(spread + EPS) * gain + shift


def dot(a, b, ca=1, cb=0):
    return lax.dot_general(a, b, (((ca,), (cb,)), ((), ())), preferred_element_type=F32)


def head_lanes(rows, which):
    lane = lax.broadcasted_iota(jnp.int32, (rows, PAIR), 1)
    return (lane < HEAD) if which == 0 else (lane >= HEAD)


def fore_kernel(
    plan, x, biases, branches, gains, shifts, ups, prefixes, wq_in, wo, wu, wd,
    wof, wuf, wdf, parf, ah, q_out, k_out, v_out, o_out, lse_out, preu, oh, a_all, wcol,
    par, pre, wq, parg, pre2,
    par_ss, par_rs, pre_sem, loc_sem, a_ss, a_rs, af_ss, z_ss, z_rs, wa_ss, wa_rs, wb_ss, wb_rs, wm_ss, wm_rs,
    o_ss, o_rs, q_ss, q_rs, qt_ss, qt_rs, q_loc,
):
    p = plan
    here = Place(p)
    s, c = here.s, here.c
    mine, full = (wo, wu, wd), (wof, wuf, wdf)
    nw = len(mine)
    first = COLUMN_FIRST
    greet(plane_peers(here) + [(s, here.twin)])

    par[...] = jnp.zeros_like(par)
    at = 0
    for part in (biases, branches, gains, shifts, ups):
        par[at : at + part.shape[0], 0 : part.shape[1]] = part[...]
        at += part.shape[0]
    pre[...] = jnp.zeros_like(pre)
    for m in range(p.M):
        for n in range(p.Q):
            pre[m * p.Q + n : m * p.Q + n + 1, :] = jnp.full((1, 128), prefixes[m, n].astype(F32))
    for g in range(p.groups):
        for h in range(p.pairs):
            for k in range(3):
                at = k * p.D + g * p.W + h * PAIR
                wq[g, h, :, k * PAIR : (k + 1) * PAIR] = wq_in[:, at : at + PAIR]
    parg[s] = par[...]
    small = []
    for k in range(1, p.S):
        to = lax.rem(s + k, p.S)
        small.append(remote(par, parg.at[s], par_ss.at[k], par_rs.at[k], to, here.r))
        small[-1].start()
    swap = remote(pre, pre2, pre_sem.at[0], pre_sem.at[1], s, here.mate)
    swap.start()

    z, nz = here.row, here.rows

    def where(w, zr, fa, fb, core):
        fy, fx = (fa, fb) if first[w] else (fb, fa)
        col = here.col if fy == 0 else 1 - here.col
        side = here.side if fx == 0 else 1 - here.side
        n, width = mine[w].shape[0], mine[w].shape[1] // 2
        rows = pl.ds(pl.multiple_of((2 * zr + col) * n + core * (n // 2), n // 2), n // 2)
        return full[w].at[rows, pl.ds(pl.multiple_of(side * width, width), width)]

    def origin(w, fa):
        n, width = mine[w].shape[0], mine[w].shape[1] // 2
        side = here.side if fa == 0 else 1 - here.side
        rows = pl.ds(pl.multiple_of(c * (n // 2), n // 2), n // 2)
        return mine[w].at[rows, pl.ds(pl.multiple_of(side * width, width), width)]

    def peer(w, second):
        return (here.beside, here.r) if first[w] == (second == 0) else (s, here.twin)

    def z_send(w, d, k):
        sign = 1 - 2 * d
        part = where(w, z - sign * (k - 1), 0, 0, c)
        src = origin(w, 0) if isinstance(k, int) and k == 1 else part
        return remote(src, part, z_ss.at[w, d, k - 1], z_rs.at[w, d, k - 1], s + 2 * sign, here.r)

    def z_came(w, d, k):
        sign = 1 - 2 * d
        part = where(w, z - sign * k, 0, 0, c)
        return remote(part, part, z_ss.at[w, d, k - 1], z_rs.at[w, d, k - 1], s, here.r)

    def to_first(w, zr, src=None):
        part = where(w, zr, 0, 0, c)
        return remote(part if src is None else src, part, wa_ss.at[w, zr], wa_rs.at[w, zr], *peer(w, 0))

    def to_second(w, fa, zr, src=None):
        part = where(w, zr, fa, 0, c)
        return remote(part if src is None else src, part, wb_ss.at[w, fa, zr], wb_rs.at[w, fa, zr], *peer(w, 1))

    def to_mate(w, fa, fb, zr, core):
        part = where(w, zr, fa, fb, core)
        at = 2 * fa + fb
        return remote(part, part, wm_ss.at[w, at, zr], wm_rs.at[w, at, zr], s, here.mate)

    def first_came(w, zr):
        part = where(w, zr, 1, 0, c)
        return remote(part, part, wa_ss.at[w, zr], wa_rs.at[w, zr], s, here.r)

    def second_came(w, fa, zr):
        part = where(w, zr, fa, 1, c)
        return remote(part, part, wb_ss.at[w, fa, zr], wb_rs.at[w, fa, zr], s, here.r)

    def on_grid(d, k):
        return z >= k if d == 0 else z + k < nz

    def can_send(d):
        return z < nz - 1 if d == 0 else z > 0

    def gather_rows(w):
        for d in (0, 1):

            @pl.when(can_send(d))
            def _():
                z_send(w, d, 1).start()

    def gather_near(w):
        if first[w]:
            to_first(w, z, origin(w, 0)).start()
        else:
            to_second(w, 0, z, origin(w, 0)).start()
            to_second(w, 1, z, origin(w, 1)).start()

    def gather_slot(w, k, lag):
        for d in (0, 1):
            sign = 1 - 2 * d

            @pl.when(jnp.logical_and(k >= 1, on_grid(d, k)))
            def _():
                at = jnp.maximum(k, 1)
                z_came(w, d, at).wait_recv()
                zr = z - sign * at

                @pl.when(can_send(d))
                def _():
                    z_send(w, d, at + 1).start()

                to_first(w, zr).start()
                to_second(w, 0, zr).start()
                to_mate(w, 0, 0, zr, c).start()

        def at_distance(j, least, body):
            for d in (0, 1):
                ok = jnp.logical_and(j >= max(least, d), on_grid(d, j))

                @pl.when(ok)
                def _():
                    body(z - (1 - 2 * d) * jnp.maximum(j, 0))

        def after_first(zr):
            first_came(w, zr).wait_recv()
            to_second(w, 1, zr).start()
            to_mate(w, 1, 0, zr, c).start()

        at_distance(k - 1, 0 if first[w] else 1, after_first)

        def after_second(fa):
            def body(zr):
                second_came(w, fa, zr).wait_recv()
                to_mate(w, fa, 1, zr, c).start()

            return body

        at_distance(k - 1 - lag, 1 if first[w] else 0, after_second(0))
        at_distance(k - 2 - lag, 0, after_second(1))

    def mate_pieces(w, zr, act):
        other = zr != z

        @pl.when(other)
        def _():
            act(0, 0)

        if first[w]:

            @pl.when(other)
            def _():
                act(0, 1)

            act(1, 0)
        else:

            @pl.when(other)
            def _():
                act(1, 0)

            act(0, 1)
        act(1, 1)

    def gather_wait(w):
        def one(zr, carry):
            mate_pieces(w, zr, lambda fa, fb: to_mate(w, fa, fb, zr, 1 - c).wait_recv())
            return carry

        lax.fori_loop(0, nz, one, 0)

    def gather_drain(w):
        def one(zr, carry):
            mate_pieces(w, zr, lambda fa, fb: to_mate(w, fa, fb, zr, c).wait_send())
            if first[w]:
                to_first(w, zr).wait_send()

                @pl.when(zr != z)
                def _():
                    to_second(w, 0, zr).wait_send()
            else:

                @pl.when(zr != z)
                def _():
                    to_first(w, zr).wait_send()

                to_second(w, 0, zr).wait_send()
            to_second(w, 1, zr).wait_send()
            for d in (0, 1):
                reach = zr <= z if d == 0 else zr < nz - z

                @pl.when(jnp.logical_and(can_send(d), reach))
                def _():
                    z_send(w, d, zr + 1).wait_send()

            return carry

        lax.fori_loop(0, nz, one, 0)

    nq_rows = wq.shape[2]
    half_rows = nq_rows // 2

    def q_rows(k, side):
        return pl.ds(pl.multiple_of(k * nq_rows + side * half_rows, half_rows), half_rows)

    def q_send(k):
        to = lax.rem(s + k, p.S)
        group = c * p.cpu + lax.rem(to, p.cpu)
        rows = pl.ds(pl.multiple_of(here.side * half_rows, half_rows), half_rows)
        src = wq.at[group, :, rows, :]
        return remote(src, wcol.at[:, q_rows(s, here.side), :], q_ss.at[k], q_rs.at[s], to, here.r)

    def q_twin(k, side):
        part = wcol.at[:, q_rows(k, side), :]
        return remote(part, part, qt_ss.at[k], qt_rs.at[k], s, here.twin)

    def q_from(k):
        return lax.rem(s + p.S - k, p.S)

    for k in range(1, p.S):
        q_send(k).start()
    for w in range(nw):
        gather_near(w)
    q_own = pltpu.make_async_copy(
        wq.at[here.group], wcol.at[:, pl.ds(pl.multiple_of(s * nq_rows, nq_rows), nq_rows), :], q_loc.at[0]
    )
    q_own.start()
    local = []
    for w in range(nw):
        n = mine[w].shape[0]
        local.append(
            pltpu.make_async_copy(mine[w], full[w].at[pl.ds(pl.multiple_of(s * n, n), n), :], loc_sem.at[w])
        )
        local[-1].start()

    for k in range(1, p.S):
        small[k - 1].wait_recv()
    parf[...] = jnp.concatenate([parg[k][:, : p.D // p.S] for k in range(p.S)], axis=1)
    gain = parf[4:5, :].astype(F32)
    shift = parf[8:9, :].astype(F32)
    rows_here = pl.ds(pl.multiple_of(lax.rem(s, p.P) * p.T, p.T), p.T)

    def first_hop(m):
        to = here.unit_of(c, m, s) * p.cpu + here.lane
        far = lambda: remote(ah.at[m], a_all.at[rows_here, :], a_ss.at[m], a_rs.at[lax.rem(s, p.P)], to, here.r)
        return to, far

    for m in range(p.M):
        ah[m] = normed(x[m].astype(F32), gain, shift).astype(BF16)
        to, far = first_hop(m)

        @pl.when(to != s)
        def _():
            far().start()

        @pl.when(to == s)
        def _():
            a_all[rows_here, :] = ah[m]

    primary = c == here.uc

    def a_rows(j):
        return pl.ds(pl.multiple_of(j * p.T, p.T), p.T)

    def a_forward(j, k):
        part = a_all.at[a_rows(j), :]
        if k == 0:
            return remote(part, part, af_ss.at[j, 0], a_rs.at[j], s, here.mate)
        to = here.unit * p.cpu + lax.rem(here.lane + k, p.cpu)
        return remote(part, part, af_ss.at[j, k], a_rs.at[j], to, here.r)

    def a_wait(j):
        part = a_all.at[a_rows(j), :]
        remote(part, part, af_ss.at[j, 0], a_rs.at[j], s, here.mate).wait_recv()

    near = p.near

    zi = here.unit - here.uq * near

    def a_at(k, body):
        for d in (0, 1):
            if k or not d:
                ok = zi >= k if d == 0 else zi + k < near

                @pl.when(jnp.logical_and(primary, ok))
                def _():
                    body(zi - (1 - 2 * d) * k)

    def a_near(jj):
        j = jj * p.cpu + here.lane

        @pl.when(here.uq * p.P + j != s)
        def _():
            a_wait(j)

        for k in list(range(1, p.cpu)) + [0]:
            a_forward(j, k).start()

    def a_far(jj):
        for k in range(1, p.cpu):
            j = jj * p.cpu + lax.rem(here.lane + k, p.cpu)
            a_wait(j)
            a_forward(j, 0).start()

    each = -(-(p.S - 1) // near)
    for k in range(near + 1):
        if k < near:
            for n in range(1 + k * each, min(1 + (k + 1) * each, p.S)):
                part = wcol.at[:, q_rows(q_from(n), here.side), :]
                remote(part, part, q_ss.at[n], q_rs.at[q_from(n)], s, here.r).wait_recv()
                q_twin(q_from(n), here.side).start()
            a_at(k, a_near)
        if k == START:
            for w in range(nw):
                gather_rows(w)
        if k >= 1:
            a_at(k - 1, a_far)
        if k >= near + 1 - EARLY:
            for w in range(nw):
                gather_slot(w, k - (near - EARLY), LAG)

    @pl.when(jnp.logical_not(primary))
    def _():
        for j in range(p.P):
            a_wait(j)

    swap.wait_recv()
    pre2[...] = jnp.where(primary, pre[...], pre2[...])
    row = here.um * p.Q + here.uq
    preu[...] = jnp.broadcast_to(pre2[pl.ds(row, 1), :], preu.shape)

    for n in range(1, p.S):
        q_twin(q_from(n), 1 - here.side).wait_recv()
    q_own.wait()
    own = pl.ds(pl.multiple_of(here.group * p.W, PAIR), p.W)
    q_bias = parf[0:1, own].astype(F32)
    v_bias = parf[1:2, own].astype(F32)

    def project(i, carry):
        rows = pl.ds(pl.multiple_of(i * BQ, BQ), BQ)
        part = a_all[rows, :]
        for h in range(p.pairs):
            lanes = slice(h * PAIR, (h + 1) * PAIR)
            got = dot(part, wcol[h])
            q_out[rows, lanes] = (got[:, :PAIR] + q_bias[:, lanes]).astype(BF16)
            k_out[rows, lanes] = got[:, PAIR : 2 * PAIR].astype(BF16)
            v_out[rows, lanes] = (got[:, 2 * PAIR :] + v_bias[:, lanes]).astype(BF16)
        return carry

    lax.fori_loop(0, p.nq, project, 0)

    prefix = preu[0:1, 0:1]
    slots = nz + 1 + LAG - EARLY
    per = -(-slots // p.nq)

    def o_copy(i):
        rows = pl.ds(pl.multiple_of(i * BQ, BQ), BQ)
        home = here.uq * p.P + i // p.pieces
        piece = lax.rem(i, p.pieces)
        there = pl.ds(pl.multiple_of(piece * BQ, BQ), BQ)
        src = o_out.at[rows, :]
        dst = oh.at[here.um, there, own]
        away = jnp.logical_or(home != s, here.uc != c)
        recv = o_rs.at[here.um, here.group, piece]
        return away, lambda: remote(src, dst, o_ss.at[i], recv, home, here.chip + here.uc), (src, dst, recv)

    def attend(i, carry):
        rows = pl.ds(pl.multiple_of(i * BQ, BQ), BQ)
        row_pos = (lax.broadcasted_iota(jnp.int32, (BQ, 1), 0) + i * BQ + 1).astype(F32)
        bound = jnp.maximum(row_pos, prefix)
        key_pos = lax.broadcasted_iota(jnp.int32, (1, LEN), 1).astype(F32)
        seen = key_pos < bound

        def pair_step(h, inner):
            lanes = pl.ds(pl.multiple_of(h * PAIR, PAIR), PAIR)
            qp, kp, vp = q_out[rows, lanes], k_out[:, lanes], v_out[:, lanes]
            halves = []
            for e in (0, 1):
                logits = dot(jnp.where(head_lanes(BQ, e), qp, jnp.zeros_like(qp)), kp, 1, 1)
                logits = jnp.where(seen, logits, MASKED)
                top = jnp.max(logits, axis=1, keepdims=True)
                powers = jnp.exp2((logits - top) * SCALE2)
                total = jnp.sum(powers, axis=1, keepdims=True)
                halves.append(dot(powers.astype(BF16), vp) * (1.0 / total))
                level = top * SCALE2 + jnp.log2(total)
                turned = jnp.broadcast_to(level, (BQ, 128)).T
                lse_out[2 * h + e, :, pl.ds(pl.multiple_of(i * BQ, BQ), BQ)] = turned[0:8]
            o_out[rows, lanes] = jnp.where(head_lanes(BQ, 0), halves[0], halves[1]).astype(BF16)
            return inner

        lax.fori_loop(0, p.pairs, pair_step, 0)
        launch(*o_copy(i))

        for extra in range(per):
            for w in range(nw):
                gather_slot(w, i * per + extra + 1 + EARLY, LAG)

        return carry

    lax.fori_loop(0, p.nq, attend, 0)

    for m in range(p.M):
        for g in range(p.groups):
            for piece in range(p.pieces):
                src = o_out.at[pl.ds(0, BQ), :]
                dst = oh.at[m, pl.ds(piece * BQ, BQ), pl.ds(g * p.W, p.W)]
                pltpu.make_async_copy(src, dst, o_rs.at[m, g, piece]).wait()

    def o_sent(i, carry):
        sent(*o_copy(i))
        return carry

    lax.fori_loop(0, p.nq, o_sent, 0)
    for copy in small:
        copy.wait_send()
    swap.wait_send()
    for copy in local:
        copy.wait()
    for n in range(1, p.S):
        q_send(n).wait_send()
        q_twin(q_from(n), here.side).wait_send()
    for m in range(p.M):
        to, far = first_hop(m)

        @pl.when(to != s)
        def _():
            far().wait_send()

    @pl.when(primary)
    def _():
        for jj in range(near):
            for k in range(p.cpu):
                a_forward(jj * p.cpu + here.lane, k).wait_send()
            for k in range(1, p.cpu):
                a_forward(jj * p.cpu + lax.rem(here.lane + k, p.cpu), 0).wait_send()

    for w in range(nw):
        gather_wait(w)
        gather_drain(w)


def fore(plan, x, small, prefixes, qkv, weights):
    p = plan
    par = (sum(part.shape[0] for part in small), max(p.width, 128))
    nz = p.S // 2
    nw = len(weights)
    any_space = pl.BlockSpec(memory_space=pl.ANY)
    vmem = pl.BlockSpec(memory_space=pltpu.VMEM)
    shape = jax.ShapeDtypeStruct
    out_shape = (
        [shape((w.shape[0] * p.S, w.shape[1]), BF16) for w in weights]
        + [shape((par[0], p.D), BF16), shape((p.M, p.T, p.D), BF16)]
        + [shape((LEN, p.W), BF16)] * 4
        + [shape((2 * p.pairs, 8, LEN), F32), shape((8, 128), F32), shape((p.M, p.T, p.D), BF16)]
        + [shape((LEN, p.D), BF16), shape((p.pairs, p.D, 3 * PAIR), BF16)]
    )
    dma = pltpu.SemaphoreType.DMA
    return pl.pallas_call(
        functools.partial(fore_kernel, p),
        out_shape=out_shape,
        in_specs=[vmem] * 6 + [pl.BlockSpec(memory_space=pltpu.SMEM)] + [vmem] * (1 + nw),
        out_specs=[any_space] * nw + [vmem] * 11,
        scratch_shapes=[
            pltpu.VMEM(par, BF16),
            pltpu.VMEM((8, 128), F32),
            pltpu.VMEM((p.groups, p.pairs, qkv.shape[0], 3 * PAIR), BF16),
            pltpu.VMEM((p.S,) + par, BF16),
            pltpu.VMEM((8, 128), F32),
            dma((p.S,)), dma((p.S,)), dma((2,)), dma((nw,)),
            dma((p.M,)), dma((p.P,)), dma((p.P, p.cpu)),
            dma((nw, 2, nz)), dma((nw, 2, nz)), dma((nw, nz)), dma((nw, nz)),
            dma((nw, 2, nz)), dma((nw, 2, nz)), dma((nw, 4, nz)), dma((nw, 4, nz)),
            dma((p.nq,)), dma((p.M, p.groups, p.pieces)),
            dma((p.S,)), dma((p.S,)), dma((p.S,)), dma((p.S,)), dma((1,)),
        ],
        compiler_params=pltpu.CompilerParams(
            collective_id=0, has_side_effects=True, vmem_limit_bytes=VMEM_LIMIT
        ),
        name="fore",
    )(x, *small, prefixes, qkv, *weights)


class GridSum:
    def __init__(self, here, grads, outs, refs):
        self.here, self.grads, self.outs = here, grads, outs
        self.nw = nw = len(grads)
        self.nz = here.rows
        self.planes = here.p.R // CORES
        self.own, self.acc, self.one, self.two, self.far = (refs[k * nw : (k + 1) * nw] for k in range(5))
        (self.ld, self.m_s, self.m_r, self.a_s, self.a_r, self.b_s, self.b_r, self.z_s, self.z_r) = refs[5 * nw : 5 * nw + 9]
        (self.x_s, self.x_r, self.t_s, self.t_r, self.f_s, self.f_r) = refs[5 * nw + 9 :]
        self.side_first = SIDE_FIRST

    @staticmethod
    def scratch(plan, shapes):
        nw = len(shapes)
        planes = plan.R // CORES
        nz = plan.S // 2
        dma = pltpu.SemaphoreType.DMA
        return (
            [pltpu.VMEM((2,) + sh, BF16) for sh in shapes]
            + [pltpu.VMEM((plan.S,) + sh, BF16) for sh in shapes]
            + [
                pltpu.VMEM((plan.S, sh[0], sh[1] // 2) if sf else (nz,) + sh, BF16)
                for sh, sf in zip(shapes, SIDE_FIRST)
            ]
            + [pltpu.VMEM((nz, sh[0], sh[1] // 2), BF16) for sh in shapes]
            + [pltpu.VMEM((max(nz, planes // 2), sh[0], sh[1] // 2), BF16) for sh in shapes]
            + [dma((nw,))]
            + [dma((nw, nz))] * 8
            + [dma((nw, planes))] * 2
            + [dma((nw,))] * 2
            + [dma((nw, 2))] * 2
        )

    @staticmethod
    def count(nw):
        return 5 * nw + 15

    def zr(self, k):
        return lax.rem(self.here.row + 1 + k, self.nz)

    def half(self, w, side):
        n = self.acc[w].shape[2] // 2
        return pl.ds(pl.multiple_of(side * n, n), n)

    def load(self, w, k):
        src = self.grads[w].at[pl.ds(2 * self.zr(k), 2), self.here.c]
        return pltpu.make_async_copy(src, self.own[w], self.ld.at[w])

    def swap(self, w, k):
        here = self.here
        pair = pl.ds(2 * self.zr(k), 2)
        return remote(
            self.grads[w].at[pair, 1 - here.c], self.acc[w].at[pair], self.m_s.at[w, k], self.m_r.at[w, k], here.s, here.mate
        )

    def first(self, w, k):
        here, zr = self.here, self.zr(k)
        if self.side_first[w]:
            pair = pl.ds(2 * zr, 2)
            src = self.acc[w].at[pair, :, self.half(w, 1 - here.side)]
            return remote(src, self.one[w].at[pair], self.a_s.at[w, k], self.a_r.at[w, k], here.s, here.twin)
        src = self.acc[w].at[2 * zr + 1 - here.col]
        return remote(src, self.one[w].at[zr], self.a_s.at[w, k], self.a_r.at[w, k], here.beside, here.r)

    def second(self, w, k):
        here, zr = self.here, self.zr(k)
        if self.side_first[w]:
            src = self.acc[w].at[2 * zr + 1 - here.col, :, self.half(w, here.side)]
            to = (here.beside, here.r)
        else:
            src = self.acc[w].at[2 * zr + here.col, :, self.half(w, 1 - here.side)]
            to = (here.s, here.twin)
        return remote(src, self.two[w].at[zr], self.b_s.at[w, k], self.b_r.at[w, k], *to)

    def final(self, w, k):
        here, zr = self.here, self.zr(k)
        src = self.acc[w].at[2 * zr + here.col, :, self.half(w, here.side)]
        return remote(
            src, self.far[w].at[here.row], self.z_s.at[w, k], self.z_r.at[w, here.row], 2 * zr + here.col, here.r
        )

    def begin(self):
        for k in range(self.nz):
            for w in range(self.nw):
                self.swap(w, k).start()
                if k == 0:
                    self.load(w, 0).start()

    def strips(self, w, body):
        def one(r, carry):
            body(pl.ds(pl.multiple_of(r * 16, 16), 16))
            return carry

        lax.fori_loop(0, self.acc[w].shape[1] // 16, one, 0)

    def event_one(self, w, k):
        zr = self.zr(k)
        pair = pl.ds(2 * zr, 2)
        self.load(w, k).wait()
        self.swap(w, k).wait_recv()
        acc, own = self.acc[w], self.own[w]

        def strip(at):
            acc[pair, at, :] = (acc[pair, at, :].astype(F32) + own[:, at, :].astype(F32)).astype(BF16)

        self.strips(w, strip)
        self.first(w, k).start()

        @pl.when(k < self.nz - 1)
        def _():
            self.load(w, jnp.minimum(k + 1, self.nz - 1)).start()

    def event_two(self, w, k):
        here, zr = self.here, self.zr(k)
        self.first(w, k).wait_recv()
        acc, one = self.acc[w], self.one[w]
        if self.side_first[w]:
            pair = pl.ds(2 * zr, 2)
            lanes = self.half(w, here.side)

            def strip(at):
                acc[pair, at, lanes] = (acc[pair, at, lanes].astype(F32) + one[pair, at, :].astype(F32)).astype(BF16)

        else:
            shard = 2 * zr + here.col

            def strip(at):
                acc[shard, at, :] = (acc[shard, at, :].astype(F32) + one[zr, at, :].astype(F32)).astype(BF16)

        self.strips(w, strip)
        self.second(w, k).start()

    def event_three(self, w, k):
        here, zr = self.here, self.zr(k)
        self.second(w, k).wait_recv()
        shard, lanes = 2 * zr + here.col, self.half(w, here.side)
        acc, two = self.acc[w], self.two[w]

        def strip(at):
            acc[shard, at, lanes] = (acc[shard, at, lanes].astype(F32) + two[zr, at, :].astype(F32)).astype(BF16)

        self.strips(w, strip)

        @pl.when(k < self.nz - 1)
        def _():
            self.final(w, k).start()

    def slots(self):
        return CADENCE * (self.nw * self.nz + 2 * SUM_LAG)

    def slot(self, n):
        @pl.when(lax.rem(n, CADENCE) == 0)
        def _():
            self.event(n // CADENCE)

    def event(self, n):
        for stage, body in ((2, self.event_three), (1, self.event_two), (0, self.event_one)):
            e = n - stage * SUM_LAG
            for w in range(self.nw):
                ok = jnp.logical_and(e >= 0, e < self.nw * self.nz)

                @pl.when(jnp.logical_and(ok, lax.rem(e, self.nw) == w))
                def _():
                    body(w, jnp.maximum(e, 0) // self.nw)

    def over(self, w, k):
        here = self.here
        pairs = self.planes // 2
        to = 2 * lax.rem(here.plane // 2 + k, pairs) + here.side
        src = self.two[w].at[0]
        return remote(
            src, self.one_slot(w, here.plane // 2), self.x_s.at[w, k], self.x_r.at[w, here.plane // 2],
            here.s, to * CORES + here.c,
        )

    def one_slot(self, w, k):
        return self.acc[w].at[k, :, self.half(w, self.here.side)]

    def to_twin(self, w, side):
        part = self.outs[w].at[self.here.c, :, self.half(w, side)]
        return remote(part, part, self.t_s.at[w], self.t_r.at[w], self.here.s, self.here.twin)

    def to_mate(self, w, core, via):
        side = self.here.side if via == 0 else 1 - self.here.side
        part = self.outs[w].at[core, :, self.half(w, side)]
        return remote(part, part, self.f_s.at[w, via], self.f_r.at[w, via], self.here.s, self.here.mate)

    def finish(self):
        here = self.here
        for w in range(self.nw):
            self.far[w][here.row] = self.acc[w][here.s, :, self.half(w, here.side)]
            for k in range(self.nz - 1):
                off = lax.rem(here.row + 1 + k, self.nz)
                part = self.far[w].at[off]
                remote(part, part, self.z_s.at[w, k], self.z_r.at[w, off], here.s, here.r).wait_recv()
            far, out, lanes = self.far[w], self.outs[w], self.half(w, here.side)

            def strip(at):
                total = far[0, at, :].astype(F32)
                for k in range(1, self.nz):
                    total = total + far[k, at, :].astype(F32)
                out[here.c, at, lanes] = total.astype(BF16)

            self.strips(w, strip)
            self.to_twin(w, here.side).start()
            self.to_mate(w, here.c, 0).start()

    def twin_to_mate(self):
        for w in range(self.nw):
            self.to_twin(w, 1 - self.here.side).wait_recv()
            self.to_mate(w, self.here.c, 1).start()

    def drain(self):
        for w in range(self.nw):
            for via in (0, 1):
                self.to_mate(w, 1 - self.here.c, via).wait_recv()
                self.to_mate(w, self.here.c, via).wait_send()
            self.to_twin(w, self.here.side).wait_send()
            for k in range(self.nz):
                self.swap(w, k).wait_send()
                self.first(w, k).wait_send()
                self.second(w, k).wait_send()
                if k < self.nz - 1:
                    self.final(w, k).wait_send()


def sum_peers(here):
    p = here.p
    planes = p.R // CORES
    far = [(here.s, lax.rem(here.plane + k, planes) * CORES + j) for k in range(1, planes) for j in range(CORES)]
    twin_chip = here.twin - here.c
    return plane_peers(here) + far + [(here.beside, twin_chip + j) for j in range(CORES)]


def split_rows(p, grad):
    rows, cols = grad.shape
    return grad.reshape(p.S, CORES, rows // (p.S * CORES), cols)


def whole_shard(halves):
    return halves.reshape(CORES * halves.shape[1], halves.shape[2]).astype(F32)


def mid_kernel(plan, nw, do_home, *refs):
    p = plan
    here = Place(p)
    s, c = here.s, here.c
    pairs = [(refs[2 * w], refs[2 * w + 1]) for w in range(nw)]
    do_all = refs[2 * nw]
    outs = refs[2 * nw + 1 : 3 * nw + 1]
    held = refs[3 * nw + 1 : 4 * nw + 1]
    do_ss, do_rs = refs[4 * nw + 1 : 4 * nw + 3]
    sems = refs[4 * nw + 3 :]
    greet(plane_peers(here))
    rows_here = pl.ds(pl.multiple_of(lax.rem(s, p.P) * p.T, p.T), p.T)

    def do_copy(m, g):
        core, lane = g // p.cpu, g % p.cpu
        to = here.unit_of(c, m, s) * p.cpu + lane
        src = do_home.at[m, :, pl.ds(g * p.W, p.W)]
        dst = do_all.at[rows_here, :]
        away = jnp.logical_or(to != s, c != core)
        recv = do_rs.at[lax.rem(s, p.P)]
        return away, lambda: remote(src, dst, do_ss.at[m, g], recv, to, here.chip + core), (src, dst, recv)

    for m in range(p.M):
        for g in range(p.groups):
            launch(*do_copy(m, g))

    def strip(w, b):
        rows = pl.ds(pl.multiple_of(b * BQ, BQ), BQ)
        return pltpu.make_async_copy(held[w].at[rows, :], outs[w].at[rows, :], sems[w].at[b])

    for w, (former, latter) in enumerate(pairs):
        count = former.shape[1] // BQ

        def one(b, carry):
            lanes = pl.ds(pl.multiple_of(b * BQ, BQ), BQ)
            held[w][lanes, :] = dot(former[:, lanes], latter[...], 0, 0).astype(BF16)
            strip(w, b).start()
            return carry

        lax.fori_loop(0, count, one, 0)

    for j in range(p.P):
        part = do_all.at[pl.ds(j * p.T, p.T), :]
        pltpu.make_async_copy(part, part, do_rs.at[j]).wait()
    for m in range(p.M):
        for g in range(p.groups):
            sent(*do_copy(m, g))
    for w, (former, latter) in enumerate(pairs):

        def done(b, carry):
            strip(w, b).wait()
            return carry

        lax.fori_loop(0, former.shape[1] // BQ, done, 0)


def mid(plan, do_home, pairs):
    p = plan
    nw = len(pairs)
    any_space = pl.BlockSpec(memory_space=pl.ANY)
    vmem = pl.BlockSpec(memory_space=pltpu.VMEM)
    dma = pltpu.SemaphoreType.DMA
    shapes = [(a.shape[1], b.shape[1]) for a, b in pairs]
    outs = pl.pallas_call(
        functools.partial(mid_kernel, p, nw),
        out_shape=[jax.ShapeDtypeStruct((LEN, p.W), BF16)] + [jax.ShapeDtypeStruct(sh, BF16) for sh in shapes],
        in_specs=[any_space] + [vmem] * (2 * nw),
        out_specs=[vmem] + [any_space] * nw,
        scratch_shapes=[pltpu.VMEM(sh, BF16) for sh in shapes]
        + [dma((p.M, p.groups)), dma((p.P,))]
        + [dma((sh[0] // BQ,)) for sh in shapes],
        compiler_params=pltpu.CompilerParams(
            collective_id=2, has_side_effects=True, vmem_limit_bytes=VMEM_LIMIT
        ),
        name="mid",
    )(do_home, *[array for pair in pairs for array in pair])
    return outs[0], outs[1:]


def back_kernel(plan, nw, *refs):
    p = plan
    here = Place(p)
    s, c = here.s, here.c
    nz, near, width = here.rows, p.near, p.width
    (q, k, v, o, lse, preu, do_all, a_all, wcol, x, stream, par, small) = refs[:13]
    grads = refs[13 : 13 + nw]
    rest = refs[13 + nw :]
    input_grad, g_out, small_out = rest[:3]
    outs = rest[3 : 3 + nw]
    rest = rest[3 + nw :]
    (low, dk_acc, dv_acc, k_turn, da_own, da_out, da_in, da_side) = rest[:8]
    x_buf, stream_buf, buf_sem, a_buf, a_sem, gq = rest[-6:]
    rest = rest[:-6]
    da_home = input_grad
    (dw_out, dw_own, dw_in, dw_far, dw_end, small_acc, small_in, small_all) = rest[8:16]
    (dm_s, dm_r, dy_s, dy_r, dh_s, dh_r, wt_s, wt_r, wz_s, wz_r, wx_s, wx_r, wd_s, wd_r) = rest[16:30]
    (ss_s, ss_r, sa_s, sa_r) = rest[30:34]
    sums = GridSum(here, grads, outs, rest[34:])
    greet(sum_peers(here))
    sums.begin()
    small_acc[...] = small[...]
    prefix = preu[0:1, 0:1]

    def block_rows(i):
        return pl.ds(pl.multiple_of(i * BQ, BQ), BQ)

    def a_load(b):
        slot = lax.rem(b, 2)
        return pltpu.make_async_copy(
            a_all.at[:, pl.ds(pl.multiple_of(b * BQ, BQ), BQ)], a_buf.at[slot], a_sem.at[slot]
        )

    def weight_part(h, dst):
        def some(b, carry):
            slot = lax.rem(b, 2)

            @pl.when(b < p.D // BQ - 1)
            def _():
                a_load(b + 1).start()

            a_load(b).wait()
            dst[pl.ds(pl.multiple_of(b * BQ, BQ), BQ), :] = dot(a_buf[slot], low[h], 0, 0).astype(BF16)
            return carry

        lax.fori_loop(0, p.D // BQ, some, 0)

    def bias_part(h):
        folds = PAIR // width
        for row, lanes in ((0, slice(0, PAIR)), (1, slice(2 * PAIR, 3 * PAIR))):
            total = jnp.sum(low[h, :, lanes].astype(F32), axis=0, keepdims=True)
            for n in range(folds):
                at = (here.group * p.pairs + h) * folds + n
                small_acc[at, row : row + 1, 0:width] = total[:, n * width : (n + 1) * width]

    def to_twin_dw():
        return remote(dw_out, dw_in, wt_s.at[0], wt_r.at[0], s, here.twin)

    def pair_step(turn, carry):
        h = lax.rem(turn + 1 + here.side, 2)
        lanes = pl.ds(pl.multiple_of(h * PAIR, PAIR), PAIR)
        k_turn[...] = k[:, lanes].astype(F32).T.astype(BF16)
        dk_acc[...] = jnp.zeros_like(dk_acc)
        dv_acc[...] = jnp.zeros_like(dv_acc)

        def query_step(n, inner):
            j = lax.rem((here.unit - here.uq * near) * p.cpu + n // p.pieces, p.P)
            i = j * p.pieces + lax.rem(n, p.pieces)
            rows = block_rows(i)

            qp, dop, op = q[rows, lanes], do_all[rows, lanes], o[rows, lanes]
            turned = (dop.astype(F32) * op.astype(F32)).T
            pos = (lax.broadcasted_iota(jnp.int32, (1, BQ), 1) + i * BQ + 1).astype(F32)
            bound = jnp.maximum(pos, prefix)
            dq_t = []
            for e in (0, 1):
                lit = head_lanes(BQ, e)
                qe = jnp.where(lit, qp, jnp.zeros_like(qp))
                de = jnp.where(lit, dop, jnp.zeros_like(dop))
                level = lse[2 * h + e, 0:1, rows]
                inner_sum = jnp.sum(turned[e * HEAD : (e + 1) * HEAD], axis=0, keepdims=True)

                def key_step(start, total):
                    keys = slice(start, start + KEYS)
                    key_pos = (lax.broadcasted_iota(jnp.int32, (KEYS, 1), 0) + start).astype(F32)
                    logits = dot(k[keys, lanes], qe, 1, 1)
                    probs = jnp.where(key_pos < bound, jnp.exp2(logits * SCALE2 - level), 0.0)
                    slope = dot(v[keys, lanes], de, 1, 1)
                    dlog = (probs * (slope - inner_sum)).astype(BF16)
                    dv_acc[keys, :] += dot(probs.astype(BF16), de)
                    dk_acc[keys, :] += dot(dlog, qe)
                    return total + dot(k_turn[e * HEAD : (e + 1) * HEAD, keys], dlog)

                total = jnp.zeros((HEAD, BQ), F32)
                for start in range(0, LEN, KEYS):
                    total = key_step(start, total)
                dq_t.append(total)
            low[h, rows, 0:PAIR] = (jnp.concatenate(dq_t, axis=0).T * SCALE).astype(BF16)
            sums.slot(turn * p.nq + n)
            return inner

        lax.fori_loop(0, p.nq, query_step, 0)
        low[h, :, PAIR : 2 * PAIR] = (dk_acc[...] * SCALE).astype(BF16)
        low[h, :, 2 * PAIR :] = dv_acc[...].astype(BF16)
        bias_part(h)

        a_load(0).start()

        @pl.when(turn == 0)
        def _():
            weight_part(h, dw_out)
            to_twin_dw().start()

        return carry

    lax.fori_loop(0, p.pairs, pair_step, 0)

    half = p.D // CORES

    def block_of(n):
        lane = lax.rem(here.lane + 1 + n // (near * p.pieces), p.cpu)
        m = lax.rem(n, near * p.pieces)
        return ((m // p.pieces) * p.cpu + lane) * p.pieces + lax.rem(m, p.pieces)

    def da_half(rows, core):
        at = pl.ds(pl.multiple_of(core * half, half), half)
        total = dot(low[0, rows, :], wcol[0, at, :], 1, 1)
        for h in range(1, p.pairs):
            total = total + dot(low[h, rows, :], wcol[h, at, :], 1, 1)
        return total

    def da_mate(n, i):
        rows = block_rows(i)
        return remote(da_out.at[rows, :], da_in.at[rows, :], dm_s.at[n], dm_r.at[i], s, here.mate)

    far_blocks = (p.cpu - 1) * near * p.pieces
    count = p.pairs * p.nq

    def side_rows(i):
        return block_rows((i // p.pieces // p.cpu) * p.pieces + lax.rem(i, p.pieces))

    def da_over(n, i):
        return remote(da_own.at[block_rows(i), :], da_side.at[side_rows(i), :], dy_s.at[n], dy_r.at[i], here.beside, here.r)

    def da_first(n, carry):
        @pl.when(n < p.nq)
        def _():
            i = block_of(n)
            rows = block_rows(i)
            da_out[rows, :] = da_half(rows, 1 - c).astype(BF16)
            da_mate(n, i).start()
            da_own[rows, :] = da_half(rows, c).astype(BF16)

        @pl.when(n > 0)
        def _():
            last = jnp.maximum(n - 1, 0)
            i = block_of(last)
            rows = block_rows(i)
            da_mate(last, i).wait_recv()
            da_own[rows, :] = (da_own[rows, :].astype(F32) + da_in[rows, :].astype(F32)).astype(BF16)

            @pl.when(last < far_blocks)
            def _():
                da_over(last, i).start()

        sums.slot(count + n)
        return carry

    lax.fori_loop(0, p.nq + 1, da_first, 0)
    count = count + p.nq + 1

    own_pair = here.side
    weight_part(own_pair, dw_own)
    to_twin_dw().wait_recv()
    dw_own[...] = (dw_own[...].astype(F32) + dw_in[...].astype(F32)).astype(BF16)
    span = 2 * width

    def dw_rows(zr):
        return pl.ds(pl.multiple_of(zr * span, span), span)

    def dw_send(n):
        zr = lax.rem(here.row + 1 + n, nz)
        return remote(
            dw_own.at[dw_rows(zr), :], dw_far.at[here.row], wz_s.at[n], wz_r.at[here.row], 2 * zr + here.col, here.r
        )

    for n in range(nz - 1):
        dw_send(n).start()

    def da_back(n, i):
        rows = block_rows(i)
        home = here.uq * p.P + i // p.pieces
        piece = lax.rem(i, p.pieces)
        dst = da_home.at[here.um, block_rows(piece), pl.ds(pl.multiple_of(c * half, half), half)]
        src = da_own.at[rows, :]
        recv = dh_r.at[here.um, c, piece]
        away = jnp.logical_or(home != s, here.uc != c)
        return away, lambda: remote(src, dst, dh_s.at[n], recv, home, here.chip + here.uc), (src, dst, recv)

    def da_second(n, carry):
        i = block_of(n)
        rows = block_rows(i)
        da_over(n, i).wait_recv()
        da_own[rows, :] = (da_own[rows, :].astype(F32) + da_side[side_rows(i), :].astype(F32)).astype(BF16)
        launch(*da_back(n, i))
        sums.slot(count + n - far_blocks)
        return carry

    lax.fori_loop(far_blocks, p.nq, da_second, 0)
    count = count + p.nq - far_blocks

    def rest_of_sums(n, carry):
        sums.slot(n)
        return carry

    lax.fori_loop(count, max(count, sums.slots()), rest_of_sums, 0)
    sums.finish()

    dw_far[here.row] = dw_own[dw_rows(here.row), :]
    for n in range(nz - 1):
        off = lax.rem(here.row + 1 + n, nz)
        remote(dw_far.at[off], dw_far.at[off], wz_s.at[n], wz_r.at[off], s, here.r).wait_recv()
    total = dw_far[0].astype(F32)
    for n in range(1, nz):
        total = total + dw_far[n].astype(F32)
    dw_end[...] = total.astype(BF16)
    slot = here.group * p.pairs + here.side
    twin_chip = here.twin - c

    def dw_give(n):
        fy, fx, fc = n // 4, n // 2 % 2, n % 2
        col = here.col if fy == 0 else 1 - here.col
        core = c if fc == 0 else 1 - c
        src = dw_end.at[pl.ds(pl.multiple_of(col * width, width), width), :]
        dst = gq.at[slot]
        to = (2 * here.row + col, (here.chip if fx == 0 else twin_chip) + core)
        return src, dst, to

    for n in range(1, 8):
        src, dst, to = dw_give(n)
        remote(src, dst, wd_s.at[n], wd_r.at[slot], *to).start()
    gq[slot] = dw_end[pl.ds(pl.multiple_of(here.col * width, width), width), :]

    def token_loads(m, piece):
        at = pl.ds(pl.multiple_of(piece * BQ, BQ), BQ)
        return (
            pltpu.make_async_copy(x.at[m, at, :], x_buf, buf_sem.at[0]),
            pltpu.make_async_copy(stream.at[m, at, :], stream_buf, buf_sem.at[1]),
        )

    blocks = p.M * p.pieces
    gain = par[4:5, :].astype(F32)

    def loads_of(n):
        return token_loads(n // p.pieces, lax.rem(n, p.pieces))

    for copy in loads_of(0):
        copy.start()

    def norm_back(n, carry):
        gain_sum, shift_sum = carry
        m, piece = n // p.pieces, lax.rem(n, p.pieces)
        at = pl.ds(pl.multiple_of(piece * BQ, BQ), BQ)
        for core in range(CORES):
            dst = da_home.at[m, at, pl.ds(core * half, half)]
            pltpu.make_async_copy(dst, dst, dh_r.at[m, core, piece]).wait()
        for copy in loads_of(n):
            copy.wait()
        values = x_buf[...].astype(F32)
        dy = da_home[m, at, :].astype(F32)
        centre = values - jnp.mean(values, axis=-1, keepdims=True)
        spread = jnp.mean(centre * centre, axis=-1, keepdims=True)
        scale = lax.rsqrt(spread + EPS)
        wn = centre * scale
        e = dy * gain
        dw = scale * (e - jnp.mean(e, axis=-1, keepdims=True) - wn * jnp.mean(e * wn, axis=-1, keepdims=True))
        input_grad[m, at, :] = (stream_buf[...] + dw).astype(BF16)

        @pl.when(n + 1 < blocks)
        def _():
            for copy in loads_of(jnp.minimum(n + 1, blocks - 1)):
                copy.start()

        return (
            gain_sum + jnp.sum(dy * wn, axis=0, keepdims=True),
            shift_sum + jnp.sum(dy, axis=0, keepdims=True),
        )

    none = jnp.zeros((1, p.D), F32)
    gain_sum, shift_sum = lax.fori_loop(0, blocks, norm_back, (none, none))
    for n in range(p.S):
        lanes = slice(n * width, (n + 1) * width)
        small_acc[n, 4:5, 0:width] = gain_sum[:, lanes]
        small_acc[n, 8:9, 0:width] = shift_sum[:, lanes]

    def tiny(n):
        to = lax.rem(s + n, p.S)
        return remote(small_acc.at[to], small_in.at[n], ss_s.at[n], ss_r.at[n], to, here.r)

    for n in range(1, p.S):
        tiny(n).start()
    sums.twin_to_mate()
    total = small_acc[s]
    for n in range(1, p.S):
        tiny(n).wait_recv()
        total = total + small_in[n]
    small_all[here.r] = total

    def every(n):
        to = lax.rem(here.r + n, p.R)
        return remote(small_all.at[here.r], small_all.at[here.r], sa_s.at[n], sa_r.at[here.r], s, to)

    for n in range(1, p.R):
        every(n).start()
    for n in range(1, p.R):
        off = lax.rem(here.r + n, p.R)
        remote(small_all.at[0], small_all.at[off], sa_s.at[n], sa_r.at[off], s, here.r).wait_recv()
    total = small_all[0]
    for n in range(1, p.R):
        total = total + small_all[n]
    small_out[...] = total

    def da_sent(n, carry):
        i = block_of(n)
        da_mate(n, i).wait_send()

        @pl.when(n < far_blocks)
        def _():
            da_over(n, i).wait_send()

        @pl.when(n >= far_blocks)
        def _():
            sent(*da_back(n, i))

        return carry

    lax.fori_loop(0, p.nq, da_sent, 0)
    to_twin_dw().wait_send()
    for n in range(nz - 1):
        dw_send(n).wait_send()
    for n in range(1, 8):
        src, dst, to = dw_give(n)
        remote(src, dst, wd_s.at[n], wd_r.at[slot], *to).wait_send()
    for n in range(p.groups * p.pairs):

        @pl.when(n != slot)
        def _():
            remote(gq.at[n], gq.at[n], wd_s.at[0], wd_r.at[n], s, here.r).wait_recv()

        for k in range(3):
            at = k * p.D + n * PAIR
            g_out[:, at : at + PAIR] = gq[n, :, k * PAIR : (k + 1) * PAIR]

    for n in range(1, p.S):
        tiny(n).wait_send()
    for n in range(1, p.R):
        every(n).wait_send()
    sums.drain()


def back(plan, units, small, grads):
    p = plan
    nw = len(grads)
    nz = p.S // 2
    planes = p.R // CORES
    split = [split_rows(p, grad) for grad in grads]
    shapes = [h.shape[2:] for h in split]
    any_space = pl.BlockSpec(memory_space=pl.ANY)
    vmem = pl.BlockSpec(memory_space=pltpu.VMEM)
    dma = pltpu.SemaphoreType.DMA
    shape = jax.ShapeDtypeStruct
    half = p.D // CORES
    outs = pl.pallas_call(
        functools.partial(back_kernel, p, nw),
        out_shape=[
            shape((p.M, p.T, p.D), BF16),
            shape((p.width, 3 * p.D), BF16),
            shape(small.shape[1:], F32),
        ]
        + [shape((CORES,) + sh, BF16) for sh in shapes],
        in_specs=[vmem] * 7 + [any_space] + [vmem] + [any_space] * 2 + [vmem] * 2 + [any_space] * nw,
        out_specs=[vmem] * (3 + nw),
        scratch_shapes=[
            pltpu.VMEM((p.pairs, LEN, 3 * PAIR), BF16),
            pltpu.VMEM((LEN, PAIR), F32),
            pltpu.VMEM((LEN, PAIR), F32),
            pltpu.VMEM((PAIR, LEN), BF16),
            pltpu.VMEM((LEN, half), BF16),
            pltpu.VMEM((LEN, half), BF16),
            pltpu.VMEM((LEN, half), BF16),
            pltpu.VMEM((p.near * p.T, half), BF16),
            pltpu.VMEM((p.D, 3 * PAIR), BF16),
            pltpu.VMEM((p.D, 3 * PAIR), BF16),
            pltpu.VMEM((p.D, 3 * PAIR), BF16),
            pltpu.VMEM((nz, 2 * p.width, 3 * PAIR), BF16),
            pltpu.VMEM((2 * p.width, 3 * PAIR), BF16),
            pltpu.VMEM(small.shape, F32),
            pltpu.VMEM(small.shape, F32),
            pltpu.VMEM((p.R,) + small.shape[1:], F32),
            dma((p.nq,)), dma((p.nq,)), dma((p.nq,)), dma((p.nq,)),
            dma((p.nq,)), dma((p.M, CORES, p.pieces)),
            dma((1,)), dma((1,)), dma((nz,)), dma((nz,)), dma((planes,)), dma((planes,)), dma((8,)), dma((8,)),
            dma((p.S,)), dma((p.S,)), dma((p.R,)), dma((p.R,)),
        ]
        + GridSum.scratch(p, shapes)
        + [pltpu.VMEM((BQ, p.D), BF16), pltpu.VMEM((BQ, p.D), F32), dma((2,))]
        + [pltpu.VMEM((2, LEN, BQ), BF16), dma((2,))]
        + [pltpu.VMEM((p.groups * p.pairs, p.width, 3 * PAIR), BF16)],
        compiler_params=pltpu.CompilerParams(
            collective_id=1, has_side_effects=True, vmem_limit_bytes=VMEM_LIMIT
        ),
        name="back",
    )(*units, small, *split)
    return outs[0], outs[1].astype(F32), outs[2], [whole_shard(part) for part in outs[3:]]


def per_device(
    sizes,
    inputs,
    prefix,
    qkv_weight,
    qv_bias,
    out_weight,
    branch_bias,
    up_weight,
    up_bias,
    down_weight,
    norm_gain,
    norm_bias,
    cotangent,
):
    p = Plan(sizes, (inputs.shape[0], 1, inputs.shape[2], inputs.shape[3]))
    tokens_all = p.M * p.T
    x = inputs[:, 0]
    width = p.D // p.S
    spare = max(128 - width, 0)
    small_in = (qv_bias, branch_bias, norm_gain, norm_bias, up_bias.reshape(-1, width))
    (wo, wu, wd, parf, _, q, k, v, o, lse, preu, o_home, a_unit, w_unit) = fore(
        p, x, small_in, prefix[:, 0], qkv_weight, (out_weight, up_weight, down_weight)
    )
    par32 = parf.astype(F32)
    bias_branch = par32[2:4]
    gains, shifts = par32[4:8], par32[8:12]
    bias_up = par32[12:].reshape(-1, p.S, width).transpose(1, 0, 2).reshape(-1)

    tokens = x.reshape(tokens_all, p.D).astype(F32)
    upstream = cotangent[:, 0].reshape(tokens_all, p.D).astype(F32)
    mixed_low = o_home.reshape(tokens_all, p.D)
    branch = dot(mixed_low, wo) + bias_branch[0]
    side, pull_side = jax.vjp(normed, branch, gains[1:2], shifts[1:2])
    stream = tokens + side
    normal_mid, pull_mid = jax.vjp(normed, stream, gains[2:3], shifts[2:3])
    middle_low = normal_mid.astype(BF16)
    upper = dot(middle_low, wu) + bias_up
    below = 0.5 * (1.0 + lax.erf(upper * math.sqrt(0.5)))
    slope = below + upper * jnp.exp(-0.5 * upper * upper) * (1.0 / math.sqrt(2.0 * math.pi))
    active_low, slope = lax.optimization_barrier(((upper * below).astype(BF16), slope))
    lower = dot(active_low, wd) + bias_branch[1]
    closing, pull_close = jax.vjp(normed, lower, gains[3:4], shifts[3:4])
    output = (stream + closing).astype(BF16)
    grad_lower, gain_three, shift_three = pull_close(upstream)
    lower_low = grad_lower.astype(BF16)
    grad_active = dot(lower_low, wd, 1, 1)
    upper_low = (grad_active * slope).astype(BF16)
    grad_middle = dot(upper_low, wu, 1, 1)
    grad_mid_in, gain_two, shift_two = pull_mid(grad_middle)
    grad_stream = grad_mid_in + upstream
    grad_branch, gain_one, shift_one = pull_side(grad_stream)
    branch_low = grad_branch.astype(BF16)
    grad_mixed = dot(branch_low, wo, 1, 1).astype(BF16)

    by_token = (p.M, p.T, p.D)
    do_unit, grads = mid(
        p,
        grad_mixed.reshape(by_token),
        ((active_low, lower_low), (middle_low, upper_low), (mixed_low, branch_low)),
    )

    def column_sum(values):
        return jnp.sum(values.astype(F32), axis=0, keepdims=True)

    du_sum = column_sum(upper_low).reshape(p.S, -1, width).transpose(1, 0, 2).reshape(-1, p.D)
    none = jnp.zeros((1, p.D), F32)
    small = jnp.concatenate(
        [
            none, none, column_sum(branch_low), column_sum(lower_low),
            none, gain_one, gain_two, gain_three,
            none, shift_one, shift_two, shift_three,
            du_sum,
        ], axis=0,
    )
    small = jnp.pad(small.reshape(-1, p.S, width).transpose(1, 0, 2), ((0, 0), (0, 0), (0, spare)))
    input_grad, sum_qkv, tiny, (sum_down, sum_up, sum_out) = back(
        p,
        (
            q, k, v, o, lse, preu, do_unit, a_unit, w_unit,
            x, grad_stream.reshape(by_token), parf,
        ),
        small, grads,
    )
    tiny = tiny[:, :width]
    shaped = (p.M, 1, p.T, p.D)
    return (
        output.reshape(shaped),
        input_grad.reshape(shaped),
        sum_qkv,
        tiny[0:2],
        sum_out,
        tiny[2:4],
        sum_up,
        tiny[12:].reshape(-1),
        sum_down,
        tiny[4:8],
        tiny[8:12],
    )


def solution(mesh):
    sizes = {name: mesh.shape[name] for name in ("shard", "replica")}
    placed = (
        P(None, "replica", "shard", None),
        P(None, "replica", None),
        P("shard", None),
        P(None, "shard"),
        P("shard", None),
        P(None, "shard"),
        P("shard", None),
        P("shard"),
        P("shard", None),
        P(None, "shard"),
        P(None, "shard"),
        P(None, "replica", "shard", None),
    )
    return jax.shard_map(
        functools.partial(per_device, sizes),
        mesh=mesh,
        in_specs=placed,
        out_specs=(
            P(None, "replica", "shard", None),
            P(None, "replica", "shard", None),
            P("shard", None),
            P(None, "shard"),
            P("shard", None),
            P(None, "shard"),
            P("shard", None),
            P("shard"),
            P("shard", None),
            P(None, "shard"),
            P(None, "shard"),
        ),
        check_vma=False,
    )
```

```python
import functools
import math

import jax
import jax.numpy as jnp
from jax import lax
from jax.experimental import pallas as pl
from jax.experimental.pallas import tpu as pltpu
from jax.sharding import PartitionSpec as P

HEAD = 64
LEN = 2048
CORES = 2
PAIR = 2 * HEAD
BQ = 256
EPS = 1e-05
MASKED = -1e30
SCALE = HEAD ** (-0.5)
SCALE2 = SCALE * math.log2(math.e)
F32 = jnp.float32
BF16 = jnp.bfloat16
MESH = pl.DeviceIdType.MESH
VMEM_LIMIT = 66_000_000
LAG = 2
KEYS = 512
SIDE_FIRST = (True, False, False)
SUM_LAG = 5
CADENCE = 1
COLUMN_FIRST = (False, True, False)
START = 1
EARLY = 1


class Plan:
    def __init__(self, mesh_shape, inputs_shape):
        self.S = mesh_shape["shard"]
        self.R = mesh_shape["replica"]
        self.M, _, self.T, self.D = inputs_shape
        self.Q = self.T * self.S // LEN
        self.P = LEN // self.T
        self.U = self.M * self.Q * CORES
        self.cpu = self.S // self.U
        self.heads = self.D // HEAD
        self.W = self.D // (CORES * self.cpu)
        self.pairs = self.W // PAIR
        self.groups = CORES * self.cpu
        self.pieces = self.T // BQ
        self.nq = LEN // BQ
        self.near = self.P // self.cpu
        self.width = self.D // self.S
        assert self.cpu == 2 and self.pairs == 2 and self.T % BQ == 0 and LEN % self.T == 0


class Place:
    def __init__(self, plan):
        self.p = plan
        self.s = lax.axis_index("shard")
        self.r = lax.axis_index("replica")
        self.c = lax.rem(self.r, CORES)
        self.chip = self.r - self.c
        self.mate = self.chip + (1 - self.c)
        self.unit = self.s // plan.cpu
        self.lane = lax.rem(self.s, plan.cpu)
        self.group = self.c * plan.cpu + self.lane
        self.uc = lax.rem(self.unit, CORES)
        self.um = lax.rem(self.unit // CORES, plan.M)
        self.uq = self.unit // (CORES * plan.M)
        self.ring = self.to_ring(self.s)
        self.plane = self.r // CORES
        self.side = lax.rem(self.plane, 2)
        self.twin = self.r + CORES * (1 - 2 * self.side)
        self.row = self.s // 2
        self.col = lax.rem(self.s, 2)
        self.beside = 2 * self.row + 1 - self.col
        self.rows = plan.S // 2

    def unit_of(self, c, m, s):
        return ((s // self.p.P) * self.p.M + m) * CORES + c

    def to_ring(self, s):
        half = self.p.S // 2
        row, col = s // 2, lax.rem(s, 2)
        return row + col * (2 * half - 1 - 2 * row)

    def from_ring(self, i):
        n = self.p.S
        return jnp.where(i < n // 2, 2 * i, 2 * (n - 1 - i) + 1)


def remote(src, dst, send, recv, s, r):
    return pltpu.make_async_remote_copy(
        src_ref=src, dst_ref=dst, send_sem=send, recv_sem=recv, device_id=(s, r), device_id_type=MESH
    )


def launch(away, far, near):
    @pl.when(away)
    def _():
        far().start()

    @pl.when(jnp.logical_not(away))
    def _():
        pltpu.make_async_copy(*near).start()


def sent(away, far, near):
    @pl.when(away)
    def _():
        far().wait_send()


def greet(peers):
    barrier = pltpu.get_barrier_semaphore()
    for s, r in peers:
        pl.semaphore_signal(barrier, inc=1, device_id=(s, r), device_id_type=MESH)
    pl.semaphore_wait(barrier, len(peers))


def plane_peers(here):
    n = here.p.S * CORES
    own = here.s * CORES + here.c
    out = []
    for k in range(1, n):
        i = lax.rem(own + k, n)
        out.append((i // CORES, here.chip + lax.rem(i, CORES)))
    return out


def normed(values, gain, shift):
    centre = values - jnp.mean(values, axis=-1, keepdims=True)
    spread = jnp.mean(centre * centre, axis=-1, keepdims=True)
    return centre * lax.rsqrt(spread + EPS) * gain + shift


def dot(a, b, ca=1, cb=0):
    return lax.dot_general(a, b, (((ca,), (cb,)), ((), ())), preferred_element_type=F32)


def head_lanes(rows, which):
    lane = lax.broadcasted_iota(jnp.int32, (rows, PAIR), 1)
    return (lane < HEAD) if which == 0 else (lane >= HEAD)


def fore_kernel(
    plan, x, biases, branches, gains, shifts, ups, prefixes, wq_in, wo, wu, wd,
    wof, wuf, wdf, parf, q_out, k_out, v_out, o_out, lse_out, preu, oh, a_all, wcol,
    ah, par, pre, wq, parg, pre2,
    par_ss, par_rs, pre_sem, loc_sem, a_ss, a_rs, af_ss, z_ss, z_rs, wa_ss, wa_rs, wb_ss, wb_rs, wm_ss, wm_rs,
    o_ss, o_rs, q_ss, q_rs, qt_ss, qt_rs, q_loc,
):
    p = plan
    here = Place(p)
    s, c = here.s, here.c
    mine, full = (wo, wu, wd), (wof, wuf, wdf)
    nw = len(mine)
    first = COLUMN_FIRST
    greet(plane_peers(here) + [(s, here.twin)])

    par[...] = jnp.zeros_like(par)
    at = 0
    for part in (biases, branches, gains, shifts, ups):
        par[at : at + part.shape[0], 0 : part.shape[1]] = part[...]
        at += part.shape[0]
    pre[...] = jnp.zeros_like(pre)
    for m in range(p.M):
        for n in range(p.Q):
            pre[m * p.Q + n : m * p.Q + n + 1, :] = jnp.full((1, 128), prefixes[m, n].astype(F32))
    for g in range(p.groups):
        for h in range(p.pairs):
            for k in range(3):
                at = k * p.D + g * p.W + h * PAIR
                wq[g, h, :, k * PAIR : (k + 1) * PAIR] = wq_in[:, at : at + PAIR]
    parg[s] = par[...]
    small = []
    for k in range(1, p.S):
        to = lax.rem(s + k, p.S)
        small.append(remote(par, parg.at[s], par_ss.at[k], par_rs.at[k], to, here.r))
        small[-1].start()
    swap = remote(pre, pre2, pre_sem.at[0], pre_sem.at[1], s, here.mate)
    swap.start()

    z, nz = here.row, here.rows

    def where(w, zr, fa, fb, core):
        fy, fx = (fa, fb) if first[w] else (fb, fa)
        col = here.col if fy == 0 else 1 - here.col
        side = here.side if fx == 0 else 1 - here.side
        n, width = mine[w].shape[0], mine[w].shape[1] // 2
        rows = pl.ds(pl.multiple_of((2 * zr + col) * n + core * (n // 2), n // 2), n // 2)
        return full[w].at[rows, pl.ds(pl.multiple_of(side * width, width), width)]

    def origin(w, fa):
        n, width = mine[w].shape[0], mine[w].shape[1] // 2
        side = here.side if fa == 0 else 1 - here.side
        rows = pl.ds(pl.multiple_of(c * (n // 2), n // 2), n // 2)
        return mine[w].at[rows, pl.ds(pl.multiple_of(side * width, width), width)]

    def peer(w, second):
        return (here.beside, here.r) if first[w] == (second == 0) else (s, here.twin)

    def z_send(w, d, k):
        sign = 1 - 2 * d
        part = where(w, z - sign * (k - 1), 0, 0, c)
        src = origin(w, 0) if isinstance(k, int) and k == 1 else part
        return remote(src, part, z_ss.at[w, d, k - 1], z_rs.at[w, d, k - 1], s + 2 * sign, here.r)

    def z_came(w, d, k):
        sign = 1 - 2 * d
        part = where(w, z - sign * k, 0, 0, c)
        return remote(part, part, z_ss.at[w, d, k - 1], z_rs.at[w, d, k - 1], s, here.r)

    def to_first(w, zr, src=None):
        part = where(w, zr, 0, 0, c)
        return remote(part if src is None else src, part, wa_ss.at[w, zr], wa_rs.at[w, zr], *peer(w, 0))

    def to_second(w, fa, zr, src=None):
        part = where(w, zr, fa, 0, c)
        return remote(part if src is None else src, part, wb_ss.at[w, fa, zr], wb_rs.at[w, fa, zr], *peer(w, 1))

    def to_mate(w, fa, fb, zr, core):
        part = where(w, zr, fa, fb, core)
        at = 2 * fa + fb
        return remote(part, part, wm_ss.at[w, at, zr], wm_rs.at[w, at, zr], s, here.mate)

    def first_came(w, zr):
        part = where(w, zr, 1, 0, c)
        return remote(part, part, wa_ss.at[w, zr], wa_rs.at[w, zr], s, here.r)

    def second_came(w, fa, zr):
        part = where(w, zr, fa, 1, c)
        return remote(part, part, wb_ss.at[w, fa, zr], wb_rs.at[w, fa, zr], s, here.r)

    def on_grid(d, k):
        return z >= k if d == 0 else z + k < nz

    def can_send(d):
        return z < nz - 1 if d == 0 else z > 0

    def gather_rows(w):
        for d in (0, 1):

            @pl.when(can_send(d))
            def _():
                z_send(w, d, 1).start()

    def gather_near(w):
        if first[w]:
            to_first(w, z, origin(w, 0)).start()
        else:
            to_second(w, 0, z, origin(w, 0)).start()
            to_second(w, 1, z, origin(w, 1)).start()

    def gather_slot(w, k, lag):
        for d in (0, 1):
            sign = 1 - 2 * d

            @pl.when(jnp.logical_and(k >= 1, on_grid(d, k)))
            def _():
                at = jnp.maximum(k, 1)
                z_came(w, d, at).wait_recv()
                zr = z - sign * at

                @pl.when(can_send(d))
                def _():
                    z_send(w, d, at + 1).start()

                to_first(w, zr).start()
                to_second(w, 0, zr).start()
                to_mate(w, 0, 0, zr, c).start()

        def at_distance(j, least, body):
            for d in (0, 1):
                ok = jnp.logical_and(j >= max(least, d), on_grid(d, j))

                @pl.when(ok)
                def _():
                    body(z - (1 - 2 * d) * jnp.maximum(j, 0))

        def after_first(zr):
            first_came(w, zr).wait_recv()
            to_second(w, 1, zr).start()
            to_mate(w, 1, 0, zr, c).start()

        at_distance(k - 1, 0 if first[w] else 1, after_first)

        def after_second(fa):
            def body(zr):
                second_came(w, fa, zr).wait_recv()
                to_mate(w, fa, 1, zr, c).start()

            return body

        at_distance(k - 1 - lag, 1 if first[w] else 0, after_second(0))
        at_distance(k - 2 - lag, 0, after_second(1))

    def mate_pieces(w, zr, act):
        other = zr != z

        @pl.when(other)
        def _():
            act(0, 0)

        if first[w]:

            @pl.when(other)
            def _():
                act(0, 1)

            act(1, 0)
        else:

            @pl.when(other)
            def _():
                act(1, 0)

            act(0, 1)
        act(1, 1)

    def gather_wait(w):
        def one(zr, carry):
            mate_pieces(w, zr, lambda fa, fb: to_mate(w, fa, fb, zr, 1 - c).wait_recv())
            return carry

        lax.fori_loop(0, nz, one, 0)

    def gather_drain(w):
        def one(zr, carry):
            mate_pieces(w, zr, lambda fa, fb: to_mate(w, fa, fb, zr, c).wait_send())
            if first[w]:
                to_first(w, zr).wait_send()

                @pl.when(zr != z)
                def _():
                    to_second(w, 0, zr).wait_send()
            else:

                @pl.when(zr != z)
                def _():
                    to_first(w, zr).wait_send()

                to_second(w, 0, zr).wait_send()
            to_second(w, 1, zr).wait_send()
            for d in (0, 1):
                reach = zr <= z if d == 0 else zr < nz - z

                @pl.when(jnp.logical_and(can_send(d), reach))
                def _():
                    z_send(w, d, zr + 1).wait_send()

            return carry

        lax.fori_loop(0, nz, one, 0)

    nq_rows = wq.shape[2]
    half_rows = nq_rows // 2

    def q_rows(k, side):
        return pl.ds(pl.multiple_of(k * nq_rows + side * half_rows, half_rows), half_rows)

    def q_send(k):
        to = lax.rem(s + k, p.S)
        group = c * p.cpu + lax.rem(to, p.cpu)
        rows = pl.ds(pl.multiple_of(here.side * half_rows, half_rows), half_rows)
        src = wq.at[group, :, rows, :]
        return remote(src, wcol.at[:, q_rows(s, here.side), :], q_ss.at[k], q_rs.at[s], to, here.r)

    def q_twin(k, side):
        part = wcol.at[:, q_rows(k, side), :]
        return remote(part, part, qt_ss.at[k], qt_rs.at[k], s, here.twin)

    def q_from(k):
        return lax.rem(s + p.S - k, p.S)

    for k in range(1, p.S):
        q_send(k).start()
    for w in range(nw):
        gather_near(w)
    q_own = pltpu.make_async_copy(
        wq.at[here.group], wcol.at[:, pl.ds(pl.multiple_of(s * nq_rows, nq_rows), nq_rows), :], q_loc.at[0]
    )
    q_own.start()
    local = []
    for w in range(nw):
        n = mine[w].shape[0]
        local.append(
            pltpu.make_async_copy(mine[w], full[w].at[pl.ds(pl.multiple_of(s * n, n), n), :], loc_sem.at[w])
        )
        local[-1].start()

    for k in range(1, p.S):
        small[k - 1].wait_recv()
    parf[...] = jnp.concatenate([parg[k][:, : p.D // p.S] for k in range(p.S)], axis=1)
    gain = parf[4:5, :].astype(F32)
    shift = parf[8:9, :].astype(F32)
    rows_here = pl.ds(pl.multiple_of(lax.rem(s, p.P) * p.T, p.T), p.T)

    def first_hop(m):
        to = here.unit_of(c, m, s) * p.cpu + here.lane
        far = lambda: remote(ah.at[m], a_all.at[rows_here, :], a_ss.at[m], a_rs.at[lax.rem(s, p.P)], to, here.r)
        return to, far

    for m in range(p.M):
        ah[m] = normed(x[m].astype(F32), gain, shift).astype(BF16)
        to, far = first_hop(m)

        @pl.when(to != s)
        def _():
            far().start()

        @pl.when(to == s)
        def _():
            a_all[rows_here, :] = ah[m]

    primary = c == here.uc

    def a_rows(j):
        return pl.ds(pl.multiple_of(j * p.T, p.T), p.T)

    def a_forward(j, k):
        part = a_all.at[a_rows(j), :]
        if k == 0:
            return remote(part, part, af_ss.at[j, 0], a_rs.at[j], s, here.mate)
        to = here.unit * p.cpu + lax.rem(here.lane + k, p.cpu)
        return remote(part, part, af_ss.at[j, k], a_rs.at[j], to, here.r)

    def a_wait(j):
        part = a_all.at[a_rows(j), :]
        remote(part, part, af_ss.at[j, 0], a_rs.at[j], s, here.mate).wait_recv()

    near = p.near

    zi = here.unit - here.uq * near

    def a_at(k, body):
        for d in (0, 1):
            if k or not d:
                ok = zi >= k if d == 0 else zi + k < near

                @pl.when(jnp.logical_and(primary, ok))
                def _():
                    body(zi - (1 - 2 * d) * k)

    def a_near(jj):
        j = jj * p.cpu + here.lane

        @pl.when(here.uq * p.P + j != s)
        def _():
            a_wait(j)

        for k in list(range(1, p.cpu)) + [0]:
            a_forward(j, k).start()

    def a_far(jj):
        for k in range(1, p.cpu):
            j = jj * p.cpu + lax.rem(here.lane + k, p.cpu)
            a_wait(j)
            a_forward(j, 0).start()

    each = -(-(p.S - 1) // near)
    for k in range(near + 1):
        if k < near:
            for n in range(1 + k * each, min(1 + (k + 1) * each, p.S)):
                part = wcol.at[:, q_rows(q_from(n), here.side), :]
                remote(part, part, q_ss.at[n], q_rs.at[q_from(n)], s, here.r).wait_recv()
                q_twin(q_from(n), here.side).start()
            a_at(k, a_near)
        if k == START:
            for w in range(nw):
                gather_rows(w)
        if k >= 1:
            a_at(k - 1, a_far)
        if k >= near + 1 - EARLY:
            for w in range(nw):
                gather_slot(w, k - (near - EARLY), LAG)

    @pl.when(jnp.logical_not(primary))
    def _():
        for j in range(p.P):
            a_wait(j)

    swap.wait_recv()
    pre2[...] = jnp.where(primary, pre[...], pre2[...])
    row = here.um * p.Q + here.uq
    preu[...] = jnp.broadcast_to(pre2[pl.ds(row, 1), :], preu.shape)

    for n in range(1, p.S):
        q_twin(q_from(n), 1 - here.side).wait_recv()
    q_own.wait()
    own = pl.ds(pl.multiple_of(here.group * p.W, PAIR), p.W)
    q_bias = parf[0:1, own].astype(F32)
    v_bias = parf[1:2, own].astype(F32)

    def project(i, carry):
        rows = pl.ds(pl.multiple_of(i * BQ, BQ), BQ)
        part = a_all[rows, :]
        for h in range(p.pairs):
            lanes = slice(h * PAIR, (h + 1) * PAIR)
            got = dot(part, wcol[h])
            q_out[rows, lanes] = (got[:, :PAIR] + q_bias[:, lanes]).astype(BF16)
            k_out[rows, lanes] = got[:, PAIR : 2 * PAIR].astype(BF16)
            v_out[rows, lanes] = (got[:, 2 * PAIR :] + v_bias[:, lanes]).astype(BF16)
        return carry

    lax.fori_loop(0, p.nq, project, 0)

    prefix = preu[0:1, 0:1]
    slots = nz + 1 + LAG - EARLY
    per = -(-slots // p.nq)

    def o_copy(i):
        rows = pl.ds(pl.multiple_of(i * BQ, BQ), BQ)
        home = here.uq * p.P + i // p.pieces
        piece = lax.rem(i, p.pieces)
        there = pl.ds(pl.multiple_of(piece * BQ, BQ), BQ)
        src = o_out.at[rows, :]
        dst = oh.at[here.um, there, own]
        away = jnp.logical_or(home != s, here.uc != c)
        recv = o_rs.at[here.um, here.group, piece]
        return away, lambda: remote(src, dst, o_ss.at[i], recv, home, here.chip + here.uc), (src, dst, recv)

    def attend(i, carry):
        rows = pl.ds(pl.multiple_of(i * BQ, BQ), BQ)
        row_pos = (lax.broadcasted_iota(jnp.int32, (BQ, 1), 0) + i * BQ + 1).astype(F32)
        bound = jnp.maximum(row_pos, prefix)
        key_pos = lax.broadcasted_iota(jnp.int32, (1, LEN), 1).astype(F32)
        seen = key_pos < bound

        def pair_step(h, inner):
            lanes = pl.ds(pl.multiple_of(h * PAIR, PAIR), PAIR)
            qp, kp, vp = q_out[rows, lanes], k_out[:, lanes], v_out[:, lanes]
            halves = []
            for e in (0, 1):
                logits = dot(jnp.where(head_lanes(BQ, e), qp, jnp.zeros_like(qp)), kp, 1, 1)
                logits = jnp.where(seen, logits, MASKED)
                top = jnp.max(logits, axis=1, keepdims=True)
                powers = jnp.exp2((logits - top) * SCALE2)
                total = jnp.sum(powers, axis=1, keepdims=True)
                halves.append(dot(powers.astype(BF16), vp) * (1.0 / total))
                level = top * SCALE2 + jnp.log2(total)
                turned = jnp.broadcast_to(level, (BQ, 128)).T
                lse_out[2 * h + e, :, pl.ds(pl.multiple_of(i * BQ, BQ), BQ)] = turned[0:8]
            o_out[rows, lanes] = jnp.where(head_lanes(BQ, 0), halves[0], halves[1]).astype(BF16)
            return inner

        lax.fori_loop(0, p.pairs, pair_step, 0)
        launch(*o_copy(i))

        for extra in range(per):
            for w in range(nw):
                gather_slot(w, i * per + extra + 1 + EARLY, LAG)

        return carry

    lax.fori_loop(0, p.nq, attend, 0)

    for m in range(p.M):
        for g in range(p.groups):
            for piece in range(p.pieces):
                src = o_out.at[pl.ds(0, BQ), :]
                dst = oh.at[m, pl.ds(piece * BQ, BQ), pl.ds(g * p.W, p.W)]
                pltpu.make_async_copy(src, dst, o_rs.at[m, g, piece]).wait()

    def o_sent(i, carry):
        sent(*o_copy(i))
        return carry

    lax.fori_loop(0, p.nq, o_sent, 0)
    for copy in small:
        copy.wait_send()
    swap.wait_send()
    for copy in local:
        copy.wait()
    for n in range(1, p.S):
        q_send(n).wait_send()
        q_twin(q_from(n), here.side).wait_send()
    for m in range(p.M):
        to, far = first_hop(m)

        @pl.when(to != s)
        def _():
            far().wait_send()

    @pl.when(primary)
    def _():
        for jj in range(near):
            for k in range(p.cpu):
                a_forward(jj * p.cpu + here.lane, k).wait_send()
            for k in range(1, p.cpu):
                a_forward(jj * p.cpu + lax.rem(here.lane + k, p.cpu), 0).wait_send()

    for w in range(nw):
        gather_wait(w)
        gather_drain(w)


def fore(plan, x, small, prefixes, qkv, weights):
    p = plan
    par = (sum(part.shape[0] for part in small), max(p.width, 128))
    nz = p.S // 2
    nw = len(weights)
    any_space = pl.BlockSpec(memory_space=pl.ANY)
    vmem = pl.BlockSpec(memory_space=pltpu.VMEM)
    shape = jax.ShapeDtypeStruct
    out_shape = (
        [shape((w.shape[0] * p.S, w.shape[1]), BF16) for w in weights]
        + [shape((par[0], p.D), BF16)]
        + [shape((LEN, p.W), BF16)] * 4
        + [shape((2 * p.pairs, 8, LEN), F32), shape((8, 128), F32), shape((p.M, p.T, p.D), BF16)]
        + [shape((LEN, p.D), BF16), shape((p.pairs, p.D, 3 * PAIR), BF16)]
    )
    dma = pltpu.SemaphoreType.DMA
    return pl.pallas_call(
        functools.partial(fore_kernel, p),
        out_shape=out_shape,
        in_specs=[vmem] * 6 + [pl.BlockSpec(memory_space=pltpu.SMEM)] + [vmem] * (1 + nw),
        out_specs=[any_space] * nw + [vmem] * 10,
        scratch_shapes=[
            pltpu.VMEM((p.M, p.T, p.D), BF16),
            pltpu.VMEM(par, BF16),
            pltpu.VMEM((8, 128), F32),
            pltpu.VMEM((p.groups, p.pairs, qkv.shape[0], 3 * PAIR), BF16),
            pltpu.VMEM((p.S,) + par, BF16),
            pltpu.VMEM((8, 128), F32),
            dma((p.S,)), dma((p.S,)), dma((2,)), dma((nw,)),
            dma((p.M,)), dma((p.P,)), dma((p.P, p.cpu)),
            dma((nw, 2, nz)), dma((nw, 2, nz)), dma((nw, nz)), dma((nw, nz)),
            dma((nw, 2, nz)), dma((nw, 2, nz)), dma((nw, 4, nz)), dma((nw, 4, nz)),
            dma((p.nq,)), dma((p.M, p.groups, p.pieces)),
            dma((p.S,)), dma((p.S,)), dma((p.S,)), dma((p.S,)), dma((1,)),
        ],
        compiler_params=pltpu.CompilerParams(
            collective_id=0, has_side_effects=True, vmem_limit_bytes=VMEM_LIMIT
        ),
        name="fore",
    )(x, *small, prefixes, qkv, *weights)


class GridSum:
    def __init__(self, here, grads, outs, refs):
        self.here, self.grads, self.outs = here, grads, outs
        self.nw = nw = len(grads)
        self.nz = here.rows
        self.planes = here.p.R // CORES
        self.own, self.acc, self.one, self.two, self.far = (refs[k * nw : (k + 1) * nw] for k in range(5))
        (self.ld, self.m_s, self.m_r, self.a_s, self.a_r, self.b_s, self.b_r, self.z_s, self.z_r) = refs[5 * nw : 5 * nw + 9]
        (self.x_s, self.x_r, self.t_s, self.t_r, self.f_s, self.f_r) = refs[5 * nw + 9 :]
        self.side_first = SIDE_FIRST

    @staticmethod
    def scratch(plan, shapes):
        nw = len(shapes)
        planes = plan.R // CORES
        nz = plan.S // 2
        dma = pltpu.SemaphoreType.DMA
        return (
            [pltpu.VMEM((2,) + sh, BF16) for sh in shapes]
            + [pltpu.VMEM((plan.S,) + sh, BF16) for sh in shapes]
            + [
                pltpu.VMEM((plan.S, sh[0], sh[1] // 2) if sf else (nz,) + sh, BF16)
                for sh, sf in zip(shapes, SIDE_FIRST)
            ]
            + [pltpu.VMEM((nz, sh[0], sh[1] // 2), BF16) for sh in shapes]
            + [pltpu.VMEM((max(nz, planes // 2), sh[0], sh[1] // 2), BF16) for sh in shapes]
            + [dma((nw,))]
            + [dma((nw, nz))] * 8
            + [dma((nw, planes))] * 2
            + [dma((nw,))] * 2
            + [dma((nw, 2))] * 2
        )

    @staticmethod
    def count(nw):
        return 5 * nw + 15

    def zr(self, k):
        return lax.rem(self.here.row + 1 + k, self.nz)

    def half(self, w, side):
        n = self.acc[w].shape[2] // 2
        return pl.ds(pl.multiple_of(side * n, n), n)

    def load(self, w, k):
        src = self.grads[w].at[pl.ds(2 * self.zr(k), 2), self.here.c]
        return pltpu.make_async_copy(src, self.own[w], self.ld.at[w])

    def swap(self, w, k):
        here = self.here
        pair = pl.ds(2 * self.zr(k), 2)
        return remote(
            self.grads[w].at[pair, 1 - here.c], self.acc[w].at[pair], self.m_s.at[w, k], self.m_r.at[w, k], here.s, here.mate
        )

    def first(self, w, k):
        here, zr = self.here, self.zr(k)
        if self.side_first[w]:
            pair = pl.ds(2 * zr, 2)
            src = self.acc[w].at[pair, :, self.half(w, 1 - here.side)]
            return remote(src, self.one[w].at[pair], self.a_s.at[w, k], self.a_r.at[w, k], here.s, here.twin)
        src = self.acc[w].at[2 * zr + 1 - here.col]
        return remote(src, self.one[w].at[zr], self.a_s.at[w, k], self.a_r.at[w, k], here.beside, here.r)

    def second(self, w, k):
        here, zr = self.here, self.zr(k)
        if self.side_first[w]:
            src = self.acc[w].at[2 * zr + 1 - here.col, :, self.half(w, here.side)]
            to = (here.beside, here.r)
        else:
            src = self.acc[w].at[2 * zr + here.col, :, self.half(w, 1 - here.side)]
            to = (here.s, here.twin)
        return remote(src, self.two[w].at[zr], self.b_s.at[w, k], self.b_r.at[w, k], *to)

    def final(self, w, k):
        here, zr = self.here, self.zr(k)
        src = self.acc[w].at[2 * zr + here.col, :, self.half(w, here.side)]
        return remote(
            src, self.far[w].at[here.row], self.z_s.at[w, k], self.z_r.at[w, here.row], 2 * zr + here.col, here.r
        )

    def begin(self):
        for k in range(self.nz):
            for w in range(self.nw):
                self.swap(w, k).start()
                if k == 0:
                    self.load(w, 0).start()

    def strips(self, w, body):
        def one(r, carry):
            body(pl.ds(pl.multiple_of(r * 16, 16), 16))
            return carry

        lax.fori_loop(0, self.acc[w].shape[1] // 16, one, 0)

    def event_one(self, w, k):
        zr = self.zr(k)
        pair = pl.ds(2 * zr, 2)
        self.load(w, k).wait()
        self.swap(w, k).wait_recv()
        acc, own = self.acc[w], self.own[w]

        def strip(at):
            acc[pair, at, :] = (acc[pair, at, :].astype(F32) + own[:, at, :].astype(F32)).astype(BF16)

        self.strips(w, strip)
        self.first(w, k).start()

        @pl.when(k < self.nz - 1)
        def _():
            self.load(w, jnp.minimum(k + 1, self.nz - 1)).start()

    def event_two(self, w, k):
        here, zr = self.here, self.zr(k)
        self.first(w, k).wait_recv()
        acc, one = self.acc[w], self.one[w]
        if self.side_first[w]:
            pair = pl.ds(2 * zr, 2)
            lanes = self.half(w, here.side)

            def strip(at):
                acc[pair, at, lanes] = (acc[pair, at, lanes].astype(F32) + one[pair, at, :].astype(F32)).astype(BF16)

        else:
            shard = 2 * zr + here.col

            def strip(at):
                acc[shard, at, :] = (acc[shard, at, :].astype(F32) + one[zr, at, :].astype(F32)).astype(BF16)

        self.strips(w, strip)
        self.second(w, k).start()

    def event_three(self, w, k):
        here, zr = self.here, self.zr(k)
        self.second(w, k).wait_recv()
        shard, lanes = 2 * zr + here.col, self.half(w, here.side)
        acc, two = self.acc[w], self.two[w]

        def strip(at):
            acc[shard, at, lanes] = (acc[shard, at, lanes].astype(F32) + two[zr, at, :].astype(F32)).astype(BF16)

        self.strips(w, strip)

        @pl.when(k < self.nz - 1)
        def _():
            self.final(w, k).start()

    def slots(self):
        return CADENCE * (self.nw * self.nz + 2 * SUM_LAG)

    def slot(self, n):
        @pl.when(lax.rem(n, CADENCE) == 0)
        def _():
            self.event(n // CADENCE)

    def event(self, n):
        for stage, body in ((2, self.event_three), (1, self.event_two), (0, self.event_one)):
            e = n - stage * SUM_LAG
            for w in range(self.nw):
                ok = jnp.logical_and(e >= 0, e < self.nw * self.nz)

                @pl.when(jnp.logical_and(ok, lax.rem(e, self.nw) == w))
                def _():
                    body(w, jnp.maximum(e, 0) // self.nw)

    def over(self, w, k):
        here = self.here
        pairs = self.planes // 2
        to = 2 * lax.rem(here.plane // 2 + k, pairs) + here.side
        src = self.two[w].at[0]
        return remote(
            src, self.one_slot(w, here.plane // 2), self.x_s.at[w, k], self.x_r.at[w, here.plane // 2],
            here.s, to * CORES + here.c,
        )

    def one_slot(self, w, k):
        return self.acc[w].at[k, :, self.half(w, self.here.side)]

    def to_twin(self, w, side):
        part = self.outs[w].at[self.here.c, :, self.half(w, side)]
        return remote(part, part, self.t_s.at[w], self.t_r.at[w], self.here.s, self.here.twin)

    def to_mate(self, w, core, via):
        side = self.here.side if via == 0 else 1 - self.here.side
        part = self.outs[w].at[core, :, self.half(w, side)]
        return remote(part, part, self.f_s.at[w, via], self.f_r.at[w, via], self.here.s, self.here.mate)

    def finish(self):
        here = self.here
        for w in range(self.nw):
            self.far[w][here.row] = self.acc[w][here.s, :, self.half(w, here.side)]
            for k in range(self.nz - 1):
                off = lax.rem(here.row + 1 + k, self.nz)
                part = self.far[w].at[off]
                remote(part, part, self.z_s.at[w, k], self.z_r.at[w, off], here.s, here.r).wait_recv()
            far, out, lanes = self.far[w], self.outs[w], self.half(w, here.side)

            def strip(at):
                total = far[0, at, :].astype(F32)
                for k in range(1, self.nz):
                    total = total + far[k, at, :].astype(F32)
                out[here.c, at, lanes] = total.astype(BF16)

            self.strips(w, strip)
            self.to_twin(w, here.side).start()
            self.to_mate(w, here.c, 0).start()

    def twin_to_mate(self):
        for w in range(self.nw):
            self.to_twin(w, 1 - self.here.side).wait_recv()
            self.to_mate(w, self.here.c, 1).start()

    def drain(self):
        for w in range(self.nw):
            for via in (0, 1):
                self.to_mate(w, 1 - self.here.c, via).wait_recv()
                self.to_mate(w, self.here.c, via).wait_send()
            self.to_twin(w, self.here.side).wait_send()
            for k in range(self.nz):
                self.swap(w, k).wait_send()
                self.first(w, k).wait_send()
                self.second(w, k).wait_send()
                if k < self.nz - 1:
                    self.final(w, k).wait_send()


def sum_peers(here):
    p = here.p
    planes = p.R // CORES
    far = [(here.s, lax.rem(here.plane + k, planes) * CORES + j) for k in range(1, planes) for j in range(CORES)]
    twin_chip = here.twin - here.c
    return plane_peers(here) + far + [(here.beside, twin_chip + j) for j in range(CORES)]


def split_rows(p, grad):
    rows, cols = grad.shape
    return grad.reshape(p.S, CORES, rows // (p.S * CORES), cols)


def whole_shard(halves):
    return halves.reshape(CORES * halves.shape[1], halves.shape[2]).astype(F32)


def back_kernel(plan, nw, *refs):
    p = plan
    here = Place(p)
    s, c = here.s, here.c
    nz, near, width = here.rows, p.near, p.width
    (q, k, v, o, lse, preu, do_home, a_all, wcol, x, stream, par, small) = refs[:13]
    grads = refs[13 : 13 + nw]
    rest = refs[13 + nw :]
    input_grad, g_out, small_out = rest[:3]
    outs = rest[3 : 3 + nw]
    rest = rest[3 + nw :]
    (do_all, low, dk_acc, dv_acc, k_turn, da_own, da_out, da_in, da_side) = rest[:9]
    x_buf, stream_buf, buf_sem, a_buf, a_sem, gq = rest[-6:]
    rest = rest[:-6]
    da_home = input_grad
    (dw_out, dw_own, dw_in, dw_far, dw_end, small_acc, small_in, small_all) = rest[9:17]
    (do_ss, do_rs, dm_s, dm_r, dy_s, dy_r, dh_s, dh_r, wt_s, wt_r, wz_s, wz_r, wx_s, wx_r, wd_s, wd_r) = rest[17:33]
    (ss_s, ss_r, sa_s, sa_r) = rest[33:37]
    sums = GridSum(here, grads, outs, rest[37:])
    greet(sum_peers(here))
    rows_here = pl.ds(pl.multiple_of(lax.rem(s, p.P) * p.T, p.T), p.T)

    def do_copy(m, g):
        core, lane = g // p.cpu, g % p.cpu
        to = here.unit_of(c, m, s) * p.cpu + lane
        src = do_home.at[m, :, pl.ds(g * p.W, p.W)]
        dst = do_all.at[rows_here, :]
        away = jnp.logical_or(to != s, c != core)
        recv = do_rs.at[lax.rem(s, p.P)]
        return away, lambda: remote(src, dst, do_ss.at[m, g], recv, to, here.chip + core), (src, dst, recv)

    for m in range(p.M):
        for g in range(p.groups):
            launch(*do_copy(m, g))
    sums.begin()
    small_acc[...] = small[...]
    prefix = preu[0:1, 0:1]

    def block_rows(i):
        return pl.ds(pl.multiple_of(i * BQ, BQ), BQ)

    def a_load(b):
        slot = lax.rem(b, 2)
        return pltpu.make_async_copy(
            a_all.at[:, pl.ds(pl.multiple_of(b * BQ, BQ), BQ)], a_buf.at[slot], a_sem.at[slot]
        )

    def weight_part(h, dst, slot_from=None):
        def some(b, carry):
            slot = lax.rem(b, 2)

            @pl.when(b < p.D // BQ - 1)
            def _():
                a_load(b + 1).start()

            a_load(b).wait()
            dst[pl.ds(pl.multiple_of(b * BQ, BQ), BQ), :] = dot(a_buf[slot], low[h], 0, 0).astype(BF16)
            if slot_from is not None:
                sums.slot(slot_from + b)
            return carry

        lax.fori_loop(0, p.D // BQ, some, 0)

    def bias_part(h):
        folds = PAIR // width
        for row, lanes in ((0, slice(0, PAIR)), (1, slice(2 * PAIR, 3 * PAIR))):
            total = jnp.sum(low[h, :, lanes].astype(F32), axis=0, keepdims=True)
            for n in range(folds):
                at = (here.group * p.pairs + h) * folds + n
                small_acc[at, row : row + 1, 0:width] = total[:, n * width : (n + 1) * width]

    def to_twin_dw():
        return remote(dw_out, dw_in, wt_s.at[0], wt_r.at[0], s, here.twin)

    def pair_step(turn, carry):
        h = lax.rem(turn + 1 + here.side, 2)
        lanes = pl.ds(pl.multiple_of(h * PAIR, PAIR), PAIR)
        k_turn[...] = k[:, lanes].astype(F32).T.astype(BF16)
        dk_acc[...] = jnp.zeros_like(dk_acc)
        dv_acc[...] = jnp.zeros_like(dv_acc)

        def query_step(n, inner):
            j = lax.rem((here.unit - here.uq * near) * p.cpu + n // p.pieces, p.P)
            i = j * p.pieces + lax.rem(n, p.pieces)
            rows = block_rows(i)

            @pl.when(jnp.logical_and(turn == 0, lax.rem(n, p.pieces) == 0))
            def _():
                part = do_all.at[pl.ds(pl.multiple_of(j * p.T, p.T), p.T), :]
                pltpu.make_async_copy(part, part, do_rs.at[j]).wait()

            qp, dop, op = q[rows, lanes], do_all[rows, lanes], o[rows, lanes]
            turned = (dop.astype(F32) * op.astype(F32)).T
            pos = (lax.broadcasted_iota(jnp.int32, (1, BQ), 1) + i * BQ + 1).astype(F32)
            bound = jnp.maximum(pos, prefix)
            dq_t = []
            for e in (0, 1):
                lit = head_lanes(BQ, e)
                qe = jnp.where(lit, qp, jnp.zeros_like(qp))
                de = jnp.where(lit, dop, jnp.zeros_like(dop))
                level = lse[2 * h + e, 0:1, rows]
                inner_sum = jnp.sum(turned[e * HEAD : (e + 1) * HEAD], axis=0, keepdims=True)
                total = jnp.zeros((HEAD, BQ), F32)
                for start in range(0, LEN, KEYS):
                    keys = slice(start, start + KEYS)
                    key_pos = (lax.broadcasted_iota(jnp.int32, (KEYS, 1), 0) + start).astype(F32)
                    logits = dot(k[keys, lanes], qe, 1, 1)
                    probs = jnp.where(key_pos < bound, jnp.exp2(logits * SCALE2 - level), 0.0)
                    slope = dot(v[keys, lanes], de, 1, 1)
                    dlog = (probs * (slope - inner_sum)).astype(BF16)
                    dv_acc[keys, :] += dot(probs.astype(BF16), de)
                    dk_acc[keys, :] += dot(dlog, qe)
                    total = total + dot(k_turn[e * HEAD : (e + 1) * HEAD, keys], dlog)
                dq_t.append(total)
            low[h, rows, 0:PAIR] = (jnp.concatenate(dq_t, axis=0).T * SCALE).astype(BF16)
            sums.slot(turn * p.nq + n)
            return inner

        lax.fori_loop(0, p.nq, query_step, 0)
        low[h, :, PAIR : 2 * PAIR] = (dk_acc[...] * SCALE).astype(BF16)
        low[h, :, 2 * PAIR :] = dv_acc[...].astype(BF16)
        bias_part(h)

        a_load(0).start()

        @pl.when(turn == 0)
        def _():
            weight_part(h, dw_out)
            to_twin_dw().start()

        return carry

    lax.fori_loop(0, p.pairs, pair_step, 0)

    half = p.D // CORES

    def block_of(n):
        lane = lax.rem(here.lane + 1 + n // (near * p.pieces), p.cpu)
        m = lax.rem(n, near * p.pieces)
        return ((m // p.pieces) * p.cpu + lane) * p.pieces + lax.rem(m, p.pieces)

    def da_half(rows, core):
        at = pl.ds(pl.multiple_of(core * half, half), half)
        total = dot(low[0, rows, :], wcol[0, at, :], 1, 1)
        for h in range(1, p.pairs):
            total = total + dot(low[h, rows, :], wcol[h, at, :], 1, 1)
        return total

    def da_mate(n, i):
        rows = block_rows(i)
        return remote(da_out.at[rows, :], da_in.at[rows, :], dm_s.at[n], dm_r.at[i], s, here.mate)

    far_blocks = (p.cpu - 1) * near * p.pieces
    count = p.pairs * p.nq

    def side_rows(i):
        return block_rows((i // p.pieces // p.cpu) * p.pieces + lax.rem(i, p.pieces))

    def da_over(n, i):
        return remote(da_own.at[block_rows(i), :], da_side.at[side_rows(i), :], dy_s.at[n], dy_r.at[i], here.beside, here.r)

    def da_first(n, carry):
        @pl.when(n < p.nq)
        def _():
            i = block_of(n)
            rows = block_rows(i)
            da_out[rows, :] = da_half(rows, 1 - c).astype(BF16)
            da_mate(n, i).start()
            da_own[rows, :] = da_half(rows, c).astype(BF16)

        @pl.when(n > 0)
        def _():
            last = jnp.maximum(n - 1, 0)
            i = block_of(last)
            rows = block_rows(i)
            da_mate(last, i).wait_recv()
            da_own[rows, :] = (da_own[rows, :].astype(F32) + da_in[rows, :].astype(F32)).astype(BF16)

            @pl.when(last < far_blocks)
            def _():
                da_over(last, i).start()

        sums.slot(count + n)
        return carry

    lax.fori_loop(0, p.nq + 1, da_first, 0)
    count = count + p.nq + 1

    own_pair = here.side
    weight_part(own_pair, dw_own, count)
    count = count + p.D // BQ
    to_twin_dw().wait_recv()
    dw_own[...] = (dw_own[...].astype(F32) + dw_in[...].astype(F32)).astype(BF16)
    span = 2 * width

    def dw_rows(zr):
        return pl.ds(pl.multiple_of(zr * span, span), span)

    def dw_send(n):
        zr = lax.rem(here.row + 1 + n, nz)
        return remote(
            dw_own.at[dw_rows(zr), :], dw_far.at[here.row], wz_s.at[n], wz_r.at[here.row], 2 * zr + here.col, here.r
        )

    for n in range(nz - 1):
        dw_send(n).start()

    def da_back(n, i):
        rows = block_rows(i)
        home = here.uq * p.P + i // p.pieces
        piece = lax.rem(i, p.pieces)
        dst = da_home.at[here.um, block_rows(piece), pl.ds(pl.multiple_of(c * half, half), half)]
        src = da_own.at[rows, :]
        recv = dh_r.at[here.um, c, piece]
        away = jnp.logical_or(home != s, here.uc != c)
        return away, lambda: remote(src, dst, dh_s.at[n], recv, home, here.chip + here.uc), (src, dst, recv)

    def da_second(n, carry):
        i = block_of(n)
        rows = block_rows(i)
        da_over(n, i).wait_recv()
        da_own[rows, :] = (da_own[rows, :].astype(F32) + da_side[side_rows(i), :].astype(F32)).astype(BF16)
        launch(*da_back(n, i))
        sums.slot(count + n - far_blocks)
        return carry

    lax.fori_loop(far_blocks, p.nq, da_second, 0)
    count = count + p.nq - far_blocks

    def rest_of_sums(n, carry):
        sums.slot(n)
        return carry

    lax.fori_loop(count, max(count, sums.slots()), rest_of_sums, 0)
    sums.finish()

    dw_far[here.row] = dw_own[dw_rows(here.row), :]
    for n in range(nz - 1):
        off = lax.rem(here.row + 1 + n, nz)
        remote(dw_far.at[off], dw_far.at[off], wz_s.at[n], wz_r.at[off], s, here.r).wait_recv()
    total = dw_far[0].astype(F32)
    for n in range(1, nz):
        total = total + dw_far[n].astype(F32)
    dw_end[...] = total.astype(BF16)
    slot = here.group * p.pairs + here.side
    twin_chip = here.twin - c

    def dw_give(n):
        fy, fx, fc = n // 4, n // 2 % 2, n % 2
        col = here.col if fy == 0 else 1 - here.col
        core = c if fc == 0 else 1 - c
        src = dw_end.at[pl.ds(pl.multiple_of(col * width, width), width), :]
        dst = gq.at[slot]
        to = (2 * here.row + col, (here.chip if fx == 0 else twin_chip) + core)
        return src, dst, to

    for n in range(1, 8):
        src, dst, to = dw_give(n)
        remote(src, dst, wd_s.at[n], wd_r.at[slot], *to).start()
    gq[slot] = dw_end[pl.ds(pl.multiple_of(here.col * width, width), width), :]

    def token_loads(m, piece):
        at = pl.ds(pl.multiple_of(piece * BQ, BQ), BQ)
        return (
            pltpu.make_async_copy(x.at[m, at, :], x_buf, buf_sem.at[0]),
            pltpu.make_async_copy(stream.at[m, at, :], stream_buf, buf_sem.at[1]),
        )

    blocks = p.M * p.pieces
    gain = par[4:5, :].astype(F32)

    def loads_of(n):
        return token_loads(n // p.pieces, lax.rem(n, p.pieces))

    for copy in loads_of(0):
        copy.start()

    def norm_back(n, carry):
        gain_sum, shift_sum = carry
        m, piece = n // p.pieces, lax.rem(n, p.pieces)
        at = pl.ds(pl.multiple_of(piece * BQ, BQ), BQ)
        for core in range(CORES):
            dst = da_home.at[m, at, pl.ds(core * half, half)]
            pltpu.make_async_copy(dst, dst, dh_r.at[m, core, piece]).wait()
        for copy in loads_of(n):
            copy.wait()
        values = x_buf[...].astype(F32)
        dy = da_home[m, at, :].astype(F32)
        centre = values - jnp.mean(values, axis=-1, keepdims=True)
        spread = jnp.mean(centre * centre, axis=-1, keepdims=True)
        scale = lax.rsqrt(spread + EPS)
        wn = centre * scale
        e = dy * gain
        dw = scale * (e - jnp.mean(e, axis=-1, keepdims=True) - wn * jnp.mean(e * wn, axis=-1, keepdims=True))
        input_grad[m, at, :] = (stream_buf[...] + dw).astype(BF16)

        @pl.when(n + 1 < blocks)
        def _():
            for copy in loads_of(jnp.minimum(n + 1, blocks - 1)):
                copy.start()

        return (
            gain_sum + jnp.sum(dy * wn, axis=0, keepdims=True),
            shift_sum + jnp.sum(dy, axis=0, keepdims=True),
        )

    none = jnp.zeros((1, p.D), F32)
    gain_sum, shift_sum = lax.fori_loop(0, blocks, norm_back, (none, none))
    for n in range(p.S):
        lanes = slice(n * width, (n + 1) * width)
        small_acc[n, 4:5, 0:width] = gain_sum[:, lanes]
        small_acc[n, 8:9, 0:width] = shift_sum[:, lanes]

    def tiny(n):
        to = lax.rem(s + n, p.S)
        return remote(small_acc.at[to], small_in.at[n], ss_s.at[n], ss_r.at[n], to, here.r)

    for n in range(1, p.S):
        tiny(n).start()
    sums.twin_to_mate()
    total = small_acc[s]
    for n in range(1, p.S):
        tiny(n).wait_recv()
        total = total + small_in[n]
    small_all[here.r] = total

    def every(n):
        to = lax.rem(here.r + n, p.R)
        return remote(small_all.at[here.r], small_all.at[here.r], sa_s.at[n], sa_r.at[here.r], s, to)

    for n in range(1, p.R):
        every(n).start()
    for n in range(1, p.R):
        off = lax.rem(here.r + n, p.R)
        remote(small_all.at[0], small_all.at[off], sa_s.at[n], sa_r.at[off], s, here.r).wait_recv()
    total = small_all[0]
    for n in range(1, p.R):
        total = total + small_all[n]
    small_out[...] = total

    for m in range(p.M):
        for g in range(p.groups):
            sent(*do_copy(m, g))

    def da_sent(n, carry):
        i = block_of(n)
        da_mate(n, i).wait_send()

        @pl.when(n < far_blocks)
        def _():
            da_over(n, i).wait_send()

        @pl.when(n >= far_blocks)
        def _():
            sent(*da_back(n, i))

        return carry

    lax.fori_loop(0, p.nq, da_sent, 0)
    to_twin_dw().wait_send()
    for n in range(nz - 1):
        dw_send(n).wait_send()
    for n in range(1, 8):
        src, dst, to = dw_give(n)
        remote(src, dst, wd_s.at[n], wd_r.at[slot], *to).wait_send()
    for n in range(p.groups * p.pairs):

        @pl.when(n != slot)
        def _():
            remote(gq.at[n], gq.at[n], wd_s.at[0], wd_r.at[n], s, here.r).wait_recv()

        for k in range(3):
            at = k * p.D + n * PAIR
            g_out[:, at : at + PAIR] = gq[n, :, k * PAIR : (k + 1) * PAIR]

    for n in range(1, p.S):
        tiny(n).wait_send()
    for n in range(1, p.R):
        every(n).wait_send()
    sums.drain()


def back(plan, units, small, grads):
    p = plan
    nw = len(grads)
    nz = p.S // 2
    planes = p.R // CORES
    split = [split_rows(p, grad) for grad in grads]
    shapes = [h.shape[2:] for h in split]
    any_space = pl.BlockSpec(memory_space=pl.ANY)
    vmem = pl.BlockSpec(memory_space=pltpu.VMEM)
    dma = pltpu.SemaphoreType.DMA
    shape = jax.ShapeDtypeStruct
    half = p.D // CORES
    outs = pl.pallas_call(
        functools.partial(back_kernel, p, nw),
        out_shape=[
            shape((p.M, p.T, p.D), BF16),
            shape((p.width, 3 * p.D), BF16),
            shape(small.shape[1:], F32),
        ]
        + [shape((CORES,) + sh, BF16) for sh in shapes],
        in_specs=[vmem] * 6 + [any_space] * 2 + [vmem] + [any_space] * 2 + [vmem] * 2 + [any_space] * nw,
        out_specs=[vmem] * (3 + nw),
        scratch_shapes=[
            pltpu.VMEM((LEN, p.W), BF16),
            pltpu.VMEM((p.pairs, LEN, 3 * PAIR), BF16),
            pltpu.VMEM((LEN, PAIR), F32),
            pltpu.VMEM((LEN, PAIR), F32),
            pltpu.VMEM((PAIR, LEN), BF16),
            pltpu.VMEM((LEN, half), BF16),
            pltpu.VMEM((LEN, half), BF16),
            pltpu.VMEM((LEN, half), BF16),
            pltpu.VMEM((p.near * p.T, half), BF16),
            pltpu.VMEM((p.D, 3 * PAIR), BF16),
            pltpu.VMEM((p.D, 3 * PAIR), BF16),
            pltpu.VMEM((p.D, 3 * PAIR), BF16),
            pltpu.VMEM((nz, 2 * p.width, 3 * PAIR), BF16),
            pltpu.VMEM((2 * p.width, 3 * PAIR), BF16),
            pltpu.VMEM(small.shape, F32),
            pltpu.VMEM(small.shape, F32),
            pltpu.VMEM((p.R,) + small.shape[1:], F32),
            dma((p.M, p.groups)), dma((p.P,)),
            dma((p.nq,)), dma((p.nq,)), dma((p.nq,)), dma((p.nq,)),
            dma((p.nq,)), dma((p.M, CORES, p.pieces)),
            dma((1,)), dma((1,)), dma((nz,)), dma((nz,)), dma((planes,)), dma((planes,)), dma((8,)), dma((8,)),
            dma((p.S,)), dma((p.S,)), dma((p.R,)), dma((p.R,)),
        ]
        + GridSum.scratch(p, shapes)
        + [pltpu.VMEM((BQ, p.D), BF16), pltpu.VMEM((BQ, p.D), F32), dma((2,))]
        + [pltpu.VMEM((2, LEN, BQ), BF16), dma((2,))]
        + [pltpu.VMEM((p.groups * p.pairs, p.width, 3 * PAIR), BF16)],
        compiler_params=pltpu.CompilerParams(
            collective_id=1, has_side_effects=True, vmem_limit_bytes=VMEM_LIMIT
        ),
        name="back",
    )(*units, small, *split)
    return outs[0], outs[1].astype(F32), outs[2], [whole_shard(part) for part in outs[3:]]


def per_device(
    sizes,
    inputs,
    prefix,
    qkv_weight,
    qv_bias,
    out_weight,
    branch_bias,
    up_weight,
    up_bias,
    down_weight,
    norm_gain,
    norm_bias,
    cotangent,
):
    p = Plan(sizes, (inputs.shape[0], 1, inputs.shape[2], inputs.shape[3]))
    tokens_all = p.M * p.T
    x = inputs[:, 0]
    width = p.D // p.S
    spare = max(128 - width, 0)
    small_in = (qv_bias, branch_bias, norm_gain, norm_bias, up_bias.reshape(-1, width))
    (wo, wu, wd, parf, q, k, v, o, lse, preu, o_home, a_unit, w_unit) = fore(
        p, x, small_in, prefix[:, 0], qkv_weight, (out_weight, up_weight, down_weight)
    )
    par32 = parf.astype(F32)
    bias_branch = par32[2:4]
    gains, shifts = par32[4:8], par32[8:12]
    bias_up = par32[12:].reshape(-1, p.S, width).transpose(1, 0, 2).reshape(-1)

    tokens = x.reshape(tokens_all, p.D).astype(F32)
    upstream = cotangent[:, 0].reshape(tokens_all, p.D).astype(F32)
    mixed_low = o_home.reshape(tokens_all, p.D)
    branch = dot(mixed_low, wo) + bias_branch[0]
    side, pull_side = jax.vjp(normed, branch, gains[1:2], shifts[1:2])
    stream = tokens + side
    normal_mid, pull_mid = jax.vjp(normed, stream, gains[2:3], shifts[2:3])
    middle_low = normal_mid.astype(BF16)
    upper = dot(middle_low, wu) + bias_up
    below = 0.5 * (1.0 + lax.erf(upper * math.sqrt(0.5)))
    slope = below + upper * jnp.exp(-0.5 * upper * upper) * (1.0 / math.sqrt(2.0 * math.pi))
    active_low, slope = lax.optimization_barrier(((upper * below).astype(BF16), slope))
    lower = dot(active_low, wd) + bias_branch[1]
    closing, pull_close = jax.vjp(normed, lower, gains[3:4], shifts[3:4])
    output = (stream + closing).astype(BF16)
    grad_lower, gain_three, shift_three = pull_close(upstream)
    lower_low = grad_lower.astype(BF16)
    grad_active = dot(lower_low, wd, 1, 1)
    upper_low = (grad_active * slope).astype(BF16)
    grad_middle = dot(upper_low, wu, 1, 1)
    grad_mid_in, gain_two, shift_two = pull_mid(grad_middle)
    grad_stream = grad_mid_in + upstream
    grad_branch, gain_one, shift_one = pull_side(grad_stream)
    branch_low = grad_branch.astype(BF16)
    grad_mixed = dot(branch_low, wo, 1, 1).astype(BF16)

    grads = (
        dot(active_low, lower_low, 0, 0).astype(BF16),
        dot(middle_low, upper_low, 0, 0).astype(BF16),
        dot(mixed_low, branch_low, 0, 0).astype(BF16),
    )
    def column_sum(values):
        return jnp.sum(values.astype(F32), axis=0, keepdims=True)

    du_sum = column_sum(upper_low).reshape(p.S, -1, width).transpose(1, 0, 2).reshape(-1, p.D)
    none = jnp.zeros((1, p.D), F32)
    small = jnp.concatenate(
        [
            none, none, column_sum(branch_low), column_sum(lower_low),
            none, gain_one, gain_two, gain_three,
            none, shift_one, shift_two, shift_three,
            du_sum,
        ], axis=0,
    )
    small = jnp.pad(small.reshape(-1, p.S, width).transpose(1, 0, 2), ((0, 0), (0, 0), (0, spare)))
    by_token = (p.M, p.T, p.D)
    input_grad, sum_qkv, tiny, (sum_down, sum_up, sum_out) = back(
        p,
        (
            q, k, v, o, lse, preu, grad_mixed.reshape(by_token), a_unit, w_unit,
            x, grad_stream.reshape(by_token), parf,
        ),
        small, grads,
    )
    tiny = tiny[:, :width]
    shaped = (p.M, 1, p.T, p.D)
    return (
        output.reshape(shaped),
        input_grad.reshape(shaped),
        sum_qkv,
        tiny[0:2],
        sum_out,
        tiny[2:4],
        sum_up,
        tiny[12:].reshape(-1),
        sum_down,
        tiny[4:8],
        tiny[8:12],
    )


def solution(mesh):
    sizes = {name: mesh.shape[name] for name in ("shard", "replica")}
    placed = (
        P(None, "replica", "shard", None),
        P(None, "replica", None),
        P("shard", None),
        P(None, "shard"),
        P("shard", None),
        P(None, "shard"),
        P("shard", None),
        P("shard"),
        P("shard", None),
        P(None, "shard"),
        P(None, "shard"),
        P(None, "replica", "shard", None),
    )
    return jax.shard_map(
        functools.partial(per_device, sizes),
        mesh=mesh,
        in_specs=placed,
        out_specs=(
            P(None, "replica", "shard", None),
            P(None, "replica", "shard", None),
            P("shard", None),
            P(None, "shard"),
            P("shard", None),
            P(None, "shard"),
            P("shard", None),
            P("shard"),
            P("shard", None),
            P(None, "shard"),
            P(None, "shard"),
        ),
        check_vma=False,
    )
```

```python
import functools
import math

import jax
import jax.numpy as jnp
from jax import lax
from jax.experimental import pallas as pl
from jax.experimental.pallas import tpu as pltpu
from jax.sharding import PartitionSpec as P

HEAD = 64
LEN = 2048
CORES = 2
PAIR = 2 * HEAD
BQ = 256
EPS = 1e-05
MASKED = -1e30
SCALE = HEAD ** (-0.5)
SCALE2 = SCALE * math.log2(math.e)
F32 = jnp.float32
BF16 = jnp.bfloat16
MESH = pl.DeviceIdType.MESH
VMEM_LIMIT = 66_000_000
LAG = 2
KEYS = 512
SIDE_FIRST = (True, False, False)
SUM_LAG = 5
CADENCE = 1
COLUMN_FIRST = (False, True, False)
START = 1
EARLY = 2


class Plan:
    def __init__(self, mesh_shape, inputs_shape):
        self.S = mesh_shape["shard"]
        self.R = mesh_shape["replica"]
        self.M, _, self.T, self.D = inputs_shape
        self.Q = self.T * self.S // LEN
        self.P = LEN // self.T
        self.U = self.M * self.Q * CORES
        self.cpu = self.S // self.U
        self.heads = self.D // HEAD
        self.W = self.D // (CORES * self.cpu)
        self.pairs = self.W // PAIR
        self.groups = CORES * self.cpu
        self.pieces = self.T // BQ
        self.nq = LEN // BQ
        self.near = self.P // self.cpu
        self.width = self.D // self.S
        assert self.cpu == 2 and self.pairs == 2 and self.T % BQ == 0 and LEN % self.T == 0


class Place:
    def __init__(self, plan):
        self.p = plan
        self.s = lax.axis_index("shard")
        self.r = lax.axis_index("replica")
        self.c = lax.rem(self.r, CORES)
        self.chip = self.r - self.c
        self.mate = self.chip + (1 - self.c)
        self.unit = self.s // plan.cpu
        self.lane = lax.rem(self.s, plan.cpu)
        self.group = self.c * plan.cpu + self.lane
        self.uc = lax.rem(self.unit, CORES)
        self.um = lax.rem(self.unit // CORES, plan.M)
        self.uq = self.unit // (CORES * plan.M)
        self.ring = self.to_ring(self.s)
        self.plane = self.r // CORES
        self.side = lax.rem(self.plane, 2)
        self.twin = self.r + CORES * (1 - 2 * self.side)
        self.row = self.s // 2
        self.col = lax.rem(self.s, 2)
        self.beside = 2 * self.row + 1 - self.col
        self.rows = plan.S // 2

    def unit_of(self, c, m, s):
        return ((s // self.p.P) * self.p.M + m) * CORES + c

    def to_ring(self, s):
        half = self.p.S // 2
        row, col = s // 2, lax.rem(s, 2)
        return row + col * (2 * half - 1 - 2 * row)

    def from_ring(self, i):
        n = self.p.S
        return jnp.where(i < n // 2, 2 * i, 2 * (n - 1 - i) + 1)


def remote(src, dst, send, recv, s, r):
    return pltpu.make_async_remote_copy(
        src_ref=src, dst_ref=dst, send_sem=send, recv_sem=recv, device_id=(s, r), device_id_type=MESH
    )


def launch(away, far, near):
    @pl.when(away)
    def _():
        far().start()

    @pl.when(jnp.logical_not(away))
    def _():
        pltpu.make_async_copy(*near).start()


def sent(away, far, near):
    @pl.when(away)
    def _():
        far().wait_send()


def greet(peers):
    barrier = pltpu.get_barrier_semaphore()
    for s, r in peers:
        pl.semaphore_signal(barrier, inc=1, device_id=(s, r), device_id_type=MESH)
    pl.semaphore_wait(barrier, len(peers))


def plane_peers(here):
    n = here.p.S * CORES
    own = here.s * CORES + here.c
    out = []
    for k in range(1, n):
        i = lax.rem(own + k, n)
        out.append((i // CORES, here.chip + lax.rem(i, CORES)))
    return out


def normed(values, gain, shift):
    centre = values - jnp.mean(values, axis=-1, keepdims=True)
    spread = jnp.mean(centre * centre, axis=-1, keepdims=True)
    return centre * lax.rsqrt(spread + EPS) * gain + shift


def dot(a, b, ca=1, cb=0):
    return lax.dot_general(a, b, (((ca,), (cb,)), ((), ())), preferred_element_type=F32)


def head_lanes(rows, which):
    lane = lax.broadcasted_iota(jnp.int32, (rows, PAIR), 1)
    return (lane < HEAD) if which == 0 else (lane >= HEAD)


def fore_kernel(
    plan, x, biases, branches, gains, shifts, ups, prefixes, wq_in, wo, wu, wd,
    wof, wuf, wdf, parf, q_out, k_out, v_out, o_out, lse_out, preu, oh, a_all, wcol,
    ah, par, pre, wq, parg, pre2,
    par_ss, par_rs, pre_sem, loc_sem, a_ss, a_rs, af_ss, z_ss, z_rs, wa_ss, wa_rs, wb_ss, wb_rs, wm_ss, wm_rs,
    o_ss, o_rs, q_ss, q_rs, qt_ss, qt_rs, q_loc,
):
    p = plan
    here = Place(p)
    s, c = here.s, here.c
    mine, full = (wo, wu, wd), (wof, wuf, wdf)
    nw = len(mine)
    first = COLUMN_FIRST
    greet(plane_peers(here) + [(s, here.twin)])

    par[...] = jnp.zeros_like(par)
    at = 0
    for part in (biases, branches, gains, shifts, ups):
        par[at : at + part.shape[0], 0 : part.shape[1]] = part[...]
        at += part.shape[0]
    pre[...] = jnp.zeros_like(pre)
    for m in range(p.M):
        for n in range(p.Q):
            pre[m * p.Q + n : m * p.Q + n + 1, :] = jnp.full((1, 128), prefixes[m, n].astype(F32))
    for g in range(p.groups):
        for h in range(p.pairs):
            for k in range(3):
                at = k * p.D + g * p.W + h * PAIR
                wq[g, h, :, k * PAIR : (k + 1) * PAIR] = wq_in[:, at : at + PAIR]
    parg[s] = par[...]
    small = []
    for k in range(1, p.S):
        to = lax.rem(s + k, p.S)
        small.append(remote(par, parg.at[s], par_ss.at[k], par_rs.at[k], to, here.r))
        small[-1].start()
    swap = remote(pre, pre2, pre_sem.at[0], pre_sem.at[1], s, here.mate)
    swap.start()

    z, nz = here.row, here.rows

    def where(w, zr, fa, fb, core):
        fy, fx = (fa, fb) if first[w] else (fb, fa)
        col = here.col if fy == 0 else 1 - here.col
        side = here.side if fx == 0 else 1 - here.side
        n, width = mine[w].shape[0], mine[w].shape[1] // 2
        rows = pl.ds(pl.multiple_of((2 * zr + col) * n + core * (n // 2), n // 2), n // 2)
        return full[w].at[rows, pl.ds(pl.multiple_of(side * width, width), width)]

    def origin(w, fa):
        n, width = mine[w].shape[0], mine[w].shape[1] // 2
        side = here.side if fa == 0 else 1 - here.side
        rows = pl.ds(pl.multiple_of(c * (n // 2), n // 2), n // 2)
        return mine[w].at[rows, pl.ds(pl.multiple_of(side * width, width), width)]

    def peer(w, second):
        return (here.beside, here.r) if first[w] == (second == 0) else (s, here.twin)

    def z_send(w, d, k):
        sign = 1 - 2 * d
        part = where(w, z - sign * (k - 1), 0, 0, c)
        src = origin(w, 0) if isinstance(k, int) and k == 1 else part
        return remote(src, part, z_ss.at[w, d, k - 1], z_rs.at[w, d, k - 1], s + 2 * sign, here.r)

    def z_came(w, d, k):
        sign = 1 - 2 * d
        part = where(w, z - sign * k, 0, 0, c)
        return remote(part, part, z_ss.at[w, d, k - 1], z_rs.at[w, d, k - 1], s, here.r)

    def to_first(w, zr, src=None):
        part = where(w, zr, 0, 0, c)
        return remote(part if src is None else src, part, wa_ss.at[w, zr], wa_rs.at[w, zr], *peer(w, 0))

    def to_second(w, fa, zr, src=None):
        part = where(w, zr, fa, 0, c)
        return remote(part if src is None else src, part, wb_ss.at[w, fa, zr], wb_rs.at[w, fa, zr], *peer(w, 1))

    def to_mate(w, fa, fb, zr, core):
        part = where(w, zr, fa, fb, core)
        at = 2 * fa + fb
        return remote(part, part, wm_ss.at[w, at, zr], wm_rs.at[w, at, zr], s, here.mate)

    def first_came(w, zr):
        part = where(w, zr, 1, 0, c)
        return remote(part, part, wa_ss.at[w, zr], wa_rs.at[w, zr], s, here.r)

    def second_came(w, fa, zr):
        part = where(w, zr, fa, 1, c)
        return remote(part, part, wb_ss.at[w, fa, zr], wb_rs.at[w, fa, zr], s, here.r)

    def on_grid(d, k):
        return z >= k if d == 0 else z + k < nz

    def can_send(d):
        return z < nz - 1 if d == 0 else z > 0

    def gather_rows(w):
        for d in (0, 1):

            @pl.when(can_send(d))
            def _():
                z_send(w, d, 1).start()

    def gather_near(w):
        if first[w]:
            to_first(w, z, origin(w, 0)).start()
        else:
            to_second(w, 0, z, origin(w, 0)).start()
            to_second(w, 1, z, origin(w, 1)).start()

    def gather_slot(w, k, lag):
        for d in (0, 1):
            sign = 1 - 2 * d

            @pl.when(jnp.logical_and(k >= 1, on_grid(d, k)))
            def _():
                at = jnp.maximum(k, 1)
                z_came(w, d, at).wait_recv()
                zr = z - sign * at

                @pl.when(can_send(d))
                def _():
                    z_send(w, d, at + 1).start()

                to_first(w, zr).start()
                to_second(w, 0, zr).start()
                to_mate(w, 0, 0, zr, c).start()

        def at_distance(j, least, body):
            for d in (0, 1):
                ok = jnp.logical_and(j >= max(least, d), on_grid(d, j))

                @pl.when(ok)
                def _():
                    body(z - (1 - 2 * d) * jnp.maximum(j, 0))

        def after_first(zr):
            first_came(w, zr).wait_recv()
            to_second(w, 1, zr).start()
            to_mate(w, 1, 0, zr, c).start()

        at_distance(k - 1, 0 if first[w] else 1, after_first)

        def after_second(fa):
            def body(zr):
                second_came(w, fa, zr).wait_recv()
                to_mate(w, fa, 1, zr, c).start()

            return body

        at_distance(k - 1 - lag, 1 if first[w] else 0, after_second(0))
        at_distance(k - 2 - lag, 0, after_second(1))

    def mate_pieces(w, zr, act):
        other = zr != z

        @pl.when(other)
        def _():
            act(0, 0)

        if first[w]:

            @pl.when(other)
            def _():
                act(0, 1)

            act(1, 0)
        else:

            @pl.when(other)
            def _():
                act(1, 0)

            act(0, 1)
        act(1, 1)

    def gather_wait(w):
        def one(zr, carry):
            mate_pieces(w, zr, lambda fa, fb: to_mate(w, fa, fb, zr, 1 - c).wait_recv())
            return carry

        lax.fori_loop(0, nz, one, 0)

    def gather_drain(w):
        def one(zr, carry):
            mate_pieces(w, zr, lambda fa, fb: to_mate(w, fa, fb, zr, c).wait_send())
            if first[w]:
                to_first(w, zr).wait_send()

                @pl.when(zr != z)
                def _():
                    to_second(w, 0, zr).wait_send()
            else:

                @pl.when(zr != z)
                def _():
                    to_first(w, zr).wait_send()

                to_second(w, 0, zr).wait_send()
            to_second(w, 1, zr).wait_send()
            for d in (0, 1):
                reach = zr <= z if d == 0 else zr < nz - z

                @pl.when(jnp.logical_and(can_send(d), reach))
                def _():
                    z_send(w, d, zr + 1).wait_send()

            return carry

        lax.fori_loop(0, nz, one, 0)

    nq_rows = wq.shape[2]
    half_rows = nq_rows // 2

    def q_rows(k, side):
        return pl.ds(pl.multiple_of(k * nq_rows + side * half_rows, half_rows), half_rows)

    def q_send(k):
        to = lax.rem(s + k, p.S)
        group = c * p.cpu + lax.rem(to, p.cpu)
        rows = pl.ds(pl.multiple_of(here.side * half_rows, half_rows), half_rows)
        src = wq.at[group, :, rows, :]
        return remote(src, wcol.at[:, q_rows(s, here.side), :], q_ss.at[k], q_rs.at[s], to, here.r)

    def q_twin(k, side):
        part = wcol.at[:, q_rows(k, side), :]
        return remote(part, part, qt_ss.at[k], qt_rs.at[k], s, here.twin)

    def q_from(k):
        return lax.rem(s + p.S - k, p.S)

    for k in range(1, p.S):
        q_send(k).start()
    for w in range(nw):
        gather_near(w)
    q_own = pltpu.make_async_copy(
        wq.at[here.group], wcol.at[:, pl.ds(pl.multiple_of(s * nq_rows, nq_rows), nq_rows), :], q_loc.at[0]
    )
    q_own.start()
    local = []
    for w in range(nw):
        n = mine[w].shape[0]
        local.append(
            pltpu.make_async_copy(mine[w], full[w].at[pl.ds(pl.multiple_of(s * n, n), n), :], loc_sem.at[w])
        )
        local[-1].start()

    for k in range(1, p.S):
        small[k - 1].wait_recv()
    parf[...] = jnp.concatenate([parg[k][:, : p.D // p.S] for k in range(p.S)], axis=1)
    gain = parf[4:5, :].astype(F32)
    shift = parf[8:9, :].astype(F32)
    rows_here = pl.ds(pl.multiple_of(lax.rem(s, p.P) * p.T, p.T), p.T)

    def first_hop(m):
        to = here.unit_of(c, m, s) * p.cpu + here.lane
        far = lambda: remote(ah.at[m], a_all.at[rows_here, :], a_ss.at[m], a_rs.at[lax.rem(s, p.P)], to, here.r)
        return to, far

    for m in range(p.M):
        ah[m] = normed(x[m].astype(F32), gain, shift).astype(BF16)
        to, far = first_hop(m)

        @pl.when(to != s)
        def _():
            far().start()

        @pl.when(to == s)
        def _():
            a_all[rows_here, :] = ah[m]

    primary = c == here.uc

    def a_rows(j):
        return pl.ds(pl.multiple_of(j * p.T, p.T), p.T)

    def a_forward(j, k):
        part = a_all.at[a_rows(j), :]
        if k == 0:
            return remote(part, part, af_ss.at[j, 0], a_rs.at[j], s, here.mate)
        to = here.unit * p.cpu + lax.rem(here.lane + k, p.cpu)
        return remote(part, part, af_ss.at[j, k], a_rs.at[j], to, here.r)

    def a_wait(j):
        part = a_all.at[a_rows(j), :]
        remote(part, part, af_ss.at[j, 0], a_rs.at[j], s, here.mate).wait_recv()

    near = p.near

    zi = here.unit - here.uq * near

    def a_at(k, body):
        for d in (0, 1):
            if k or not d:
                ok = zi >= k if d == 0 else zi + k < near

                @pl.when(jnp.logical_and(primary, ok))
                def _():
                    body(zi - (1 - 2 * d) * k)

    def a_near(jj):
        j = jj * p.cpu + here.lane

        @pl.when(here.uq * p.P + j != s)
        def _():
            a_wait(j)

        for k in list(range(1, p.cpu)) + [0]:
            a_forward(j, k).start()

    def a_far(jj):
        for k in range(1, p.cpu):
            j = jj * p.cpu + lax.rem(here.lane + k, p.cpu)
            a_wait(j)
            a_forward(j, 0).start()

    each = -(-(p.S - 1) // near)
    for k in range(near + 1):
        if k < near:
            for n in range(1 + k * each, min(1 + (k + 1) * each, p.S)):
                part = wcol.at[:, q_rows(q_from(n), here.side), :]
                remote(part, part, q_ss.at[n], q_rs.at[q_from(n)], s, here.r).wait_recv()
                q_twin(q_from(n), here.side).start()
            a_at(k, a_near)
        if k == START:
            for w in range(nw):
                gather_rows(w)
        if k >= 1:
            a_at(k - 1, a_far)
        if k >= near + 1 - EARLY:
            for w in range(nw):
                gather_slot(w, k - (near - EARLY), LAG)

    @pl.when(jnp.logical_not(primary))
    def _():
        for j in range(p.P):
            a_wait(j)

    swap.wait_recv()
    pre2[...] = jnp.where(primary, pre[...], pre2[...])
    row = here.um * p.Q + here.uq
    preu[...] = jnp.broadcast_to(pre2[pl.ds(row, 1), :], preu.shape)

    for n in range(1, p.S):
        q_twin(q_from(n), 1 - here.side).wait_recv()
    q_own.wait()
    own = pl.ds(pl.multiple_of(here.group * p.W, PAIR), p.W)
    q_bias = parf[0:1, own].astype(F32)
    v_bias = parf[1:2, own].astype(F32)

    def project(i, carry):
        rows = pl.ds(pl.multiple_of(i * BQ, BQ), BQ)
        part = a_all[rows, :]
        for h in range(p.pairs):
            lanes = slice(h * PAIR, (h + 1) * PAIR)
            got = dot(part, wcol[h])
            q_out[rows, lanes] = (got[:, :PAIR] + q_bias[:, lanes]).astype(BF16)
            k_out[rows, lanes] = got[:, PAIR : 2 * PAIR].astype(BF16)
            v_out[rows, lanes] = (got[:, 2 * PAIR :] + v_bias[:, lanes]).astype(BF16)
        return carry

    lax.fori_loop(0, p.nq, project, 0)

    prefix = preu[0:1, 0:1]
    slots = nz + 1 + LAG - EARLY
    per = -(-slots // p.nq)

    def o_copy(i):
        rows = pl.ds(pl.multiple_of(i * BQ, BQ), BQ)
        home = here.uq * p.P + i // p.pieces
        piece = lax.rem(i, p.pieces)
        there = pl.ds(pl.multiple_of(piece * BQ, BQ), BQ)
        src = o_out.at[rows, :]
        dst = oh.at[here.um, there, own]
        away = jnp.logical_or(home != s, here.uc != c)
        recv = o_rs.at[here.um, here.group, piece]
        return away, lambda: remote(src, dst, o_ss.at[i], recv, home, here.chip + here.uc), (src, dst, recv)

    def attend(i, carry):
        rows = pl.ds(pl.multiple_of(i * BQ, BQ), BQ)
        row_pos = (lax.broadcasted_iota(jnp.int32, (BQ, 1), 0) + i * BQ + 1).astype(F32)
        bound = jnp.maximum(row_pos, prefix)
        key_pos = lax.broadcasted_iota(jnp.int32, (1, LEN), 1).astype(F32)
        seen = key_pos < bound

        def pair_step(h, inner):
            lanes = pl.ds(pl.multiple_of(h * PAIR, PAIR), PAIR)
            qp, kp, vp = q_out[rows, lanes], k_out[:, lanes], v_out[:, lanes]
            halves = []
            for e in (0, 1):
                logits = dot(jnp.where(head_lanes(BQ, e), qp, jnp.zeros_like(qp)), kp, 1, 1)
                logits = jnp.where(seen, logits, MASKED)
                top = jnp.max(logits, axis=1, keepdims=True)
                powers = jnp.exp2((logits - top) * SCALE2)
                total = jnp.sum(powers, axis=1, keepdims=True)
                halves.append(dot(powers.astype(BF16), vp) * (1.0 / total))
                level = top * SCALE2 + jnp.log2(total)
                turned = jnp.broadcast_to(level, (BQ, 128)).T
                lse_out[2 * h + e, :, pl.ds(pl.multiple_of(i * BQ, BQ), BQ)] = turned[0:8]
            o_out[rows, lanes] = jnp.where(head_lanes(BQ, 0), halves[0], halves[1]).astype(BF16)
            return inner

        lax.fori_loop(0, p.pairs, pair_step, 0)
        launch(*o_copy(i))

        for extra in range(per):
            for w in range(nw):
                gather_slot(w, i * per + extra + 1 + EARLY, LAG)

        return carry

    lax.fori_loop(0, p.nq, attend, 0)

    for m in range(p.M):
        for g in range(p.groups):
            for piece in range(p.pieces):
                src = o_out.at[pl.ds(0, BQ), :]
                dst = oh.at[m, pl.ds(piece * BQ, BQ), pl.ds(g * p.W, p.W)]
                pltpu.make_async_copy(src, dst, o_rs.at[m, g, piece]).wait()

    def o_sent(i, carry):
        sent(*o_copy(i))
        return carry

    lax.fori_loop(0, p.nq, o_sent, 0)
    for copy in small:
        copy.wait_send()
    swap.wait_send()
    for copy in local:
        copy.wait()
    for n in range(1, p.S):
        q_send(n).wait_send()
        q_twin(q_from(n), here.side).wait_send()
    for m in range(p.M):
        to, far = first_hop(m)

        @pl.when(to != s)
        def _():
            far().wait_send()

    @pl.when(primary)
    def _():
        for jj in range(near):
            for k in range(p.cpu):
                a_forward(jj * p.cpu + here.lane, k).wait_send()
            for k in range(1, p.cpu):
                a_forward(jj * p.cpu + lax.rem(here.lane + k, p.cpu), 0).wait_send()

    for w in range(nw):
        gather_wait(w)
        gather_drain(w)


def fore(plan, x, small, prefixes, qkv, weights):
    p = plan
    par = (sum(part.shape[0] for part in small), max(p.width, 128))
    nz = p.S // 2
    nw = len(weights)
    any_space = pl.BlockSpec(memory_space=pl.ANY)
    vmem = pl.BlockSpec(memory_space=pltpu.VMEM)
    shape = jax.ShapeDtypeStruct
    out_shape = (
        [shape((w.shape[0] * p.S, w.shape[1]), BF16) for w in weights]
        + [shape((par[0], p.D), BF16)]
        + [shape((LEN, p.W), BF16)] * 4
        + [shape((2 * p.pairs, 8, LEN), F32), shape((8, 128), F32), shape((p.M, p.T, p.D), BF16)]
        + [shape((LEN, p.D), BF16), shape((p.pairs, p.D, 3 * PAIR), BF16)]
    )
    dma = pltpu.SemaphoreType.DMA
    return pl.pallas_call(
        functools.partial(fore_kernel, p),
        out_shape=out_shape,
        in_specs=[vmem] * 6 + [pl.BlockSpec(memory_space=pltpu.SMEM)] + [vmem] * (1 + nw),
        out_specs=[any_space] * nw + [vmem] * 10,
        scratch_shapes=[
            pltpu.VMEM((p.M, p.T, p.D), BF16),
            pltpu.VMEM(par, BF16),
            pltpu.VMEM((8, 128), F32),
            pltpu.VMEM((p.groups, p.pairs, qkv.shape[0], 3 * PAIR), BF16),
            pltpu.VMEM((p.S,) + par, BF16),
            pltpu.VMEM((8, 128), F32),
            dma((p.S,)), dma((p.S,)), dma((2,)), dma((nw,)),
            dma((p.M,)), dma((p.P,)), dma((p.P, p.cpu)),
            dma((nw, 2, nz)), dma((nw, 2, nz)), dma((nw, nz)), dma((nw, nz)),
            dma((nw, 2, nz)), dma((nw, 2, nz)), dma((nw, 4, nz)), dma((nw, 4, nz)),
            dma((p.nq,)), dma((p.M, p.groups, p.pieces)),
            dma((p.S,)), dma((p.S,)), dma((p.S,)), dma((p.S,)), dma((1,)),
        ],
        compiler_params=pltpu.CompilerParams(
            collective_id=0, has_side_effects=True, vmem_limit_bytes=VMEM_LIMIT
        ),
        name="fore",
    )(x, *small, prefixes, qkv, *weights)


class GridSum:
    def __init__(self, here, grads, outs, refs):
        self.here, self.grads, self.outs = here, grads, outs
        self.nw = nw = len(grads)
        self.nz = here.rows
        self.planes = here.p.R // CORES
        self.own, self.acc, self.one, self.two, self.far = (refs[k * nw : (k + 1) * nw] for k in range(5))
        (self.ld, self.m_s, self.m_r, self.a_s, self.a_r, self.b_s, self.b_r, self.z_s, self.z_r) = refs[5 * nw : 5 * nw + 9]
        (self.x_s, self.x_r, self.t_s, self.t_r, self.f_s, self.f_r) = refs[5 * nw + 9 :]
        self.side_first = SIDE_FIRST

    @staticmethod
    def scratch(plan, shapes):
        nw = len(shapes)
        planes = plan.R // CORES
        nz = plan.S // 2
        dma = pltpu.SemaphoreType.DMA
        return (
            [pltpu.VMEM((2,) + sh, BF16) for sh in shapes]
            + [pltpu.VMEM((plan.S,) + sh, BF16) for sh in shapes]
            + [
                pltpu.VMEM((plan.S, sh[0], sh[1] // 2) if sf else (nz,) + sh, BF16)
                for sh, sf in zip(shapes, SIDE_FIRST)
            ]
            + [pltpu.VMEM((nz, sh[0], sh[1] // 2), BF16) for sh in shapes]
            + [pltpu.VMEM((max(nz, planes // 2), sh[0], sh[1] // 2), BF16) for sh in shapes]
            + [dma((nw,))]
            + [dma((nw, nz))] * 8
            + [dma((nw, planes))] * 2
            + [dma((nw,))] * 2
            + [dma((nw, 2))] * 2
        )

    @staticmethod
    def count(nw):
        return 5 * nw + 15

    def zr(self, k):
        return lax.rem(self.here.row + 1 + k, self.nz)

    def half(self, w, side):
        n = self.acc[w].shape[2] // 2
        return pl.ds(pl.multiple_of(side * n, n), n)

    def load(self, w, k):
        src = self.grads[w].at[pl.ds(2 * self.zr(k), 2), self.here.c]
        return pltpu.make_async_copy(src, self.own[w], self.ld.at[w])

    def swap(self, w, k):
        here = self.here
        pair = pl.ds(2 * self.zr(k), 2)
        return remote(
            self.grads[w].at[pair, 1 - here.c], self.acc[w].at[pair], self.m_s.at[w, k], self.m_r.at[w, k], here.s, here.mate
        )

    def first(self, w, k):
        here, zr = self.here, self.zr(k)
        if self.side_first[w]:
            pair = pl.ds(2 * zr, 2)
            src = self.acc[w].at[pair, :, self.half(w, 1 - here.side)]
            return remote(src, self.one[w].at[pair], self.a_s.at[w, k], self.a_r.at[w, k], here.s, here.twin)
        src = self.acc[w].at[2 * zr + 1 - here.col]
        return remote(src, self.one[w].at[zr], self.a_s.at[w, k], self.a_r.at[w, k], here.beside, here.r)

    def second(self, w, k):
        here, zr = self.here, self.zr(k)
        if self.side_first[w]:
            src = self.acc[w].at[2 * zr + 1 - here.col, :, self.half(w, here.side)]
            to = (here.beside, here.r)
        else:
            src = self.acc[w].at[2 * zr + here.col, :, self.half(w, 1 - here.side)]
            to = (here.s, here.twin)
        return remote(src, self.two[w].at[zr], self.b_s.at[w, k], self.b_r.at[w, k], *to)

    def final(self, w, k):
        here, zr = self.here, self.zr(k)
        src = self.acc[w].at[2 * zr + here.col, :, self.half(w, here.side)]
        return remote(
            src, self.far[w].at[here.row], self.z_s.at[w, k], self.z_r.at[w, here.row], 2 * zr + here.col, here.r
        )

    def begin(self):
        for k in range(self.nz):
            for w in range(self.nw):
                self.swap(w, k).start()
                if k == 0:
                    self.load(w, 0).start()

    def strips(self, w, body):
        def one(r, carry):
            body(pl.ds(pl.multiple_of(r * 16, 16), 16))
            return carry

        lax.fori_loop(0, self.acc[w].shape[1] // 16, one, 0)

    def event_one(self, w, k):
        zr = self.zr(k)
        pair = pl.ds(2 * zr, 2)
        self.load(w, k).wait()
        self.swap(w, k).wait_recv()
        acc, own = self.acc[w], self.own[w]

        def strip(at):
            acc[pair, at, :] = (acc[pair, at, :].astype(F32) + own[:, at, :].astype(F32)).astype(BF16)

        self.strips(w, strip)
        self.first(w, k).start()

        @pl.when(k < self.nz - 1)
        def _():
            self.load(w, jnp.minimum(k + 1, self.nz - 1)).start()

    def event_two(self, w, k):
        here, zr = self.here, self.zr(k)
        self.first(w, k).wait_recv()
        acc, one = self.acc[w], self.one[w]
        if self.side_first[w]:
            pair = pl.ds(2 * zr, 2)
            lanes = self.half(w, here.side)

            def strip(at):
                acc[pair, at, lanes] = (acc[pair, at, lanes].astype(F32) + one[pair, at, :].astype(F32)).astype(BF16)

        else:
            shard = 2 * zr + here.col

            def strip(at):
                acc[shard, at, :] = (acc[shard, at, :].astype(F32) + one[zr, at, :].astype(F32)).astype(BF16)

        self.strips(w, strip)
        self.second(w, k).start()

    def event_three(self, w, k):
        here, zr = self.here, self.zr(k)
        self.second(w, k).wait_recv()
        shard, lanes = 2 * zr + here.col, self.half(w, here.side)
        acc, two = self.acc[w], self.two[w]

        def strip(at):
            acc[shard, at, lanes] = (acc[shard, at, lanes].astype(F32) + two[zr, at, :].astype(F32)).astype(BF16)

        self.strips(w, strip)

        @pl.when(k < self.nz - 1)
        def _():
            self.final(w, k).start()

    def slots(self):
        return CADENCE * (self.nw * self.nz + 2 * SUM_LAG)

    def slot(self, n):
        @pl.when(lax.rem(n, CADENCE) == 0)
        def _():
            self.event(n // CADENCE)

    def event(self, n):
        for stage, body in ((2, self.event_three), (1, self.event_two), (0, self.event_one)):
            e = n - stage * SUM_LAG
            for w in range(self.nw):
                ok = jnp.logical_and(e >= 0, e < self.nw * self.nz)

                @pl.when(jnp.logical_and(ok, lax.rem(e, self.nw) == w))
                def _():
                    body(w, jnp.maximum(e, 0) // self.nw)

    def over(self, w, k):
        here = self.here
        pairs = self.planes // 2
        to = 2 * lax.rem(here.plane // 2 + k, pairs) + here.side
        src = self.two[w].at[0]
        return remote(
            src, self.one_slot(w, here.plane // 2), self.x_s.at[w, k], self.x_r.at[w, here.plane // 2],
            here.s, to * CORES + here.c,
        )

    def one_slot(self, w, k):
        return self.acc[w].at[k, :, self.half(w, self.here.side)]

    def to_twin(self, w, side):
        part = self.outs[w].at[self.here.c, :, self.half(w, side)]
        return remote(part, part, self.t_s.at[w], self.t_r.at[w], self.here.s, self.here.twin)

    def to_mate(self, w, core, via):
        side = self.here.side if via == 0 else 1 - self.here.side
        part = self.outs[w].at[core, :, self.half(w, side)]
        return remote(part, part, self.f_s.at[w, via], self.f_r.at[w, via], self.here.s, self.here.mate)

    def finish(self):
        here = self.here
        for w in range(self.nw):
            self.far[w][here.row] = self.acc[w][here.s, :, self.half(w, here.side)]
            for k in range(self.nz - 1):
                off = lax.rem(here.row + 1 + k, self.nz)
                part = self.far[w].at[off]
                remote(part, part, self.z_s.at[w, k], self.z_r.at[w, off], here.s, here.r).wait_recv()
            far, out, lanes = self.far[w], self.outs[w], self.half(w, here.side)

            def strip(at):
                total = far[0, at, :].astype(F32)
                for k in range(1, self.nz):
                    total = total + far[k, at, :].astype(F32)
                out[here.c, at, lanes] = total.astype(BF16)

            self.strips(w, strip)
            self.to_twin(w, here.side).start()
            self.to_mate(w, here.c, 0).start()

    def twin_to_mate(self):
        for w in range(self.nw):
            self.to_twin(w, 1 - self.here.side).wait_recv()
            self.to_mate(w, self.here.c, 1).start()

    def drain(self):
        for w in range(self.nw):
            for via in (0, 1):
                self.to_mate(w, 1 - self.here.c, via).wait_recv()
                self.to_mate(w, self.here.c, via).wait_send()
            self.to_twin(w, self.here.side).wait_send()
            for k in range(self.nz):
                self.swap(w, k).wait_send()
                self.first(w, k).wait_send()
                self.second(w, k).wait_send()
                if k < self.nz - 1:
                    self.final(w, k).wait_send()


def sum_peers(here):
    p = here.p
    planes = p.R // CORES
    far = [(here.s, lax.rem(here.plane + k, planes) * CORES + j) for k in range(1, planes) for j in range(CORES)]
    twin_chip = here.twin - here.c
    return plane_peers(here) + far + [(here.beside, twin_chip + j) for j in range(CORES)]


def split_rows(p, grad):
    rows, cols = grad.shape
    return grad.reshape(p.S, CORES, rows // (p.S * CORES), cols)


def whole_shard(halves):
    return halves.reshape(CORES * halves.shape[1], halves.shape[2]).astype(F32)


def back_kernel(plan, nw, *refs):
    p = plan
    here = Place(p)
    s, c = here.s, here.c
    nz, near, width = here.rows, p.near, p.width
    (q, k, v, o, lse, preu, do_home, a_all, wcol, x, stream, par, small) = refs[:13]
    grads = refs[13 : 13 + nw]
    rest = refs[13 + nw :]
    input_grad, g_out, small_out = rest[:3]
    outs = rest[3 : 3 + nw]
    rest = rest[3 + nw :]
    (do_all, low, dk_acc, dv_acc, k_turn, da_own, da_out, da_in, da_side) = rest[:9]
    x_buf, stream_buf, buf_sem, a_buf, a_sem, gq = rest[-6:]
    rest = rest[:-6]
    da_home = input_grad
    (dw_out, dw_own, dw_in, dw_far, dw_end, small_acc, small_in, small_all) = rest[9:17]
    (do_ss, do_rs, dm_s, dm_r, dy_s, dy_r, dh_s, dh_r, wt_s, wt_r, wz_s, wz_r, wx_s, wx_r, wd_s, wd_r) = rest[17:33]
    (ss_s, ss_r, sa_s, sa_r) = rest[33:37]
    sums = GridSum(here, grads, outs, rest[37:])
    greet(sum_peers(here))
    rows_here = pl.ds(pl.multiple_of(lax.rem(s, p.P) * p.T, p.T), p.T)

    def do_copy(m, g):
        core, lane = g // p.cpu, g % p.cpu
        to = here.unit_of(c, m, s) * p.cpu + lane
        src = do_home.at[m, :, pl.ds(g * p.W, p.W)]
        dst = do_all.at[rows_here, :]
        away = jnp.logical_or(to != s, c != core)
        recv = do_rs.at[lax.rem(s, p.P)]
        return away, lambda: remote(src, dst, do_ss.at[m, g], recv, to, here.chip + core), (src, dst, recv)

    for m in range(p.M):
        for g in range(p.groups):
            launch(*do_copy(m, g))
    sums.begin()
    small_acc[...] = small[...]
    prefix = preu[0:1, 0:1]

    def block_rows(i):
        return pl.ds(pl.multiple_of(i * BQ, BQ), BQ)

    def a_load(b):
        slot = lax.rem(b, 2)
        return pltpu.make_async_copy(
            a_all.at[:, pl.ds(pl.multiple_of(b * BQ, BQ), BQ)], a_buf.at[slot], a_sem.at[slot]
        )

    def weight_part(h, dst, slot_from=None):
        def some(b, carry):
            slot = lax.rem(b, 2)

            @pl.when(b < p.D // BQ - 1)
            def _():
                a_load(b + 1).start()

            a_load(b).wait()
            dst[pl.ds(pl.multiple_of(b * BQ, BQ), BQ), :] = dot(a_buf[slot], low[h], 0, 0).astype(BF16)
            if slot_from is not None:
                sums.slot(slot_from + b)
            return carry

        lax.fori_loop(0, p.D // BQ, some, 0)

    def bias_part(h):
        folds = PAIR // width
        for row, lanes in ((0, slice(0, PAIR)), (1, slice(2 * PAIR, 3 * PAIR))):
            total = jnp.sum(low[h, :, lanes].astype(F32), axis=0, keepdims=True)
            for n in range(folds):
                at = (here.group * p.pairs + h) * folds + n
                small_acc[at, row : row + 1, 0:width] = total[:, n * width : (n + 1) * width]

    def to_twin_dw():
        return remote(dw_out, dw_in, wt_s.at[0], wt_r.at[0], s, here.twin)

    def pair_step(turn, carry):
        h = lax.rem(turn + 1 + here.side, 2)
        lanes = pl.ds(pl.multiple_of(h * PAIR, PAIR), PAIR)
        k_turn[...] = k[:, lanes].astype(F32).T.astype(BF16)
        dk_acc[...] = jnp.zeros_like(dk_acc)
        dv_acc[...] = jnp.zeros_like(dv_acc)

        def query_step(n, inner):
            j = lax.rem((here.unit - here.uq * near) * p.cpu + n // p.pieces, p.P)
            i = j * p.pieces + lax.rem(n, p.pieces)
            rows = block_rows(i)

            @pl.when(jnp.logical_and(turn == 0, lax.rem(n, p.pieces) == 0))
            def _():
                part = do_all.at[pl.ds(pl.multiple_of(j * p.T, p.T), p.T), :]
                pltpu.make_async_copy(part, part, do_rs.at[j]).wait()

            qp, dop, op = q[rows, lanes], do_all[rows, lanes], o[rows, lanes]
            turned = (dop.astype(F32) * op.astype(F32)).T
            pos = (lax.broadcasted_iota(jnp.int32, (1, BQ), 1) + i * BQ + 1).astype(F32)
            bound = jnp.maximum(pos, prefix)
            dq_t = []
            for e in (0, 1):
                lit = head_lanes(BQ, e)
                qe = jnp.where(lit, qp, jnp.zeros_like(qp))
                de = jnp.where(lit, dop, jnp.zeros_like(dop))
                level = lse[2 * h + e, 0:1, rows]
                inner_sum = jnp.sum(turned[e * HEAD : (e + 1) * HEAD], axis=0, keepdims=True)
                total = jnp.zeros((HEAD, BQ), F32)
                for start in range(0, LEN, KEYS):
                    keys = slice(start, start + KEYS)
                    key_pos = (lax.broadcasted_iota(jnp.int32, (KEYS, 1), 0) + start).astype(F32)
                    logits = dot(k[keys, lanes], qe, 1, 1)
                    probs = jnp.where(key_pos < bound, jnp.exp2(logits * SCALE2 - level), 0.0)
                    slope = dot(v[keys, lanes], de, 1, 1)
                    dlog = (probs * (slope - inner_sum)).astype(BF16)
                    dv_acc[keys, :] += dot(probs.astype(BF16), de)
                    dk_acc[keys, :] += dot(dlog, qe)
                    total = total + dot(k_turn[e * HEAD : (e + 1) * HEAD, keys], dlog)
                dq_t.append(total)
            low[h, rows, 0:PAIR] = (jnp.concatenate(dq_t, axis=0).T * SCALE).astype(BF16)
            sums.slot(turn * p.nq + n)
            return inner

        lax.fori_loop(0, p.nq, query_step, 0)
        low[h, :, PAIR : 2 * PAIR] = (dk_acc[...] * SCALE).astype(BF16)
        low[h, :, 2 * PAIR :] = dv_acc[...].astype(BF16)
        bias_part(h)

        a_load(0).start()

        @pl.when(turn == 0)
        def _():
            weight_part(h, dw_out)
            to_twin_dw().start()

        return carry

    lax.fori_loop(0, p.pairs, pair_step, 0)

    half = p.D // CORES

    def block_of(n):
        lane = lax.rem(here.lane + 1 + n // (near * p.pieces), p.cpu)
        m = lax.rem(n, near * p.pieces)
        return ((m // p.pieces) * p.cpu + lane) * p.pieces + lax.rem(m, p.pieces)

    def da_half(rows, core):
        at = pl.ds(pl.multiple_of(core * half, half), half)
        total = dot(low[0, rows, :], wcol[0, at, :], 1, 1)
        for h in range(1, p.pairs):
            total = total + dot(low[h, rows, :], wcol[h, at, :], 1, 1)
        return total

    def da_mate(n, i):
        rows = block_rows(i)
        return remote(da_out.at[rows, :], da_in.at[rows, :], dm_s.at[n], dm_r.at[i], s, here.mate)

    far_blocks = (p.cpu - 1) * near * p.pieces
    count = p.pairs * p.nq

    def side_rows(i):
        return block_rows((i // p.pieces // p.cpu) * p.pieces + lax.rem(i, p.pieces))

    def da_over(n, i):
        return remote(da_own.at[block_rows(i), :], da_side.at[side_rows(i), :], dy_s.at[n], dy_r.at[i], here.beside, here.r)

    def da_first(n, carry):
        @pl.when(n < p.nq)
        def _():
            i = block_of(n)
            rows = block_rows(i)
            da_out[rows, :] = da_half(rows, 1 - c).astype(BF16)
            da_mate(n, i).start()
            da_own[rows, :] = da_half(rows, c).astype(BF16)

        @pl.when(n > 0)
        def _():
            last = jnp.maximum(n - 1, 0)
            i = block_of(last)
            rows = block_rows(i)
            da_mate(last, i).wait_recv()
            da_own[rows, :] = (da_own[rows, :].astype(F32) + da_in[rows, :].astype(F32)).astype(BF16)

            @pl.when(last < far_blocks)
            def _():
                da_over(last, i).start()

        sums.slot(count + n)
        return carry

    lax.fori_loop(0, p.nq + 1, da_first, 0)
    count = count + p.nq + 1

    own_pair = here.side
    weight_part(own_pair, dw_own, count)
    count = count + p.D // BQ
    to_twin_dw().wait_recv()
    dw_own[...] = (dw_own[...].astype(F32) + dw_in[...].astype(F32)).astype(BF16)
    span = 2 * width

    def dw_rows(zr):
        return pl.ds(pl.multiple_of(zr * span, span), span)

    def dw_send(n):
        zr = lax.rem(here.row + 1 + n, nz)
        return remote(
            dw_own.at[dw_rows(zr), :], dw_far.at[here.row], wz_s.at[n], wz_r.at[here.row], 2 * zr + here.col, here.r
        )

    for n in range(nz - 1):
        dw_send(n).start()

    def da_back(n, i):
        rows = block_rows(i)
        home = here.uq * p.P + i // p.pieces
        piece = lax.rem(i, p.pieces)
        dst = da_home.at[here.um, block_rows(piece), pl.ds(pl.multiple_of(c * half, half), half)]
        src = da_own.at[rows, :]
        recv = dh_r.at[here.um, c, piece]
        away = jnp.logical_or(home != s, here.uc != c)
        return away, lambda: remote(src, dst, dh_s.at[n], recv, home, here.chip + here.uc), (src, dst, recv)

    def da_second(n, carry):
        i = block_of(n)
        rows = block_rows(i)
        da_over(n, i).wait_recv()
        da_own[rows, :] = (da_own[rows, :].astype(F32) + da_side[side_rows(i), :].astype(F32)).astype(BF16)
        launch(*da_back(n, i))
        sums.slot(count + n - far_blocks)
        return carry

    lax.fori_loop(far_blocks, p.nq, da_second, 0)
    count = count + p.nq - far_blocks

    def rest_of_sums(n, carry):
        sums.slot(n)
        return carry

    lax.fori_loop(count, max(count, sums.slots()), rest_of_sums, 0)
    sums.finish()

    dw_far[here.row] = dw_own[dw_rows(here.row), :]
    for n in range(nz - 1):
        off = lax.rem(here.row + 1 + n, nz)
        remote(dw_far.at[off], dw_far.at[off], wz_s.at[n], wz_r.at[off], s, here.r).wait_recv()
    total = dw_far[0].astype(F32)
    for n in range(1, nz):
        total = total + dw_far[n].astype(F32)
    dw_end[...] = total.astype(BF16)
    slot = here.group * p.pairs + here.side
    twin_chip = here.twin - c

    def dw_give(n):
        fy, fx, fc = n // 4, n // 2 % 2, n % 2
        col = here.col if fy == 0 else 1 - here.col
        core = c if fc == 0 else 1 - c
        src = dw_end.at[pl.ds(pl.multiple_of(col * width, width), width), :]
        dst = gq.at[slot]
        to = (2 * here.row + col, (here.chip if fx == 0 else twin_chip) + core)
        return src, dst, to

    for n in range(1, 8):
        src, dst, to = dw_give(n)
        remote(src, dst, wd_s.at[n], wd_r.at[slot], *to).start()
    gq[slot] = dw_end[pl.ds(pl.multiple_of(here.col * width, width), width), :]

    def token_loads(m, piece):
        at = pl.ds(pl.multiple_of(piece * BQ, BQ), BQ)
        return (
            pltpu.make_async_copy(x.at[m, at, :], x_buf, buf_sem.at[0]),
            pltpu.make_async_copy(stream.at[m, at, :], stream_buf, buf_sem.at[1]),
        )

    blocks = p.M * p.pieces
    gain = par[4:5, :].astype(F32)

    def loads_of(n):
        return token_loads(n // p.pieces, lax.rem(n, p.pieces))

    for copy in loads_of(0):
        copy.start()

    def norm_back(n, carry):
        gain_sum, shift_sum = carry
        m, piece = n // p.pieces, lax.rem(n, p.pieces)
        at = pl.ds(pl.multiple_of(piece * BQ, BQ), BQ)
        for core in range(CORES):
            dst = da_home.at[m, at, pl.ds(core * half, half)]
            pltpu.make_async_copy(dst, dst, dh_r.at[m, core, piece]).wait()
        for copy in loads_of(n):
            copy.wait()
        values = x_buf[...].astype(F32)
        dy = da_home[m, at, :].astype(F32)
        centre = values - jnp.mean(values, axis=-1, keepdims=True)
        spread = jnp.mean(centre * centre, axis=-1, keepdims=True)
        scale = lax.rsqrt(spread + EPS)
        wn = centre * scale
        e = dy * gain
        dw = scale * (e - jnp.mean(e, axis=-1, keepdims=True) - wn * jnp.mean(e * wn, axis=-1, keepdims=True))
        input_grad[m, at, :] = (stream_buf[...] + dw).astype(BF16)

        @pl.when(n + 1 < blocks)
        def _():
            for copy in loads_of(jnp.minimum(n + 1, blocks - 1)):
                copy.start()

        return (
            gain_sum + jnp.sum(dy * wn, axis=0, keepdims=True),
            shift_sum + jnp.sum(dy, axis=0, keepdims=True),
        )

    none = jnp.zeros((1, p.D), F32)
    gain_sum, shift_sum = lax.fori_loop(0, blocks, norm_back, (none, none))
    for n in range(p.S):
        lanes = slice(n * width, (n + 1) * width)
        small_acc[n, 4:5, 0:width] = gain_sum[:, lanes]
        small_acc[n, 8:9, 0:width] = shift_sum[:, lanes]

    def tiny(n):
        to = lax.rem(s + n, p.S)
        return remote(small_acc.at[to], small_in.at[n], ss_s.at[n], ss_r.at[n], to, here.r)

    for n in range(1, p.S):
        tiny(n).start()
    sums.twin_to_mate()
    total = small_acc[s]
    for n in range(1, p.S):
        tiny(n).wait_recv()
        total = total + small_in[n]
    small_all[here.r] = total

    def every(n):
        to = lax.rem(here.r + n, p.R)
        return remote(small_all.at[here.r], small_all.at[here.r], sa_s.at[n], sa_r.at[here.r], s, to)

    for n in range(1, p.R):
        every(n).start()
    for n in range(1, p.R):
        off = lax.rem(here.r + n, p.R)
        remote(small_all.at[0], small_all.at[off], sa_s.at[n], sa_r.at[off], s, here.r).wait_recv()
    total = small_all[0]
    for n in range(1, p.R):
        total = total + small_all[n]
    small_out[...] = total

    for m in range(p.M):
        for g in range(p.groups):
            sent(*do_copy(m, g))

    def da_sent(n, carry):
        i = block_of(n)
        da_mate(n, i).wait_send()

        @pl.when(n < far_blocks)
        def _():
            da_over(n, i).wait_send()

        @pl.when(n >= far_blocks)
        def _():
            sent(*da_back(n, i))

        return carry

    lax.fori_loop(0, p.nq, da_sent, 0)
    to_twin_dw().wait_send()
    for n in range(nz - 1):
        dw_send(n).wait_send()
    for n in range(1, 8):
        src, dst, to = dw_give(n)
        remote(src, dst, wd_s.at[n], wd_r.at[slot], *to).wait_send()
    for n in range(p.groups * p.pairs):

        @pl.when(n != slot)
        def _():
            remote(gq.at[n], gq.at[n], wd_s.at[0], wd_r.at[n], s, here.r).wait_recv()

        for k in range(3):
            at = k * p.D + n * PAIR
            g_out[:, at : at + PAIR] = gq[n, :, k * PAIR : (k + 1) * PAIR]

    for n in range(1, p.S):
        tiny(n).wait_send()
    for n in range(1, p.R):
        every(n).wait_send()
    sums.drain()


def back(plan, units, small, grads):
    p = plan
    nw = len(grads)
    nz = p.S // 2
    planes = p.R // CORES
    split = [split_rows(p, grad) for grad in grads]
    shapes = [h.shape[2:] for h in split]
    any_space = pl.BlockSpec(memory_space=pl.ANY)
    vmem = pl.BlockSpec(memory_space=pltpu.VMEM)
    dma = pltpu.SemaphoreType.DMA
    shape = jax.ShapeDtypeStruct
    half = p.D // CORES
    outs = pl.pallas_call(
        functools.partial(back_kernel, p, nw),
        out_shape=[
            shape((p.M, p.T, p.D), BF16),
            shape((p.width, 3 * p.D), BF16),
            shape(small.shape[1:], F32),
        ]
        + [shape((CORES,) + sh, BF16) for sh in shapes],
        in_specs=[vmem] * 6 + [any_space] * 2 + [vmem] + [any_space] * 2 + [vmem] * 2 + [any_space] * nw,
        out_specs=[vmem] * (3 + nw),
        scratch_shapes=[
            pltpu.VMEM((LEN, p.W), BF16),
            pltpu.VMEM((p.pairs, LEN, 3 * PAIR), BF16),
            pltpu.VMEM((LEN, PAIR), F32),
            pltpu.VMEM((LEN, PAIR), F32),
            pltpu.VMEM((PAIR, LEN), BF16),
            pltpu.VMEM((LEN, half), BF16),
            pltpu.VMEM((LEN, half), BF16),
            pltpu.VMEM((LEN, half), BF16),
            pltpu.VMEM((p.near * p.T, half), BF16),
            pltpu.VMEM((p.D, 3 * PAIR), BF16),
            pltpu.VMEM((p.D, 3 * PAIR), BF16),
            pltpu.VMEM((p.D, 3 * PAIR), BF16),
            pltpu.VMEM((nz, 2 * p.width, 3 * PAIR), BF16),
            pltpu.VMEM((2 * p.width, 3 * PAIR), BF16),
            pltpu.VMEM(small.shape, F32),
            pltpu.VMEM(small.shape, F32),
            pltpu.VMEM((p.R,) + small.shape[1:], F32),
            dma((p.M, p.groups)), dma((p.P,)),
            dma((p.nq,)), dma((p.nq,)), dma((p.nq,)), dma((p.nq,)),
            dma((p.nq,)), dma((p.M, CORES, p.pieces)),
            dma((1,)), dma((1,)), dma((nz,)), dma((nz,)), dma((planes,)), dma((planes,)), dma((8,)), dma((8,)),
            dma((p.S,)), dma((p.S,)), dma((p.R,)), dma((p.R,)),
        ]
        + GridSum.scratch(p, shapes)
        + [pltpu.VMEM((BQ, p.D), BF16), pltpu.VMEM((BQ, p.D), F32), dma((2,))]
        + [pltpu.VMEM((2, LEN, BQ), BF16), dma((2,))]
        + [pltpu.VMEM((p.groups * p.pairs, p.width, 3 * PAIR), BF16)],
        compiler_params=pltpu.CompilerParams(
            collective_id=1, has_side_effects=True, vmem_limit_bytes=VMEM_LIMIT
        ),
        name="back",
    )(*units, small, *split)
    return outs[0], outs[1].astype(F32), outs[2], [whole_shard(part) for part in outs[3:]]


def per_device(
    sizes,
    inputs,
    prefix,
    qkv_weight,
    qv_bias,
    out_weight,
    branch_bias,
    up_weight,
    up_bias,
    down_weight,
    norm_gain,
    norm_bias,
    cotangent,
):
    p = Plan(sizes, (inputs.shape[0], 1, inputs.shape[2], inputs.shape[3]))
    tokens_all = p.M * p.T
    x = inputs[:, 0]
    width = p.D // p.S
    spare = max(128 - width, 0)
    small_in = (qv_bias, branch_bias, norm_gain, norm_bias, up_bias.reshape(-1, width))
    (wo, wu, wd, parf, q, k, v, o, lse, preu, o_home, a_unit, w_unit) = fore(
        p, x, small_in, prefix[:, 0], qkv_weight, (out_weight, up_weight, down_weight)
    )
    par32 = parf.astype(F32)
    bias_branch = par32[2:4]
    gains, shifts = par32[4:8], par32[8:12]
    bias_up = par32[12:].reshape(-1, p.S, width).transpose(1, 0, 2).reshape(-1)

    tokens = x.reshape(tokens_all, p.D).astype(F32)
    upstream = cotangent[:, 0].reshape(tokens_all, p.D).astype(F32)
    mixed_low = o_home.reshape(tokens_all, p.D)
    branch = dot(mixed_low, wo) + bias_branch[0]
    side, pull_side = jax.vjp(normed, branch, gains[1:2], shifts[1:2])
    stream = tokens + side
    normal_mid, pull_mid = jax.vjp(normed, stream, gains[2:3], shifts[2:3])
    middle_low = normal_mid.astype(BF16)
    upper = dot(middle_low, wu) + bias_up
    below = 0.5 * (1.0 + lax.erf(upper * math.sqrt(0.5)))
    slope = below + upper * jnp.exp(-0.5 * upper * upper) * (1.0 / math.sqrt(2.0 * math.pi))
    active_low, slope = lax.optimization_barrier(((upper * below).astype(BF16), slope))
    lower = dot(active_low, wd) + bias_branch[1]
    closing, pull_close = jax.vjp(normed, lower, gains[3:4], shifts[3:4])
    output = (stream + closing).astype(BF16)
    grad_lower, gain_three, shift_three = pull_close(upstream)
    lower_low = grad_lower.astype(BF16)
    grad_active = dot(lower_low, wd, 1, 1)
    upper_low = (grad_active * slope).astype(BF16)
    grad_middle = dot(upper_low, wu, 1, 1)
    grad_mid_in, gain_two, shift_two = pull_mid(grad_middle)
    grad_stream = grad_mid_in + upstream
    grad_branch, gain_one, shift_one = pull_side(grad_stream)
    branch_low = grad_branch.astype(BF16)
    grad_mixed = dot(branch_low, wo, 1, 1).astype(BF16)

    grads = (
        dot(active_low, lower_low, 0, 0).astype(BF16),
        dot(middle_low, upper_low, 0, 0).astype(BF16),
        dot(mixed_low, branch_low, 0, 0).astype(BF16),
    )
    def column_sum(values):
        return jnp.sum(values.astype(F32), axis=0, keepdims=True)

    du_sum = column_sum(upper_low).reshape(p.S, -1, width).transpose(1, 0, 2).reshape(-1, p.D)
    none = jnp.zeros((1, p.D), F32)
    small = jnp.concatenate(
        [
            none, none, column_sum(branch_low), column_sum(lower_low),
            none, gain_one, gain_two, gain_three,
            none, shift_one, shift_two, shift_three,
            du_sum,
        ], axis=0,
    )
    small = jnp.pad(small.reshape(-1, p.S, width).transpose(1, 0, 2), ((0, 0), (0, 0), (0, spare)))
    by_token = (p.M, p.T, p.D)
    input_grad, sum_qkv, tiny, (sum_down, sum_up, sum_out) = back(
        p,
        (
            q, k, v, o, lse, preu, grad_mixed.reshape(by_token), a_unit, w_unit,
            x, grad_stream.reshape(by_token), parf,
        ),
        small, grads,
    )
    tiny = tiny[:, :width]
    shaped = (p.M, 1, p.T, p.D)
    return (
        output.reshape(shaped),
        input_grad.reshape(shaped),
        sum_qkv,
        tiny[0:2],
        sum_out,
        tiny[2:4],
        sum_up,
        tiny[12:].reshape(-1),
        sum_down,
        tiny[4:8],
        tiny[8:12],
    )


def solution(mesh):
    sizes = {name: mesh.shape[name] for name in ("shard", "replica")}
    placed = (
        P(None, "replica", "shard", None),
        P(None, "replica", None),
        P("shard", None),
        P(None, "shard"),
        P("shard", None),
        P(None, "shard"),
        P("shard", None),
        P("shard"),
        P("shard", None),
        P(None, "shard"),
        P(None, "shard"),
        P(None, "replica", "shard", None),
    )
    return jax.shard_map(
        functools.partial(per_device, sizes),
        mesh=mesh,
        in_specs=placed,
        out_specs=(
            P(None, "replica", "shard", None),
            P(None, "replica", "shard", None),
            P("shard", None),
            P(None, "shard"),
            P("shard", None),
            P(None, "shard"),
            P("shard", None),
            P("shard"),
            P("shard", None),
            P(None, "shard"),
            P(None, "shard"),
        ),
        check_vma=False,
    )
```
